32 devices in a mesh: clip: 2 (over x), tile: 8 (over z, y), chan: 2 (over core).
Axes of the slice: x: 2, y: 2, z: 4, core: 2. Of those that a mesh axis runs over, the one named last changes fastest.
Arguments:
- owner_latent: bfloat16 [16, 5, 1536], P(('clip', 'tile')), parts along dimension 0, may hold values from -40 to 40, as said below
- tile_counts: int32 [16], P('clip'), parts along dimension 0, may hold values from 1 to 5, as said below
- stem_weight: bfloat16 [27, 16, 384], P(None, None, 'chan'), may hold values from -0.3125 to 0.3125
- stem_bias: float32 [384], P('chan'), may hold values from -1.5 to 1.5
- first_gain: float32 [384], P('chan'), may hold values from 0.5 to 1.5
- first_shift: float32 [384], P('chan'), may hold values from -2.5 to 2.5
- first_weight: bfloat16 [27, 384, 384], P(None, None, 'chan'), may hold values from -0.0625 to 0.0625
- first_bias: float32 [384], P('chan'), may hold values from -2.5 to 2.5
- second_gain: float32 [384], P('chan'), may hold values from 0.5 to 1.5
- second_shift: float32 [384], P('chan'), may hold values from -2.5 to 2.5
- second_weight: bfloat16 [27, 384, 384], P(None, None, 'chan'), may hold values from -0.0625 to 0.0625
- second_bias: float32 [384], P('chan'), may hold values from -1.5 to 1.5
- upsample_weight: bfloat16 [9, 384, 192], replicated, may hold values from -0.109375 to 0.109375
- upsample_bias: float32 [192], replicated, may hold values from -1.5 to 1.5
Outputs:
- upsampled: bfloat16 [8, 48, 32, 192], P(('clip', 'chan'), None, 'tile'), parts along dimension 0
The draws below stay inside these ranges and needn't reach their ends.
There are 2 independent parts, one for each index of `clip`. The reference program is written for one: setup_inputs(seed, part) draws one part's arguments, and reference() takes and returns one part's arrays. A program takes and returns all parts, laid end to end along the dimension named above; an argument that names none is the same for every part. Nothing has to cross between parts.
Inputs may be any that keep to these rules, and one draw needn't show every extreme that they name: Owner o holds latent columns starts[o] to starts[o] + tile_counts[o] - 1 in its first slots, in order; every count is at least 1; the owners of each aligned group of 4 together hold exactly the 8 columns of the strips of the devices with the same group's indices along tile. `owner_latent`: slots at or beyond an owner's count hold no latent column.
All inputs are finite; a program needn't handle non-finite values.
Results may differ from the reference program's by a relative error of at most 0.012.
Values may be sent and summed in bfloat16 or wider, within the bound.
No kernel may reach another device: no remote copies, remote signals or barrier semaphores. Data moves between devices by JAX's collectives and lax.ppermute only.
A program may use at most 128 MiB of HBM per device.

```python
import jax
import jax.numpy as jnp
from jax import lax

ZC = 16
CH = 384
GROUPS = 32
F = 4
H = 24
W_DEV = 2
SLOTS = 5
WIDTH = 16
ROW = 1536
CH_OUT = 192
N_TILE = 8


def owner_counts(key):
    base_key = jax.random.fold_in(key, 11)
    first_key, second_key, third_key = jax.random.split(base_key, 3)
    group_total = N_TILE // 4
    patterns = jnp.array([[4 * W_DEV - 3, 1, 1, 1], [W_DEV, W_DEV, W_DEV, W_DEV], [2 * W_DEV - 1, 2 * W_DEV - 1, 1, 1]], dtype=jnp.int32)
    chosen = jax.random.randint(first_key, (group_total,), 0, 3)
    forced = jax.random.randint(second_key, (), 0, group_total)
    chosen = jnp.where(jnp.arange(group_total, dtype=jnp.int32) == forced, 0, chosen)
    loads = patterns[chosen]
    scores = jax.random.randint(third_key, (group_total, 4), 0, 1 << 20) * 4 + jnp.arange(4, dtype=jnp.int32)[None, :]
    order = jnp.argsort(scores, axis=1)
    loads = jnp.take_along_axis(loads, order, axis=1)
    return loads.reshape(-1).astype(jnp.int32)


def draw_tile_counts(key, part):
    return owner_counts(key)


def draw_owner_latent(key, part):
    loads = owner_counts(key)
    starts = (jnp.cumsum(loads) - loads).astype(jnp.int32)
    slot_index = jnp.arange(SLOTS, dtype=jnp.int32)
    columns = jnp.minimum(starts[:, None] + slot_index[None, :], WIDTH - 1).astype(jnp.float32)
    position = columns / (WIDTH - 1)
    value_key, row_key, channel_key = jax.random.split(jax.random.fold_in(key, 12), 3)
    column_scale = 0.25 * jnp.exp(jnp.log(8.0) * position)
    base = jnp.clip(jax.random.normal(value_key, (N_TILE, SLOTS, F, H, ZC), jnp.float32), -4.0, 4.0)
    offset = 1.2 * jnp.clip(jax.random.normal(channel_key, (ZC,), jnp.float32), -3.0, 3.0)
    row_scale = jnp.exp(jax.random.uniform(row_key, (H,), jnp.float32, jnp.log(0.3), jnp.log(3.0)))
    values = (base * row_scale[None, None, None, :, None] + offset[None, None, None, None, :]) * column_scale[:, :, None, None, None]
    return values.reshape(N_TILE, SLOTS, F * H * ZC).astype(jnp.bfloat16)


def shard_levels(own_key, shape, shards, least, high):
    loudness, own = 1.0, jax.random.fold_in(own_key, 6)
    for axis_at, blocks in shards:
        heights = jnp.exp(jax.random.uniform(jax.random.fold_in(own, axis_at), (blocks,), jnp.float32, least / len(shards), high / len(shards)))
        loudness = loudness * jnp.repeat(heights, shape[axis_at] // blocks).reshape([-1 if axis == axis_at else 1 for axis in range(len(shape))])
    return loudness


def normal_values(key, dims, scale, bound, pieces=(), kind=jnp.bfloat16):
    values = jax.random.normal(key, dims, jnp.float32) * scale
    if len(pieces) > 0:
        values = shard_levels(key, dims, pieces, -0.22, 0.18) * values
    return jnp.clip(values, min=-bound, max=bound).astype(kind)


def setup_inputs(seed: int = 0, part: int = 0) -> dict:
    key_of = jax.random.split(jax.random.key(seed), 15)
    part_splits = jax.random.split(jax.random.fold_in(key_of[14], part), 15)
    return {
        "owner_latent": draw_owner_latent(jax.random.fold_in(jax.random.fold_in(key_of[14], part), 71), part),
        "tile_counts": draw_tile_counts(jax.random.fold_in(jax.random.fold_in(key_of[14], part), 71), part),
        "stem_weight": normal_values(key_of[2], (27, ZC, CH), (27 * ZC) ** -0.5, 0.3125, ((2, 2),)),
        "stem_bias": normal_values(key_of[3], (CH,), 0.3, 1.5, ((0, 2),), jnp.float32),
        "first_gain": jnp.clip(1.0 + 0.1 * jax.random.normal(key_of[4], (CH,), jnp.float32), 0.5, 1.5),
        "first_shift": normal_values(key_of[5], (CH,), 0.5, 2.5, ((0, 2),), jnp.float32),
        "first_weight": normal_values(key_of[6], (27, CH, CH), (27 * CH) ** -0.5, 0.0625, ((2, 2),)),
        "first_bias": normal_values(key_of[7], (CH,), 0.5, 2.5, ((0, 2),), jnp.float32),
        "second_gain": jnp.clip(1.0 + 0.1 * jax.random.normal(key_of[8], (CH,), jnp.float32), 0.5, 1.5),
        "second_shift": normal_values(key_of[9], (CH,), 0.5, 2.5, ((0, 2),), jnp.float32),
        "second_weight": normal_values(key_of[10], (27, CH, CH), (27 * CH) ** -0.5, 0.0625, ((2, 2),)),
        "second_bias": normal_values(key_of[11], (CH,), 0.3, 1.5, ((0, 2),), jnp.float32),
        "upsample_weight": normal_values(key_of[12], (9, CH, CH_OUT), (9 * CH) ** -0.5, 0.109375),
        "upsample_bias": normal_values(key_of[13], (CH_OUT,), 0.3, 1.5, (), jnp.float32),
    }


EPSILON = 1e-06

def causal_conv(values, weight):
    frame_count, row_count, column_count, _ = values.shape
    padded = jnp.pad(values, ((2, 0), (1, 1), (1, 1), (0, 0)))
    running = jnp.zeros((frame_count * row_count * column_count, weight.shape[2]), jnp.float32)
    for frame_shift in range(3):
        for row_shift in range(3):
            for column_shift in range(3):
                window = padded[frame_shift:frame_shift + frame_count, row_shift:row_shift + row_count, column_shift:column_shift + column_count, :]
                tap_weight = weight[9 * frame_shift + 3 * row_shift + column_shift]
                running = running + jnp.dot(window.reshape(-1, values.shape[3]), tap_weight, preferred_element_type=jnp.float32)
    return running

def group_act(stored, gain, shift):
    values = stored.astype(jnp.float32).reshape(-1, GROUPS, CH // GROUPS)
    group_mean = lax.optimization_barrier(jnp.mean(values, axis=(0, 2)))
    spread = values - group_mean[None, :, None]
    variance = lax.optimization_barrier(jnp.mean(spread * spread, axis=(0, 2)))
    scaled = (spread * lax.rsqrt(variance + EPSILON)[None, :, None]).reshape(-1, CH)
    scaled = scaled * gain[None, :] + shift[None, :]
    return jax.nn.silu(scaled).astype(jnp.bfloat16)

def reference(owner_latent, tile_counts, stem_weight, stem_bias, first_gain, first_shift, first_weight, first_bias, second_gain, second_shift, second_weight, second_bias, upsample_weight, upsample_bias):
    counts = tile_counts.astype(jnp.int32)
    starts = (jnp.cumsum(counts) - counts).astype(jnp.int32)
    slot_index = jnp.arange(SLOTS, dtype=jnp.int32)
    columns = (starts[:, None] + slot_index[None, :]).reshape(-1)
    usable = (slot_index[None, :] < counts[:, None]).reshape(-1)
    wanted = jnp.arange(WIDTH, dtype=jnp.int32)
    matches = (columns[None, :] == wanted[:, None]) & usable[None, :]
    latent = jnp.dot(matches.astype(jnp.bfloat16), owner_latent.reshape(N_TILE * SLOTS, ROW), preferred_element_type=jnp.float32)
    latent = latent.astype(jnp.bfloat16).reshape(WIDTH, F, H, ZC).transpose(1, 2, 0, 3)
    hidden_zero = (causal_conv(latent, stem_weight) + stem_bias[None, :]).astype(jnp.bfloat16)
    first_act = group_act(hidden_zero, first_gain, first_shift).reshape(F, H, WIDTH, CH)
    first_out = (causal_conv(first_act, first_weight) + first_bias[None, :]).astype(jnp.bfloat16)
    second_act = group_act(first_out, second_gain, second_shift).reshape(F, H, WIDTH, CH)
    second_out = causal_conv(second_act, second_weight) + second_bias[None, :]
    hidden_one = (hidden_zero.astype(jnp.float32) + second_out).astype(jnp.bfloat16).reshape(F, H, WIDTH, CH)
    doubled = jnp.repeat(jnp.repeat(hidden_one, 2, axis=1), 2, axis=2)
    padded = jnp.pad(doubled, ((0, 0), (1, 1), (1, 1), (0, 0)))
    running = jnp.zeros((F * 2 * H * 2 * WIDTH, CH_OUT), jnp.float32)
    for row_shift in range(3):
        for column_shift in range(3):
            window = padded[:, row_shift:row_shift + 2 * H, column_shift:column_shift + 2 * WIDTH, :]
            running = running + jnp.dot(window.reshape(-1, CH), upsample_weight[3 * row_shift + column_shift], preferred_element_type=jnp.float32)
    upsampled = (running + upsample_bias[None, :]).astype(jnp.bfloat16)
    return upsampled.reshape(F, 2 * H, 2 * WIDTH, CH_OUT)
```

```python
import functools

import jax
import jax.numpy as jnp
from jax import lax
from jax.experimental import pallas as pl
from jax.experimental.pallas import tpu as pltpu
from jax.sharding import PartitionSpec as P

GROUPS = 32
F = 4
H = 24
W_DEV = 2
HALO = 2
PITCH = 8
H_PAD = 32
EPSILON = 1e-06


def joined(own, other, core):
    low = jnp.concatenate([own, other], axis=-1)
    high = jnp.concatenate([other, own], axis=-1)
    return jnp.where(core == 0, low, high)


def group_mean(column_sums, per_group, cells):
    channels = column_sums.shape[1]
    row = lax.broadcasted_iota(jnp.int32, (channels, channels), 0).astype(jnp.float32)
    column = lax.broadcasted_iota(jnp.int32, (channels, channels), 1).astype(jnp.float32)
    same = jnp.floor((row + 0.5) / per_group) == jnp.floor((column + 0.5) / per_group)
    total = jnp.dot(
        column_sums,
        same.astype(jnp.float32),
        precision=lax.Precision.HIGHEST,
        preferred_element_type=jnp.float32,
    )
    return total[0:1] * (1.0 / (cells * per_group))


def put(ref, place, value):
    for block in range(ref.shape[0]):
        part = value[:, block * 128 : (block + 1) * 128]
        ref[block, place, 0 : part.shape[1]] = part


def take(ref, place, channels):
    parts = []
    for block in range(ref.shape[0]):
        parts.append(ref[block, place, :][:, : channels - block * 128])
    return jnp.concatenate(parts, axis=1)


def silu(value):
    half = 0.5 * value
    return half + half * jnp.tanh(half)


def first_kernel(
    power,
    counts,
    owners,
    stem_own,
    stem_other,
    small_own,
    small_other,
    weight,
    act_out,
    hidden_out,
    shifted,
    patches,
    stem_full,
    hidden,
    acts,
    produced,
    sums,
):
    tile_count = counts.shape[0]
    width = tile_count * W_DEV
    me = lax.axis_index("tile")
    core = lax.axis_index("chan")
    zc, half = stem_own.shape[1], stem_own.shape[2]
    full = 2 * half
    frame_lanes = H_PAD * zc
    pieces = max(1, width // 16)
    rows = H // pieces
    cells = F * H * width
    leftmost = me * W_DEV - HALO

    slots = PITCH * tile_count
    lane = lax.broadcasted_iota(jnp.int32, (3 * width, slots), 1)
    owner_at = lane // PITCH
    slot_at = lane - owner_at * PITCH
    held = jnp.full((3 * width, slots), -5, jnp.int32)
    start = jnp.int32(0)
    for owner in range(tile_count):
        place = (me ^ owner) if power else jnp.int32(owner)
        count = counts[owner]
        held = jnp.where((owner_at == place) & (slot_at < count), start + slot_at, held)
        start = start + count
    position = lax.broadcasted_iota(jnp.int32, (3 * width, slots), 0)
    shift = (position >= width).astype(jnp.int32) + (position >= 2 * width).astype(jnp.int32)
    column = position - shift * width + leftmost
    column = jnp.where(column < 0, column + width, column)
    column = jnp.where(column >= width, column - width, column)
    selection = (held == column + shift - 1).astype(jnp.bfloat16)
    for frame in range(F):
        lanes = slice(frame * frame_lanes, (frame + 1) * frame_lanes)
        chosen = jnp.dot(selection, owners[:, lanes], preferred_element_type=jnp.float32)
        shifted[:, frame] = chosen.reshape(3, width, frame_lanes)

    stem_full[...] = jnp.zeros(stem_full.shape, jnp.bfloat16)
    for tap in range(27):
        a, b, e = tap // 9, tap // 3 % 3, tap % 3
        at = e * 4 * zc + b * zc
        stem_full[a, at : at + zc, :] = joined(stem_own[tap], stem_other[tap], core)
    stem_bias = joined(small_own[0:1], small_other[0:1], core)
    first_gain = joined(small_own[1:2], small_other[1:2], core)
    first_shift = joined(small_own[2:3], small_other[2:3], core)

    per_block = 128 // zc
    lane128 = lax.broadcasted_iota(jnp.int32, (F, width, 128), 2)
    for row in range(H):
        block = row // per_block * 128
        offset = row % per_block * zc
        window = shifted[:, :, :, block : block + 256]
        one = pltpu.roll(window[0], (256 - offset) % 256, axis=2)[:, :, :128]
        two = pltpu.roll(window[1], (320 - offset) % 256, axis=2)[:, :, :128]
        three = pltpu.roll(window[2], (256 - offset) % 256, axis=2)[:, :, :128]
        patches[:, row, :, 0:128] = jnp.where(lane128 < 64, one, two).astype(jnp.bfloat16)
        patches[:, row, :, 128:256] = three.astype(jnp.bfloat16)

    def over_pieces(body):
        if pieces == 1:
            body(0)
        else:
            lax.fori_loop(0, pieces, lambda i, _: (body(i * rows), 0)[1], 0)

    def span(frame, row):
        return pl.ds(pl.multiple_of((frame * H + row) * width, 16), rows * width)

    sums[...] = jnp.zeros_like(sums)
    for frame in range(F):

        def stem(row):
            total = jnp.zeros((rows * width, full), jnp.float32)
            for a in range(max(0, 2 - frame), 3):
                lhs = patches[frame + a - 2, pl.ds(row, rows)].reshape(rows * width, 256)
                total += jnp.dot(lhs, stem_full[a], preferred_element_type=jnp.float32)
            value = (total + stem_bias).astype(jnp.bfloat16).astype(jnp.float32)
            put(hidden, span(frame, row), value)
            sums[0:1, :] += jnp.sum(value, axis=0, keepdims=True)

        over_pieces(stem)

    per_group = full // GROUPS
    mean = group_mean(jnp.broadcast_to(sums[0:1, :], (8, full)), per_group, cells)
    for frame in range(F):

        def squares(row):
            spread = take(hidden, span(frame, row), full) - mean
            sums[1:2, :] += jnp.sum(spread * spread, axis=0, keepdims=True)

        over_pieces(squares)
    variance = group_mean(jnp.broadcast_to(sums[1:2, :], (8, full)), per_group, cells)
    scale = lax.rsqrt(variance + EPSILON) * first_gain

    spot = lax.broadcasted_iota(jnp.int32, (1, width, full), 1) + leftmost
    spot = jnp.where(spot < 0, spot + width, spot)
    spot = jnp.where(spot >= width, spot - width, spot)
    zero_row = jnp.zeros((width, full), jnp.bfloat16)
    for e in range(3):
        for frame in range(F):
            acts[e, frame, 0] = zero_row
            acts[e, frame, H + 1] = zero_row
    for frame in range(F):

        def activate(row):
            spread = take(hidden, span(frame, row), full) - mean
            value = silu(spread * scale + first_shift).reshape(rows, width, full)
            left = jnp.where(spot == 0, 0.0, pltpu.roll(value, 1, axis=1))
            right = jnp.where(spot == width - 1, 0.0, pltpu.roll(value, width - 1, axis=1))
            place = pl.ds(row + 1, rows)
            acts[0, frame, place] = left.astype(jnp.bfloat16)
            acts[1, frame, place] = value.astype(jnp.bfloat16)
            acts[2, frame, place] = right.astype(jnp.bfloat16)

        over_pieces(activate)

    first_bias = small_own[4:5]
    for frame in range(F):

        def convolve(row):
            total = jnp.zeros((rows * width, half), jnp.float32)
            for a in range(max(0, 2 - frame), 3):
                for b in range(3):
                    lhs = jnp.concatenate(
                        [
                            acts[e, frame + a - 2, pl.ds(row + b, rows)].reshape(rows * width, full)
                            for e in range(3)
                        ],
                        axis=1,
                    )
                    tap = 9 * a + 3 * b
                    rhs = weight[tap : tap + 3].reshape(3 * full, half)
                    total += jnp.dot(lhs, rhs, preferred_element_type=jnp.float32)
            value = (total + first_bias).astype(jnp.bfloat16).astype(jnp.float32)
            put(produced, span(frame, row), value)
            sums[2:3, 0:half] += jnp.sum(value, axis=0, keepdims=True)

        over_pieces(convolve)

    mean = group_mean(jnp.broadcast_to(sums[2:3, 0:half], (8, half)), per_group, cells)
    for frame in range(F):

        def squares_again(row):
            spread = take(produced, span(frame, row), half) - mean
            sums[3:4, 0:half] += jnp.sum(spread * spread, axis=0, keepdims=True)

        over_pieces(squares_again)
    variance = group_mean(jnp.broadcast_to(sums[3:4, 0:half], (8, half)), per_group, cells)
    scale = lax.rsqrt(variance + EPSILON) * small_own[5:6]
    second_shift = small_own[6:7]
    for spot_at in range(W_DEV + 2 * HALO):
        value = take(produced, pl.ds(spot_at, F * H, stride=width), half)
        value = silu((value - mean) * scale + second_shift)
        real = (leftmost + spot_at >= 0) & (leftmost + spot_at < width)
        act_out[spot_at] = jnp.where(real, value, 0.0).astype(jnp.bfloat16)
    frames = F // 2
    for spot_at in range(1, W_DEV + 3):
        begin = core * (frames * H * width) + spot_at
        value = take(hidden, pl.ds(begin, frames * H, stride=width), full)
        hidden_out[spot_at - 1] = value.astype(jnp.bfloat16)


def second_kernel(
    tile_count,
    act_own,
    act_other,
    hidden_in,
    weight_own,
    weight_other,
    small_own,
    small_other,
    up_weight,
    up_bias,
    out,
    slots,
    taps,
    flat,
):
    width = tile_count * W_DEV
    me = lax.axis_index("tile")
    core = lax.axis_index("chan")
    columns, cells, half = act_own.shape
    full = 2 * half
    frames = F // 2
    rows = frames * H
    inner = columns - 2
    slots[...] = jnp.zeros_like(slots)
    for column in range(columns):
        value = joined(
            act_own[column].astype(jnp.float32), act_other[column].astype(jnp.float32), core
        )
        before = jnp.where(core == 0, 0.0, value[0:rows])
        now = jnp.where(core == 0, value[0:rows], value[rows:])
        for slot in range(frames):
            at = slot * 32 + 8
            slots[column, at : at + H, :] = before[slot * H : (slot + 1) * H]
            at = (slot + frames) * 32 + 8
            slots[column, at : at + H, :] = now[slot * H : (slot + 1) * H]
    for a in range(3):
        for b in range(3):
            parts = []
            for frame in range(frames):
                at = (frame + a) * 32 + 7 + b
                parts.append(slots[:, at : at + H, :])
            taps[3 * a + b] = jnp.concatenate(parts, axis=1).astype(jnp.bfloat16)
    mine = jnp.zeros((inner * rows, half), jnp.float32)
    theirs = jnp.zeros((inner * rows, half), jnp.float32)
    for pair in range(9):
        lhs = jnp.concatenate(
            [taps[pair, e : e + inner].reshape(inner * rows, full) for e in range(3)], axis=1
        )
        rhs = weight_own[3 * pair : 3 * pair + 3].reshape(3 * full, half)
        mine += jnp.dot(lhs, rhs, preferred_element_type=jnp.float32)
        rhs = weight_other[3 * pair : 3 * pair + 3].reshape(3 * full, half)
        theirs += jnp.dot(lhs, rhs, preferred_element_type=jnp.float32)
    second_out = joined(mine + small_own[3:4], theirs + small_other[3:4], core)
    hidden = hidden_in[...].astype(jnp.float32) + second_out.reshape(inner, rows, full)
    spot = lax.broadcasted_iota(jnp.int32, (inner, rows, full), 0) + me * W_DEV - 1
    hidden = jnp.where((spot >= 0) & (spot < width), hidden, 0.0).astype(jnp.bfloat16)
    hidden = hidden.reshape(inner * rows, full)

    line = lax.broadcasted_iota(jnp.int32, (inner * frames, H, half), 1)
    upper, lower = [], []
    for e in range(3):
        made = [
            jnp.dot(hidden, up_weight[3 * b + e], preferred_element_type=jnp.float32).reshape(
                inner * frames, H, half
            )
            for b in range(3)
        ]
        above = jnp.where(line == 0, 0.0, pltpu.roll(made[0], 1, axis=1))
        below = jnp.where(line == H - 1, 0.0, pltpu.roll(made[2], H - 1, axis=1))
        upper.append((above + made[1] + made[2]).reshape(inner, frames, H, half))
        lower.append((made[0] + made[1] + below).reshape(inner, frames, H, half))
    bias = up_bias[...]
    span = 2 * W_DEV
    for parity, sums in ((0, upper), (1, lower)):
        for x in range(W_DEV):
            at = x + 1
            for side in range(2):
                if side == 0:
                    value = sums[0][at - 1] + sums[1][at] + sums[2][at]
                else:
                    value = sums[0][at] + sums[1][at] + sums[2][at + 1]
                for frame in range(frames):
                    begin = frame * 2 * H * span + parity * span + 2 * x + side
                    put(flat, pl.ds(begin, H, stride=2 * span), value[frame] + bias)
    out[...] = take(flat, slice(None), out.shape[-1]).astype(jnp.bfloat16).reshape(out.shape)


def gathered(block, axis):
    count = lax.axis_size(axis)
    if count & (count - 1):
        return lax.all_gather(block, axis, axis=0, tiled=True), False
    step = 1
    while step < count:
        moved = lax.ppermute(block, axis, [(i, i ^ step) for i in range(count)])
        block = jnp.concatenate([block, moved], axis=0)
        step *= 2
    return block, True


def on_device(
    owner_latent,
    tile_counts,
    stem_weight,
    stem_bias,
    first_gain,
    first_shift,
    first_weight,
    first_bias,
    second_gain,
    second_shift,
    second_weight,
    second_bias,
    upsample_weight,
    upsample_bias,
):
    tile_count = lax.axis_size("tile")
    width = tile_count * W_DEV
    _, slot_count, row_length = owner_latent.shape
    zc, half = stem_weight.shape[1], stem_weight.shape[2]
    full = 2 * half
    out_channels = upsample_weight.shape[2]
    swap = [(0, 1), (1, 0)]
    frames = F // 2

    padded = owner_latent.reshape(1, slot_count, F, H, zc)
    padded = jnp.pad(
        padded, ((0, 0), (0, PITCH - slot_count), (0, 0), (1, H_PAD - H - 1), (0, 0))
    ).reshape(1, PITCH, F * H_PAD * zc)
    small = jnp.stack(
        [
            stem_bias,
            first_gain,
            first_shift,
            second_bias,
            first_bias,
            second_gain,
            second_shift,
            jnp.zeros_like(stem_bias),
        ]
    )
    small_other = lax.ppermute(small, "chan", swap)
    stem_other = lax.ppermute(stem_weight, "chan", swap)
    second_other = lax.ppermute(second_weight, "chan", swap)
    owners, power = gathered(padded, "tile")
    owners = owners.reshape(tile_count * PITCH, F * H_PAD * zc)

    window = W_DEV + 2 * HALO
    vmem = pl.BlockSpec(memory_space=pltpu.VMEM)
    act, hidden = pl.pallas_call(
        functools.partial(first_kernel, power),
        out_shape=(
            jax.ShapeDtypeStruct((window, F * H, half), jnp.bfloat16),
            jax.ShapeDtypeStruct((window - 2, frames * H, full), jnp.bfloat16),
        ),
        in_specs=[pl.BlockSpec(memory_space=pltpu.SMEM)] + [vmem] * 6,
        out_specs=(vmem, vmem),
        scratch_shapes=[
            pltpu.VMEM((3, F, width, H_PAD * zc), jnp.float32),
            pltpu.VMEM((F, H, width, 256), jnp.bfloat16),
            pltpu.VMEM((3, 256, full), jnp.bfloat16),
            pltpu.VMEM((full // 128, F * H * width, 128), jnp.float32),
            pltpu.VMEM((3, F, H + 2, width, full), jnp.bfloat16),
            pltpu.VMEM((pl.cdiv(half, 128), F * H * width, 128), jnp.float32),
            pltpu.VMEM((8, full), jnp.float32),
        ],
        cost_estimate=pl.CostEstimate(
            flops=2 * F * H * width * 27 * full * half * 3 // 4,
            bytes_accessed=27 * full * half * 2,
            transcendentals=F * H * width * full,
        ),
        compiler_params=pltpu.CompilerParams(vmem_limit_bytes=60 * 1024 * 1024),
    )(tile_counts, owners, stem_weight, stem_other, small, small_other, first_weight)

    act_other = lax.ppermute(act, "chan", swap)

    out = pl.pallas_call(
        functools.partial(second_kernel, tile_count),
        out_shape=jax.ShapeDtypeStruct((frames, 2 * H, 2 * W_DEV, out_channels), jnp.bfloat16),
        in_specs=[vmem] * 9,
        out_specs=vmem,
        scratch_shapes=[
            pltpu.VMEM((window, 2 * frames * 32 + 8, full), jnp.float32),
            pltpu.VMEM((9, window, frames * H, full), jnp.bfloat16),
            pltpu.VMEM((pl.cdiv(out_channels, 128), frames * 2 * H * 2 * W_DEV, 128), jnp.float32),
        ],
        cost_estimate=pl.CostEstimate(
            flops=2 * 4 * 48 * 27 * full * full,
            bytes_accessed=2 * 27 * full * half * 2,
            transcendentals=0,
        ),
        compiler_params=pltpu.CompilerParams(vmem_limit_bytes=40 * 1024 * 1024),
    )(
        act,
        act_other,
        hidden,
        second_weight,
        second_other,
        small,
        small_other,
        upsample_weight,
        upsample_bias.reshape(1, -1),
    )
    return out


def solution(mesh):
    placed = (
        P(("clip", "tile"), None, None),
        P("clip"),
        P(None, None, "chan"),
        P("chan"),
        P("chan"),
        P("chan"),
        P(None, None, "chan"),
        P("chan"),
        P("chan"),
        P("chan"),
        P(None, None, "chan"),
        P("chan"),
        P(),
        P(),
    )
    return jax.shard_map(
        on_device,
        mesh=mesh,
        in_specs=placed,
        out_specs=P(("clip", "chan"), None, "tile", None),
        check_vma=False,
    )
```

```python
import functools

import jax
import jax.numpy as jnp
from jax import lax
from jax.experimental import pallas as pl
from jax.experimental.pallas import tpu as pltpu
from jax.sharding import PartitionSpec as P

GROUPS = 32
F = 4
H = 24
W_DEV = 2
HALO = 2
PITCH = 8
H_PAD = 32
EPSILON = 1e-06


def joined(own, other, core):
    low = jnp.concatenate([own, other], axis=-1)
    high = jnp.concatenate([other, own], axis=-1)
    return jnp.where(core == 0, low, high)


def group_mean(column_sums, per_group, cells):
    channels = column_sums.shape[1]
    row = lax.broadcasted_iota(jnp.int32, (channels, channels), 0).astype(jnp.float32)
    column = lax.broadcasted_iota(jnp.int32, (channels, channels), 1).astype(jnp.float32)
    same = jnp.floor((row + 0.5) / per_group) == jnp.floor((column + 0.5) / per_group)
    total = jnp.dot(
        column_sums,
        same.astype(jnp.float32),
        precision=lax.Precision.HIGHEST,
        preferred_element_type=jnp.float32,
    )
    return total[0:1] * (1.0 / (cells * per_group))


def put(ref, place, value):
    for block in range(ref.shape[0]):
        part = value[:, block * 128 : (block + 1) * 128]
        ref[block, place, 0 : part.shape[1]] = part


def take(ref, place, channels):
    parts = []
    for block in range(ref.shape[0]):
        parts.append(ref[block, place, :][:, : channels - block * 128])
    return jnp.concatenate(parts, axis=1)


def times(lhs, weight, taps):
    rhs = jnp.concatenate([weight[tap] for tap in taps], axis=1)
    return lax.dot_general(lhs, rhs, (((1,), (1,)), ((), ())), preferred_element_type=jnp.float32)


def silu(value):
    half = 0.5 * value
    return half + half * jnp.tanh(half)


def first_kernel(
    power,
    counts,
    owners,
    stem_own,
    stem_other,
    small_own,
    small_other,
    weight_far,
    act_out,
    hidden_out,
    shifted,
    patches,
    stem_full,
    hidden,
    acts,
    produced,
    sums,
    weight,
    arrival,
):
    fetch = pltpu.make_async_copy(weight_far, weight, arrival)
    fetch.start()
    tile_count = counts.shape[0]
    width = tile_count * W_DEV
    me = lax.axis_index("tile")
    core = lax.axis_index("chan")
    zc, half = stem_own.shape[1], stem_own.shape[2]
    full = 2 * half
    frame_lanes = H_PAD * zc
    pieces = max(1, width // 16)
    rows = H // pieces
    cells = F * H * width
    leftmost = me * W_DEV - HALO

    slots = PITCH * tile_count
    lane = lax.broadcasted_iota(jnp.int32, (3 * width, slots), 1)
    owner_at = lane // PITCH
    slot_at = lane - owner_at * PITCH
    held = jnp.full((3 * width, slots), -5, jnp.int32)
    start = jnp.int32(0)
    for owner in range(tile_count):
        place = (me ^ owner) if power else jnp.int32(owner)
        count = counts[owner]
        held = jnp.where((owner_at == place) & (slot_at < count), start + slot_at, held)
        start = start + count
    position = lax.broadcasted_iota(jnp.int32, (3 * width, slots), 0)
    shift = (position >= width).astype(jnp.int32) + (position >= 2 * width).astype(jnp.int32)
    column = position - shift * width + leftmost
    column = jnp.where(column < 0, column + width, column)
    column = jnp.where(column >= width, column - width, column)
    selection = (held == column + shift - 1).astype(jnp.bfloat16)
    for frame in range(F):
        lanes = slice(frame * frame_lanes, (frame + 1) * frame_lanes)
        chosen = jnp.dot(selection, owners[:, lanes], preferred_element_type=jnp.float32)
        shifted[:, frame] = chosen.reshape(3, width, frame_lanes)

    stem_full[...] = jnp.zeros(stem_full.shape, jnp.bfloat16)
    for tap in range(27):
        a, b, e = tap // 9, tap // 3 % 3, tap % 3
        at = e * 4 * zc + b * zc
        stem_full[a, at : at + zc, :] = joined(stem_own[tap], stem_other[tap], core)
    stem_bias = joined(small_own[0:1], small_other[0:1], core)
    first_gain = joined(small_own[1:2], small_other[1:2], core)
    first_shift = joined(small_own[2:3], small_other[2:3], core)

    per_block = 128 // zc
    lane128 = lax.broadcasted_iota(jnp.int32, (F, width, 128), 2)
    for row in range(H):
        block = row // per_block * 128
        offset = row % per_block * zc
        window = shifted[:, :, :, block : block + 256]
        one = pltpu.roll(window[0], (256 - offset) % 256, axis=2)[:, :, :128]
        two = pltpu.roll(window[1], (320 - offset) % 256, axis=2)[:, :, :128]
        three = pltpu.roll(window[2], (256 - offset) % 256, axis=2)[:, :, :128]
        patches[:, row, :, 0:128] = jnp.where(lane128 < 64, one, two).astype(jnp.bfloat16)
        patches[:, row, :, 128:256] = three.astype(jnp.bfloat16)

    def over_pieces(body):
        if pieces == 1:
            body(0)
        else:
            lax.fori_loop(0, pieces, lambda i, _: (body(i * rows), 0)[1], 0)

    def span(frame, row):
        return pl.ds(pl.multiple_of((frame * H + row) * width, 16), rows * width)

    sums[...] = jnp.zeros_like(sums)
    for frame in range(F):

        def stem(row):
            total = jnp.zeros((rows * width, full), jnp.float32)
            for a in range(max(0, 2 - frame), 3):
                lhs = patches[frame + a - 2, pl.ds(row, rows)].reshape(rows * width, 256)
                total += jnp.dot(lhs, stem_full[a], preferred_element_type=jnp.float32)
            value = (total + stem_bias).astype(jnp.bfloat16).astype(jnp.float32)
            put(hidden, span(frame, row), value)
            sums[0:1, :] += jnp.sum(value, axis=0, keepdims=True)

        over_pieces(stem)

    per_group = full // GROUPS
    mean = group_mean(jnp.broadcast_to(sums[0:1, :], (8, full)), per_group, cells)
    for frame in range(F):

        def squares(row):
            spread = take(hidden, span(frame, row), full) - mean
            sums[1:2, :] += jnp.sum(spread * spread, axis=0, keepdims=True)

        over_pieces(squares)
    variance = group_mean(jnp.broadcast_to(sums[1:2, :], (8, full)), per_group, cells)
    scale = lax.rsqrt(variance + EPSILON) * first_gain

    spot = lax.broadcasted_iota(jnp.int32, (1, width, full), 1) + leftmost
    spot = jnp.where(spot < 0, spot + width, spot)
    spot = jnp.where(spot >= width, spot - width, spot)
    zero_row = jnp.zeros((width, full), jnp.bfloat16)
    for e in range(3):
        for frame in range(F):
            acts[e, frame, 0] = zero_row
            acts[e, frame, H + 1] = zero_row
    for frame in range(F):

        def activate(row):
            spread = take(hidden, span(frame, row), full) - mean
            value = silu(spread * scale + first_shift).reshape(rows, width, full)
            left = jnp.where(spot == 0, 0.0, pltpu.roll(value, 1, axis=1))
            right = jnp.where(spot == width - 1, 0.0, pltpu.roll(value, width - 1, axis=1))
            place = pl.ds(row + 1, rows)
            acts[0, frame, place] = left.astype(jnp.bfloat16)
            acts[1, frame, place] = value.astype(jnp.bfloat16)
            acts[2, frame, place] = right.astype(jnp.bfloat16)

        over_pieces(activate)

    fetch.wait()
    first_bias = small_own[4:5]
    for frame in range(F):

        def convolve(row):
            total = jnp.zeros((rows * width, half), jnp.float32)
            for a in range(max(0, 2 - frame), 3):
                for b in range(3):
                    lhs = jnp.concatenate(
                        [
                            acts[e, frame + a - 2, pl.ds(row + b, rows)].reshape(rows * width, full)
                            for e in range(3)
                        ],
                        axis=1,
                    )
                    tap = 9 * a + 3 * b
                    total += times(lhs, weight, range(tap, tap + 3))
            value = (total + first_bias).astype(jnp.bfloat16).astype(jnp.float32)
            put(produced, span(frame, row), value)
            sums[2:3, 0:half] += jnp.sum(value, axis=0, keepdims=True)

        over_pieces(convolve)

    mean = group_mean(jnp.broadcast_to(sums[2:3, 0:half], (8, half)), per_group, cells)
    for frame in range(F):

        def squares_again(row):
            spread = take(produced, span(frame, row), half) - mean
            sums[3:4, 0:half] += jnp.sum(spread * spread, axis=0, keepdims=True)

        over_pieces(squares_again)
    variance = group_mean(jnp.broadcast_to(sums[3:4, 0:half], (8, half)), per_group, cells)
    scale = lax.rsqrt(variance + EPSILON) * small_own[5:6]
    second_shift = small_own[6:7]
    for spot_at in range(W_DEV + 2 * HALO):
        value = take(produced, pl.ds(spot_at, F * H, stride=width), half)
        value = silu((value - mean) * scale + second_shift)
        real = (leftmost + spot_at >= 0) & (leftmost + spot_at < width)
        act_out[spot_at] = jnp.where(real, value, 0.0).astype(jnp.bfloat16)
    frames = F // 2
    for spot_at in range(1, W_DEV + 3):
        begin = core * (frames * H * width) + spot_at
        value = take(hidden, pl.ds(begin, frames * H, stride=width), full)
        hidden_out[spot_at - 1] = value.astype(jnp.bfloat16)


def second_kernel(
    tile_count,
    act_own,
    act_other,
    hidden_in,
    weight_own,
    weight_far,
    small_own,
    small_other,
    up_weight,
    up_bias,
    out,
    slots,
    taps,
    flat,
    weight_other,
    arrival,
):
    fetch = pltpu.make_async_copy(weight_far, weight_other, arrival)
    fetch.start()
    width = tile_count * W_DEV
    me = lax.axis_index("tile")
    core = lax.axis_index("chan")
    columns, cells, half = act_own.shape
    full = 2 * half
    frames = F // 2
    rows = frames * H
    inner = columns - 2
    slots[...] = jnp.zeros_like(slots)
    for column in range(columns):
        value = joined(
            act_own[column].astype(jnp.float32), act_other[column].astype(jnp.float32), core
        )
        before = jnp.where(core == 0, 0.0, value[0:rows])
        now = jnp.where(core == 0, value[0:rows], value[rows:])
        for slot in range(frames):
            at = slot * 32 + 8
            slots[column, at : at + H, :] = before[slot * H : (slot + 1) * H]
            at = (slot + frames) * 32 + 8
            slots[column, at : at + H, :] = now[slot * H : (slot + 1) * H]
    for a in range(3):
        for b in range(3):
            parts = []
            for frame in range(frames):
                at = (frame + a) * 32 + 7 + b
                parts.append(slots[:, at : at + H, :])
            taps[3 * a + b] = jnp.concatenate(parts, axis=1).astype(jnp.bfloat16)


    def convolve(weight):
        total = jnp.zeros((inner * rows, half), jnp.float32)
        for pair in range(9):
            lhs = jnp.concatenate(
                [taps[pair, e : e + inner].reshape(inner * rows, full) for e in range(3)], axis=1
            )
            total += times(lhs, weight, range(3 * pair, 3 * pair + 3))
        return total

    mine = convolve(weight_own)
    fetch.wait()
    theirs = convolve(weight_other)
    second_out = joined(mine + small_own[3:4], theirs + small_other[3:4], core)
    hidden = hidden_in[...].astype(jnp.float32) + second_out.reshape(inner, rows, full)
    spot = lax.broadcasted_iota(jnp.int32, (inner, rows, full), 0) + me * W_DEV - 1
    hidden = jnp.where((spot >= 0) & (spot < width), hidden, 0.0).astype(jnp.bfloat16)
    hidden = hidden.reshape(inner * rows, full)

    line = lax.broadcasted_iota(jnp.int32, (inner * frames, H, half), 1)
    upper, lower = [], []
    for e in range(3):
        made = [
            times(hidden, up_weight, [3 * b + e]).reshape(inner * frames, H, half)
            for b in range(3)
        ]
        above = jnp.where(line == 0, 0.0, pltpu.roll(made[0], 1, axis=1))
        below = jnp.where(line == H - 1, 0.0, pltpu.roll(made[2], H - 1, axis=1))
        upper.append((above + made[1] + made[2]).reshape(inner, frames, H, half))
        lower.append((made[0] + made[1] + below).reshape(inner, frames, H, half))
    bias = up_bias[...]
    span = 2 * W_DEV
    for parity, sums in ((0, upper), (1, lower)):
        for x in range(W_DEV):
            at = x + 1
            for side in range(2):
                if side == 0:
                    value = sums[0][at - 1] + sums[1][at] + sums[2][at]
                else:
                    value = sums[0][at] + sums[1][at] + sums[2][at + 1]
                for frame in range(frames):
                    begin = frame * 2 * H * span + parity * span + 2 * x + side
                    put(flat, pl.ds(begin, H, stride=2 * span), value[frame] + bias)
    out[...] = take(flat, slice(None), out.shape[-1]).astype(jnp.bfloat16).reshape(out.shape)


def gathered(block, axis):
    count = lax.axis_size(axis)
    if count & (count - 1):
        return lax.all_gather(block, axis, axis=0, tiled=True), False
    step = 1
    while step < count:
        moved = lax.ppermute(block, axis, [(i, i ^ step) for i in range(count)])
        block = jnp.concatenate([block, moved], axis=0)
        step *= 2
    return block, True


def on_device(
    owner_latent,
    tile_counts,
    stem_weight,
    stem_bias,
    first_gain,
    first_shift,
    first_weight,
    first_bias,
    second_gain,
    second_shift,
    second_weight,
    second_bias,
    upsample_weight,
    upsample_bias,
):
    tile_count = lax.axis_size("tile")
    width = tile_count * W_DEV
    _, slot_count, row_length = owner_latent.shape
    zc, half = stem_weight.shape[1], stem_weight.shape[2]
    full = 2 * half
    out_channels = upsample_weight.shape[2]
    first_weight = first_weight.transpose(0, 2, 1)
    second_weight = second_weight.transpose(0, 2, 1)
    upsample_weight = upsample_weight.transpose(0, 2, 1)
    swap = [(0, 1), (1, 0)]
    frames = F // 2

    padded = owner_latent.reshape(1, slot_count, F, H, zc)
    padded = jnp.pad(
        padded, ((0, 0), (0, PITCH - slot_count), (0, 0), (1, H_PAD - H - 1), (0, 0))
    ).reshape(1, PITCH, F * H_PAD * zc)
    small = jnp.stack(
        [
            stem_bias,
            first_gain,
            first_shift,
            second_bias,
            first_bias,
            second_gain,
            second_shift,
            jnp.zeros_like(stem_bias),
        ]
    )
    small_other = lax.ppermute(small, "chan", swap)
    stem_other = lax.ppermute(stem_weight, "chan", swap)
    second_other = lax.ppermute(second_weight, "chan", swap)
    owners, power = gathered(padded, "tile")
    owners = owners.reshape(tile_count * PITCH, F * H_PAD * zc)

    window = W_DEV + 2 * HALO
    vmem = pl.BlockSpec(memory_space=pltpu.VMEM)
    far = pl.BlockSpec(memory_space=pltpu.HBM)
    act, hidden = pl.pallas_call(
        functools.partial(first_kernel, power),
        out_shape=(
            jax.ShapeDtypeStruct((window, F * H, half), jnp.bfloat16),
            jax.ShapeDtypeStruct((window - 2, frames * H, full), jnp.bfloat16),
        ),
        in_specs=[pl.BlockSpec(memory_space=pltpu.SMEM)] + [vmem] * 5 + [far],
        out_specs=(vmem, vmem),
        scratch_shapes=[
            pltpu.VMEM((3, F, width, H_PAD * zc), jnp.float32),
            pltpu.VMEM((F, H, width, 256), jnp.bfloat16),
            pltpu.VMEM((3, 256, full), jnp.bfloat16),
            pltpu.VMEM((full // 128, F * H * width, 128), jnp.float32),
            pltpu.VMEM((3, F, H + 2, width, full), jnp.bfloat16),
            pltpu.VMEM((pl.cdiv(half, 128), F * H * width, 128), jnp.float32),
            pltpu.VMEM((8, full), jnp.float32),
            pltpu.VMEM(first_weight.shape, jnp.bfloat16),
            pltpu.SemaphoreType.DMA,
        ],
        cost_estimate=pl.CostEstimate(
            flops=2 * F * H * width * 27 * full * half * 3 // 4,
            bytes_accessed=27 * full * half * 2,
            transcendentals=F * H * width * full,
        ),
        compiler_params=pltpu.CompilerParams(vmem_limit_bytes=min(60, 12 + 12 * width // 16) * 1024 * 1024),
    )(tile_counts, owners, stem_weight, stem_other, small, small_other, first_weight)

    act_other = lax.ppermute(act, "chan", swap)

    out = pl.pallas_call(
        functools.partial(second_kernel, tile_count),
        out_shape=jax.ShapeDtypeStruct((frames, 2 * H, 2 * W_DEV, out_channels), jnp.bfloat16),
        in_specs=[vmem] * 4 + [far] + [vmem] * 4,
        out_specs=vmem,
        scratch_shapes=[
            pltpu.VMEM((window, 2 * frames * 32 + 8, full), jnp.float32),
            pltpu.VMEM((9, window, frames * H, full), jnp.bfloat16),
            pltpu.VMEM((pl.cdiv(out_channels, 128), frames * 2 * H * 2 * W_DEV, 128), jnp.float32),
            pltpu.VMEM(second_weight.shape, jnp.bfloat16),
            pltpu.SemaphoreType.DMA,
        ],
        cost_estimate=pl.CostEstimate(
            flops=2 * 4 * 48 * 27 * full * full,
            bytes_accessed=2 * 27 * full * half * 2,
            transcendentals=0,
        ),
        compiler_params=pltpu.CompilerParams(vmem_limit_bytes=24 * 1024 * 1024),
    )(
        act,
        act_other,
        hidden,
        second_weight,
        second_other,
        small,
        small_other,
        upsample_weight,
        upsample_bias.reshape(1, -1),
    )
    return out


def solution(mesh):
    placed = (
        P(("clip", "tile"), None, None),
        P("clip"),
        P(None, None, "chan"),
        P("chan"),
        P("chan"),
        P("chan"),
        P(None, None, "chan"),
        P("chan"),
        P("chan"),
        P("chan"),
        P(None, None, "chan"),
        P("chan"),
        P(),
        P(),
    )
    return jax.shard_map(
        on_device,
        mesh=mesh,
        in_specs=placed,
        out_specs=P(("clip", "chan"), None, "tile", None),
        check_vma=False,
    )
```

```python
import functools

import jax
import jax.numpy as jnp
from jax import lax
from jax.experimental import pallas as pl
from jax.experimental.pallas import tpu as pltpu
from jax.sharding import PartitionSpec as P

GROUPS = 32
F = 4
H = 24
W_DEV = 2
HALO = 2
PITCH = 8
H_PAD = 32
EPSILON = 1e-06


def joined(own, other, core):
    low = jnp.concatenate([own, other], axis=-1)
    high = jnp.concatenate([other, own], axis=-1)
    return jnp.where(core == 0, low, high)


def group_mean(column_sums, per_group, cells):
    channels = column_sums.shape[1]
    row = lax.broadcasted_iota(jnp.int32, (channels, channels), 0).astype(jnp.float32)
    column = lax.broadcasted_iota(jnp.int32, (channels, channels), 1).astype(jnp.float32)
    same = jnp.floor((row + 0.5) / per_group) == jnp.floor((column + 0.5) / per_group)
    total = jnp.dot(
        column_sums,
        same.astype(jnp.float32),
        precision=lax.Precision.HIGHEST,
        preferred_element_type=jnp.float32,
    )
    return total[0:1] * (1.0 / (cells * per_group))


def put(ref, place, value):
    for block in range(ref.shape[0]):
        part = value[:, block * 128 : (block + 1) * 128]
        ref[block, place, 0 : part.shape[1]] = part


def take(ref, place, channels):
    parts = []
    for block in range(ref.shape[0]):
        parts.append(ref[block, place, :][:, : channels - block * 128])
    return jnp.concatenate(parts, axis=1)


def times(lhs, weight, taps):
    rhs = jnp.concatenate([weight[tap] for tap in taps], axis=1)
    return lax.dot_general(lhs, rhs, (((1,), (1,)), ((), ())), preferred_element_type=jnp.float32)


def silu(value):
    half = 0.5 * value
    return half + half * jnp.tanh(half)


def prepare_kernel(
    power, counts, stem_own, stem_other, small_own, small_other, selection, stem_full, vectors
):
    tile_count = counts.shape[0]
    width = tile_count * W_DEV
    me = lax.axis_index("tile")
    core = lax.axis_index("chan")
    zc = stem_own.shape[1]
    leftmost = me * W_DEV - HALO

    slots = PITCH * tile_count
    lane = lax.broadcasted_iota(jnp.int32, (3 * width, slots), 1)
    owner_at = lane // PITCH
    slot_at = lane - owner_at * PITCH
    held = jnp.full((3 * width, slots), -5, jnp.int32)
    start = jnp.int32(0)
    for owner in range(tile_count):
        place = (me ^ owner) if power else jnp.int32(owner)
        count = counts[owner]
        held = jnp.where((owner_at == place) & (slot_at < count), start + slot_at, held)
        start = start + count
    position = lax.broadcasted_iota(jnp.int32, (3 * width, slots), 0)
    shift = (position >= width).astype(jnp.int32) + (position >= 2 * width).astype(jnp.int32)
    column = position - shift * width + leftmost
    column = jnp.where(column < 0, column + width, column)
    column = jnp.where(column >= width, column - width, column)
    selection[...] = (held == column + shift - 1).astype(jnp.bfloat16)

    stem_full[...] = jnp.zeros(stem_full.shape, jnp.bfloat16)
    for tap in range(27):
        a, b, e = tap // 9, tap // 3 % 3, tap % 3
        at = e * 4 * zc + b * zc
        stem_full[a, at : at + zc, :] = joined(stem_own[tap], stem_other[tap], core)
    vectors[...] = joined(small_own[...], small_other[...], core)


def first_kernel(
    owners,
    selection,
    stem_full,
    vectors,
    small_own,
    weight_far,
    act_out,
    hidden_out,
    shifted,
    patches,
    hidden,
    acts,
    produced,
    sums,
    weight,
    arrival,
):
    fetch = pltpu.make_async_copy(weight_far, weight, arrival)
    fetch.start()
    tile_count = owners.shape[0] // PITCH
    width = tile_count * W_DEV
    me = lax.axis_index("tile")
    core = lax.axis_index("chan")
    full, half = vectors.shape[1], small_own.shape[1]
    frame_lanes = owners.shape[1] // F
    zc = frame_lanes // H_PAD
    pieces = max(1, width // 16)
    rows = H // pieces
    cells = F * H * width
    leftmost = me * W_DEV - HALO
    for frame in range(F):
        lanes = slice(frame * frame_lanes, (frame + 1) * frame_lanes)
        chosen = jnp.dot(selection[...], owners[:, lanes], preferred_element_type=jnp.float32)
        shifted[:, frame] = chosen.reshape(3, width, frame_lanes)

    stem_bias = vectors[0:1]
    first_gain = vectors[1:2]
    first_shift = vectors[2:3]

    per_block = 128 // zc
    lane128 = lax.broadcasted_iota(jnp.int32, (F, width, 128), 2)
    for row in range(H):
        block = row // per_block * 128
        offset = row % per_block * zc
        window = shifted[:, :, :, block : block + 256]
        one = pltpu.roll(window[0], (256 - offset) % 256, axis=2)[:, :, :128]
        two = pltpu.roll(window[1], (320 - offset) % 256, axis=2)[:, :, :128]
        three = pltpu.roll(window[2], (256 - offset) % 256, axis=2)[:, :, :128]
        patches[:, row, :, 0:128] = jnp.where(lane128 < 64, one, two).astype(jnp.bfloat16)
        patches[:, row, :, 128:256] = three.astype(jnp.bfloat16)

    def over_pieces(body):
        if pieces == 1:
            body(0)
        else:
            lax.fori_loop(0, pieces, lambda i, _: (body(i * rows), 0)[1], 0)

    def span(frame, row):
        return pl.ds(pl.multiple_of((frame * H + row) * width, 16), rows * width)

    sums[...] = jnp.zeros_like(sums)
    for frame in range(F):

        def stem(row):
            total = jnp.zeros((rows * width, full), jnp.float32)
            for a in range(max(0, 2 - frame), 3):
                lhs = patches[frame + a - 2, pl.ds(row, rows)].reshape(rows * width, 256)
                total += jnp.dot(lhs, stem_full[a], preferred_element_type=jnp.float32)
            value = (total + stem_bias).astype(jnp.bfloat16).astype(jnp.float32)
            put(hidden, span(frame, row), value)
            sums[0:1, :] += jnp.sum(value, axis=0, keepdims=True)

        over_pieces(stem)

    per_group = full // GROUPS
    mean = group_mean(jnp.broadcast_to(sums[0:1, :], (8, full)), per_group, cells)
    for frame in range(F):

        def squares(row):
            spread = take(hidden, span(frame, row), full) - mean
            sums[1:2, :] += jnp.sum(spread * spread, axis=0, keepdims=True)

        over_pieces(squares)
    variance = group_mean(jnp.broadcast_to(sums[1:2, :], (8, full)), per_group, cells)
    scale = lax.rsqrt(variance + EPSILON) * first_gain

    spot = lax.broadcasted_iota(jnp.int32, (1, width, full), 1) + leftmost
    spot = jnp.where(spot < 0, spot + width, spot)
    spot = jnp.where(spot >= width, spot - width, spot)
    zero_row = jnp.zeros((width, full), jnp.bfloat16)
    for e in range(3):
        for frame in range(F):
            acts[e, frame, 0] = zero_row
            acts[e, frame, H + 1] = zero_row
    for frame in range(F):

        def activate(row):
            spread = take(hidden, span(frame, row), full) - mean
            value = silu(spread * scale + first_shift).reshape(rows, width, full)
            left = jnp.where(spot == 0, 0.0, pltpu.roll(value, 1, axis=1))
            right = jnp.where(spot == width - 1, 0.0, pltpu.roll(value, width - 1, axis=1))
            place = pl.ds(row + 1, rows)
            acts[0, frame, place] = left.astype(jnp.bfloat16)
            acts[1, frame, place] = value.astype(jnp.bfloat16)
            acts[2, frame, place] = right.astype(jnp.bfloat16)

        over_pieces(activate)

    fetch.wait()
    first_bias = small_own[4:5]
    for frame in range(F):

        def convolve(row):
            used = range(max(0, 2 - frame) * 9, 27)
            lhs = jnp.concatenate(
                [
                    acts[tap % 3, frame + tap // 9 - 2, pl.ds(row + tap // 3 % 3, rows)].reshape(
                        rows * width, full
                    )
                    for tap in used
                ],
                axis=1,
            )
            total = times(lhs, weight, used)
            value = (total + first_bias).astype(jnp.bfloat16).astype(jnp.float32)
            put(produced, span(frame, row), value)
            sums[2:3, 0:half] += jnp.sum(value, axis=0, keepdims=True)

        over_pieces(convolve)

    mean = group_mean(jnp.broadcast_to(sums[2:3, 0:half], (8, half)), per_group, cells)
    for frame in range(F):

        def squares_again(row):
            spread = take(produced, span(frame, row), half) - mean
            sums[3:4, 0:half] += jnp.sum(spread * spread, axis=0, keepdims=True)

        over_pieces(squares_again)
    variance = group_mean(jnp.broadcast_to(sums[3:4, 0:half], (8, half)), per_group, cells)
    scale = lax.rsqrt(variance + EPSILON) * small_own[5:6]
    second_shift = small_own[6:7]
    for spot_at in range(W_DEV + 2 * HALO):
        value = take(produced, pl.ds(spot_at, F * H, stride=width), half)
        value = silu((value - mean) * scale + second_shift)
        real = (leftmost + spot_at >= 0) & (leftmost + spot_at < width)
        act_out[spot_at] = jnp.where(real, value, 0.0).astype(jnp.bfloat16)
    frames = F // 2
    for spot_at in range(1, W_DEV + 3):
        begin = core * (frames * H * width) + spot_at
        value = take(hidden, pl.ds(begin, frames * H, stride=width), full)
        hidden_out[spot_at - 1] = value.astype(jnp.bfloat16)


def second_kernel(
    tile_count,
    act_own,
    act_other,
    hidden_in,
    weight_own,
    weight_far,
    vectors,
    up_weight,
    up_bias,
    out,
    slots,
    taps,
    flat,
    weight_other,
    arrival,
):
    fetch = pltpu.make_async_copy(weight_far, weight_other, arrival)
    fetch.start()
    width = tile_count * W_DEV
    me = lax.axis_index("tile")
    core = lax.axis_index("chan")
    columns, cells, half = act_own.shape
    full = 2 * half
    frames = F // 2
    rows = frames * H
    inner = columns - 2
    slots[...] = jnp.zeros_like(slots)
    for column in range(columns):
        value = joined(
            act_own[column].astype(jnp.float32), act_other[column].astype(jnp.float32), core
        )
        before = jnp.where(core == 0, 0.0, value[0:rows])
        now = jnp.where(core == 0, value[0:rows], value[rows:])
        for slot in range(frames):
            at = slot * 32 + 8
            slots[column, at : at + H, :] = before[slot * H : (slot + 1) * H]
            at = (slot + frames) * 32 + 8
            slots[column, at : at + H, :] = now[slot * H : (slot + 1) * H]
    for a in range(3):
        for b in range(3):
            parts = []
            for frame in range(frames):
                at = (frame + a) * 32 + 7 + b
                parts.append(slots[:, at : at + H, :])
            taps[3 * a + b] = jnp.concatenate(parts, axis=1).astype(jnp.bfloat16)


    def convolve(weight):
        lhs = jnp.concatenate(
            [
                taps[tap // 3, tap % 3 : tap % 3 + inner].reshape(inner * rows, full)
                for tap in range(27)
            ],
            axis=1,
        )
        return times(lhs, weight, range(27))

    mine = convolve(weight_own)
    fetch.wait()
    theirs = convolve(weight_other)
    second_out = joined(mine, theirs, core) + vectors[3:4]
    hidden = hidden_in[...].astype(jnp.float32) + second_out.reshape(inner, rows, full)
    spot = lax.broadcasted_iota(jnp.int32, (inner, rows, full), 0) + me * W_DEV - 1
    hidden = jnp.where((spot >= 0) & (spot < width), hidden, 0.0).astype(jnp.bfloat16)
    hidden = hidden.reshape(inner * rows, full)

    line = lax.broadcasted_iota(jnp.int32, (inner * frames, H, half), 1)
    upper, lower = [], []
    for e in range(3):
        made = [
            times(hidden, up_weight, [3 * b + e]).reshape(inner * frames, H, half)
            for b in range(3)
        ]
        above = jnp.where(line == 0, 0.0, pltpu.roll(made[0], 1, axis=1))
        below = jnp.where(line == H - 1, 0.0, pltpu.roll(made[2], H - 1, axis=1))
        upper.append((above + made[1] + made[2]).reshape(inner, frames, H, half))
        lower.append((made[0] + made[1] + below).reshape(inner, frames, H, half))
    bias = up_bias[...]
    span = 2 * W_DEV
    for parity, sums in ((0, upper), (1, lower)):
        for x in range(W_DEV):
            at = x + 1
            for side in range(2):
                if side == 0:
                    value = sums[0][at - 1] + sums[1][at] + sums[2][at]
                else:
                    value = sums[0][at] + sums[1][at] + sums[2][at + 1]
                for frame in range(frames):
                    begin = frame * 2 * H * span + parity * span + 2 * x + side
                    put(flat, pl.ds(begin, H, stride=2 * span), value[frame] + bias)
    out[...] = take(flat, slice(None), out.shape[-1]).astype(jnp.bfloat16).reshape(out.shape)


def gathered(block, axis):
    count = lax.axis_size(axis)
    if count & (count - 1):
        return lax.all_gather(block, axis, axis=0, tiled=True), False
    step = 1
    while step < count:
        moved = lax.ppermute(block, axis, [(i, i ^ step) for i in range(count)])
        block = jnp.concatenate([block, moved], axis=0)
        step *= 2
    return block, True


def on_device(
    owner_latent,
    tile_counts,
    stem_weight,
    stem_bias,
    first_gain,
    first_shift,
    first_weight,
    first_bias,
    second_gain,
    second_shift,
    second_weight,
    second_bias,
    upsample_weight,
    upsample_bias,
):
    tile_count = lax.axis_size("tile")
    width = tile_count * W_DEV
    _, slot_count, row_length = owner_latent.shape
    zc, half = stem_weight.shape[1], stem_weight.shape[2]
    full = 2 * half
    out_channels = upsample_weight.shape[2]
    first_weight = first_weight.transpose(0, 2, 1)
    second_weight = second_weight.transpose(0, 2, 1)
    upsample_weight = upsample_weight.transpose(0, 2, 1)
    swap = [(0, 1), (1, 0)]
    frames = F // 2

    padded = owner_latent.reshape(1, slot_count, F, H, zc)
    padded = jnp.pad(
        padded, ((0, 0), (0, PITCH - slot_count), (0, 0), (1, H_PAD - H - 1), (0, 0))
    ).reshape(1, PITCH, F * H_PAD * zc)
    small = jnp.stack(
        [
            stem_bias,
            first_gain,
            first_shift,
            second_bias,
            first_bias,
            second_gain,
            second_shift,
            jnp.zeros_like(stem_bias),
        ]
    )
    small_other = lax.ppermute(small, "chan", swap)
    stem_other = lax.ppermute(stem_weight, "chan", swap)
    second_other = lax.ppermute(second_weight, "chan", swap)
    owners, power = gathered(padded, "tile")
    owners = owners.reshape(tile_count * PITCH, F * H_PAD * zc)

    window = W_DEV + 2 * HALO
    vmem = pl.BlockSpec(memory_space=pltpu.VMEM)
    far = pl.BlockSpec(memory_space=pltpu.HBM)
    selection, stem_full, vectors = pl.pallas_call(
        functools.partial(prepare_kernel, power),
        out_shape=(
            jax.ShapeDtypeStruct((3 * width, PITCH * tile_count), jnp.bfloat16),
            jax.ShapeDtypeStruct((3, 256, full), jnp.bfloat16),
            jax.ShapeDtypeStruct((small.shape[0], full), jnp.float32),
        ),
        in_specs=[pl.BlockSpec(memory_space=pltpu.SMEM)] + [vmem] * 4,
        out_specs=(vmem,) * 3,
        cost_estimate=pl.CostEstimate(flops=10**8, bytes_accessed=10**6, transcendentals=0),
        compiler_params=pltpu.CompilerParams(vmem_limit_bytes=8 * 1024 * 1024),
    )(tile_counts, stem_weight, stem_other, small, small_other)
    act, hidden = pl.pallas_call(
        first_kernel,
        out_shape=(
            jax.ShapeDtypeStruct((window, F * H, half), jnp.bfloat16),
            jax.ShapeDtypeStruct((window - 2, frames * H, full), jnp.bfloat16),
        ),
        in_specs=[vmem] * 5 + [far],
        out_specs=(vmem, vmem),
        scratch_shapes=[
            pltpu.VMEM((3, F, width, H_PAD * zc), jnp.float32),
            pltpu.VMEM((F, H, width, 256), jnp.bfloat16),
            pltpu.VMEM((full // 128, F * H * width, 128), jnp.float32),
            pltpu.VMEM((3, F, H + 2, width, full), jnp.bfloat16),
            pltpu.VMEM((pl.cdiv(half, 128), F * H * width, 128), jnp.float32),
            pltpu.VMEM((8, full), jnp.float32),
            pltpu.VMEM(first_weight.shape, jnp.bfloat16),
            pltpu.SemaphoreType.DMA,
        ],
        cost_estimate=pl.CostEstimate(
            flops=2 * F * H * width * 27 * full * half * 3 // 4,
            bytes_accessed=27 * full * half * 2,
            transcendentals=F * H * width * full,
        ),
        compiler_params=pltpu.CompilerParams(
            vmem_limit_bytes=min(60, 12 + 12 * width // 16) * 1024 * 1024
        ),
    )(
        owners,
        selection,
        stem_full,
        vectors,
        small,
        pltpu.with_memory_space_constraint(first_weight, pltpu.HBM),
    )

    act_other = lax.ppermute(act, "chan", swap)

    out = pl.pallas_call(
        functools.partial(second_kernel, tile_count),
        out_shape=jax.ShapeDtypeStruct((frames, 2 * H, 2 * W_DEV, out_channels), jnp.bfloat16),
        in_specs=[vmem] * 4 + [far] + [vmem] * 3,
        out_specs=vmem,
        scratch_shapes=[
            pltpu.VMEM((window, 2 * frames * 32 + 8, full), jnp.float32),
            pltpu.VMEM((9, window, frames * H, full), jnp.bfloat16),
            pltpu.VMEM((pl.cdiv(out_channels, 128), frames * 2 * H * 2 * W_DEV, 128), jnp.float32),
            pltpu.VMEM(second_weight.shape, jnp.bfloat16),
            pltpu.SemaphoreType.DMA,
        ],
        cost_estimate=pl.CostEstimate(
            flops=2 * 4 * 48 * 27 * full * full,
            bytes_accessed=2 * 27 * full * half * 2,
            transcendentals=0,
        ),
        compiler_params=pltpu.CompilerParams(vmem_limit_bytes=24 * 1024 * 1024),
    )(
        act,
        act_other,
        hidden,
        second_weight,
        pltpu.with_memory_space_constraint(second_other, pltpu.HBM),
        vectors,
        upsample_weight,
        upsample_bias.reshape(1, -1),
    )
    return out


def solution(mesh):
    placed = (
        P(("clip", "tile"), None, None),
        P("clip"),
        P(None, None, "chan"),
        P("chan"),
        P("chan"),
        P("chan"),
        P(None, None, "chan"),
        P("chan"),
        P("chan"),
        P("chan"),
        P(None, None, "chan"),
        P("chan"),
        P(),
        P(),
    )
    return jax.shard_map(
        on_device,
        mesh=mesh,
        in_specs=placed,
        out_specs=P(("clip", "chan"), None, "tile", None),
        check_vma=False,
    )
```

```python
import functools

import jax
import jax.numpy as jnp
from jax import lax
from jax.experimental import pallas as pl
from jax.experimental.pallas import tpu as pltpu
from jax.sharding import PartitionSpec as P

GROUPS = 32
F = 4
H = 24
W_DEV = 2
HALO = 2
PITCH = 8
H_PAD = 32
EPSILON = 1e-06


def joined(own, other, core):
    low = jnp.concatenate([own, other], axis=-1)
    high = jnp.concatenate([other, own], axis=-1)
    return jnp.where(core == 0, low, high)


def group_mean(column_sums, per_group, cells):
    channels = column_sums.shape[1]
    row = lax.broadcasted_iota(jnp.int32, (channels, channels), 0).astype(jnp.float32)
    column = lax.broadcasted_iota(jnp.int32, (channels, channels), 1).astype(jnp.float32)
    same = jnp.floor((row + 0.5) / per_group) == jnp.floor((column + 0.5) / per_group)
    total = jnp.dot(
        column_sums,
        same.astype(jnp.float32),
        precision=lax.Precision.HIGHEST,
        preferred_element_type=jnp.float32,
    )
    return total[0:1] * (1.0 / (cells * per_group))


def put(ref, place, value):
    for block in range(ref.shape[0]):
        part = value[:, block * 128 : (block + 1) * 128]
        ref[block, place, 0 : part.shape[1]] = part


def take(ref, place, channels):
    parts = []
    for block in range(ref.shape[0]):
        parts.append(ref[block, place, :][:, : channels - block * 128])
    return jnp.concatenate(parts, axis=1)


def squares(ref, mean):
    channels = mean.shape[1]
    step = 64

    def add(i, total):
        spread = take(ref, pl.ds(pl.multiple_of(i * step, step), step), channels) - mean
        return total + jnp.sum((spread * spread).reshape(step // 8, 8, channels), axis=0)

    total = lax.fori_loop(
        0, ref.shape[1] // step, add, jnp.zeros((8, channels), jnp.float32), unroll=2
    )
    return jnp.broadcast_to(jnp.sum(total, axis=0, keepdims=True), (8, channels))


def times(lhs, weight, taps):
    rhs = jnp.concatenate([weight[tap] for tap in taps], axis=1)
    return lax.dot_general(lhs, rhs, (((1,), (1,)), ((), ())), preferred_element_type=jnp.float32)


def silu(value):
    half = 0.5 * value
    return half + half * jnp.tanh(half)


def prepare_kernel(
    power, counts, stem_own, stem_other, small_own, small_other, selection, stem_full, vectors
):
    tile_count = counts.shape[0]
    width = tile_count * W_DEV
    me = lax.axis_index("tile")
    core = lax.axis_index("chan")
    zc = stem_own.shape[1]
    leftmost = me * W_DEV - HALO

    slots = PITCH * tile_count
    lane = lax.broadcasted_iota(jnp.int32, (3 * width, slots), 1)
    owner_at = lane // PITCH
    slot_at = lane - owner_at * PITCH
    held = jnp.full((3 * width, slots), -5, jnp.int32)
    start = jnp.int32(0)
    for owner in range(tile_count):
        place = (me ^ owner) if power else jnp.int32(owner)
        count = counts[owner]
        held = jnp.where((owner_at == place) & (slot_at < count), start + slot_at, held)
        start = start + count
    position = lax.broadcasted_iota(jnp.int32, (3 * width, slots), 0)
    shift = (position >= width).astype(jnp.int32) + (position >= 2 * width).astype(jnp.int32)
    column = position - shift * width + leftmost
    column = jnp.where(column < 0, column + width, column)
    column = jnp.where(column >= width, column - width, column)
    selection[...] = (held == column + shift - 1).astype(jnp.bfloat16)

    stem_full[...] = jnp.zeros(stem_full.shape, jnp.bfloat16)
    for tap in range(27):
        a, b, e = tap // 9, tap // 3 % 3, tap % 3
        at = e * 4 * zc + b * zc
        stem_full[a, at : at + zc, :] = joined(stem_own[tap], stem_other[tap], core)
    vectors[...] = joined(small_own[...], small_other[...], core)


def first_kernel(
    owners,
    selection,
    stem_full,
    vectors,
    small_own,
    weight_far,
    unread,
    act_out,
    hidden_out,
    shifted,
    patches,
    hidden,
    acts,
    produced,
    sums,
    weight,
    arrival,
):
    fetch = pltpu.make_async_copy(weight_far, weight, arrival)
    fetch.start()
    tile_count = owners.shape[0] // PITCH
    width = tile_count * W_DEV
    me = lax.axis_index("tile")
    core = lax.axis_index("chan")
    full, half = vectors.shape[1], small_own.shape[1]
    frame_lanes = owners.shape[1] // F
    zc = frame_lanes // H
    pieces = max(1, width // 16)
    rows = H // pieces
    cells = F * H * width
    leftmost = me * W_DEV - HALO
    for frame in range(F):
        lanes = slice(frame * frame_lanes, (frame + 1) * frame_lanes)
        chosen = jnp.dot(selection[...], owners[:, lanes], preferred_element_type=jnp.float32)
        blank = jnp.zeros((3 * width, shifted.shape[3] - frame_lanes), jnp.float32)
        chosen = pltpu.roll(jnp.concatenate([chosen, blank], axis=1), zc, axis=1)
        shifted[:, frame] = chosen.reshape(3, width, shifted.shape[3])

    stem_bias = vectors[0:1]
    first_gain = vectors[1:2]
    first_shift = vectors[2:3]

    per_block = 128 // zc
    lane128 = lax.broadcasted_iota(jnp.int32, (F, width, 128), 2)
    for row in range(H):
        block = row // per_block * 128
        offset = row % per_block * zc
        window = shifted[:, :, :, block : block + 256]
        one = pltpu.roll(window[0], (256 - offset) % 256, axis=2)[:, :, :128]
        two = pltpu.roll(window[1], (320 - offset) % 256, axis=2)[:, :, :128]
        three = pltpu.roll(window[2], (256 - offset) % 256, axis=2)[:, :, :128]
        patches[:, row, :, 0:128] = jnp.where(lane128 < 64, one, two).astype(jnp.bfloat16)
        patches[:, row, :, 128:256] = three.astype(jnp.bfloat16)

    def over_pieces(body):
        if pieces == 1:
            body(0)
        else:
            lax.fori_loop(0, pieces, lambda i, _: (body(i * rows), 0)[1], 0)

    def span(frame, row):
        return pl.ds(pl.multiple_of((frame * H + row) * width, 16), rows * width)

    sums[...] = jnp.zeros_like(sums)
    for frame in range(F):

        def stem(row):
            total = jnp.zeros((rows * width, full), jnp.float32)
            for a in range(max(0, 2 - frame), 3):
                lhs = patches[frame + a - 2, pl.ds(row, rows)].reshape(rows * width, 256)
                total += jnp.dot(lhs, stem_full[a], preferred_element_type=jnp.float32)
            value = (total + stem_bias).astype(jnp.bfloat16).astype(jnp.float32)
            put(hidden, span(frame, row), value)
            sums[0:1, :] += jnp.sum(value, axis=0, keepdims=True)

        over_pieces(stem)

    per_group = full // GROUPS
    mean = group_mean(jnp.broadcast_to(sums[0:1, :], (8, full)), per_group, cells)
    variance = group_mean(squares(hidden, mean), per_group, cells)
    scale = lax.rsqrt(variance + EPSILON) * first_gain

    spot = lax.broadcasted_iota(jnp.int32, (1, width, full), 1) + leftmost
    spot = jnp.where(spot < 0, spot + width, spot)
    spot = jnp.where(spot >= width, spot - width, spot)
    zero_row = jnp.zeros((width, full), jnp.bfloat16)
    for e in range(3):
        for frame in range(F):
            acts[e, frame, 0] = zero_row
            acts[e, frame, H + 1] = zero_row
    for frame in range(F):

        def activate(i, _):
            row = i * 2
            place = pl.ds(pl.multiple_of((frame * H + row) * width, 16), 2 * width)
            spread = take(hidden, place, full) - mean
            value = silu(spread * scale + first_shift).reshape(2, width, full)
            left = jnp.where(spot == 0, 0.0, pltpu.roll(value, 1, axis=1))
            right = jnp.where(spot == width - 1, 0.0, pltpu.roll(value, width - 1, axis=1))
            place = pl.ds(row + 1, 2)
            acts[0, frame, place] = left.astype(jnp.bfloat16)
            acts[1, frame, place] = value.astype(jnp.bfloat16)
            acts[2, frame, place] = right.astype(jnp.bfloat16)
            return _

        lax.fori_loop(0, H // 2, activate, 0, unroll=2)

    fetch.wait()
    first_bias = small_own[4:5]
    for frame in range(F):

        def convolve(row):
            used = range(max(0, 2 - frame) * 9, 27)
            lhs = jnp.concatenate(
                [
                    acts[tap % 3, frame + tap // 9 - 2, pl.ds(row + tap // 3 % 3, rows)].reshape(
                        rows * width, full
                    )
                    for tap in used
                ],
                axis=1,
            )
            total = times(lhs, weight, used)
            value = (total + first_bias).astype(jnp.bfloat16).astype(jnp.float32)
            put(produced, span(frame, row), value)
            sums[2:3, 0:half] += jnp.sum(value, axis=0, keepdims=True)

        over_pieces(convolve)

    mean = group_mean(jnp.broadcast_to(sums[2:3, 0:half], (8, half)), per_group, cells)
    variance = group_mean(squares(produced, mean), per_group, cells)
    scale = lax.rsqrt(variance + EPSILON) * small_own[5:6]
    second_shift = small_own[6:7]
    for spot_at in range(W_DEV + 2 * HALO):
        value = take(produced, pl.ds(spot_at, F * H, stride=width), half)
        value = silu((value - mean) * scale + second_shift)
        real = (leftmost + spot_at >= 0) & (leftmost + spot_at < width)
        act_out[spot_at] = jnp.where(real, value, 0.0).astype(jnp.bfloat16)
    frames = F // 2
    for spot_at in range(1, W_DEV + 3):
        begin = core * (frames * H * width) + spot_at
        value = take(hidden, pl.ds(begin, frames * H, stride=width), full)
        hidden_out[spot_at - 1] = value.astype(jnp.bfloat16)


def second_kernel(
    tile_count,
    act_own,
    act_other,
    hidden_in,
    weight_own,
    weight_other,
    vectors,
    up_weight,
    up_bias,
    out,
    slots,
    taps,
    flat,
):
    width = tile_count * W_DEV
    me = lax.axis_index("tile")
    core = lax.axis_index("chan")
    columns, cells, half = act_own.shape
    full = 2 * half
    frames = F // 2
    rows = frames * H
    inner = columns - 2
    slots[...] = jnp.zeros_like(slots)
    for column in range(columns):
        value = joined(
            act_own[column].astype(jnp.float32), act_other[column].astype(jnp.float32), core
        )
        before = jnp.where(core == 0, 0.0, value[0:rows])
        now = jnp.where(core == 0, value[0:rows], value[rows:])
        for slot in range(frames):
            at = slot * 32 + 8
            slots[column, at : at + H, :] = before[slot * H : (slot + 1) * H]
            at = (slot + frames) * 32 + 8
            slots[column, at : at + H, :] = now[slot * H : (slot + 1) * H]
    for a in range(3):
        for b in range(3):
            parts = []
            for frame in range(frames):
                at = (frame + a) * 32 + 7 + b
                parts.append(slots[:, at : at + H, :])
            taps[3 * a + b] = jnp.concatenate(parts, axis=1).astype(jnp.bfloat16)


    def convolve(weight):
        lhs = jnp.concatenate(
            [
                taps[tap // 3, tap % 3 : tap % 3 + inner].reshape(inner * rows, full)
                for tap in range(27)
            ],
            axis=1,
        )
        return times(lhs, weight, range(27))

    mine = convolve(weight_own)
    theirs = convolve(weight_other)
    second_out = joined(mine, theirs, core) + vectors[3:4]
    hidden = hidden_in[...].astype(jnp.float32) + second_out.reshape(inner, rows, full)
    spot = lax.broadcasted_iota(jnp.int32, (inner, rows, full), 0) + me * W_DEV - 1
    hidden = jnp.where((spot >= 0) & (spot < width), hidden, 0.0).astype(jnp.bfloat16)
    hidden = hidden.reshape(inner * rows, full)

    line = lax.broadcasted_iota(jnp.int32, (inner * frames, H, half), 1)
    upper, lower = [], []
    pad = jnp.zeros((256 - half % 256, full), jnp.bfloat16)
    rhs = jnp.concatenate(
        [part for tap in range(9) for part in (up_weight[tap], pad)], axis=0
    )
    spread = rhs.shape[0] // 9
    every = lax.dot_general(
        hidden, rhs, (((1,), (1,)), ((), ())), preferred_element_type=jnp.float32
    )
    for e in range(3):
        made = []
        for b in range(3):
            at = (3 * b + e) * spread
            made.append(every[:, at : at + half].reshape(inner * frames, H, half))
        above = jnp.where(line == 0, 0.0, pltpu.roll(made[0], 1, axis=1))
        below = jnp.where(line == H - 1, 0.0, pltpu.roll(made[2], H - 1, axis=1))
        upper.append((above + made[1] + made[2]).reshape(inner, frames, H, half))
        lower.append((made[0] + made[1] + below).reshape(inner, frames, H, half))
    bias = up_bias[...]
    span = 2 * W_DEV
    for parity, sums in ((0, upper), (1, lower)):
        for x in range(W_DEV):
            at = x + 1
            for side in range(2):
                if side == 0:
                    value = sums[0][at - 1] + sums[1][at] + sums[2][at]
                else:
                    value = sums[0][at] + sums[1][at] + sums[2][at + 1]
                for frame in range(frames):
                    begin = frame * 2 * H * span + parity * span + 2 * x + side
                    put(flat, pl.ds(begin, H, stride=2 * span), value[frame] + bias)
    out[...] = take(flat, slice(None), out.shape[-1]).astype(jnp.bfloat16).reshape(out.shape)


def exchanged(block, step):
    count = lax.axis_size("tile")
    moved = lax.ppermute(block, "tile", [(i, i ^ step) for i in range(count)])
    return jnp.concatenate([block, moved], axis=0)


def on_device(
    owner_latent,
    tile_counts,
    stem_weight,
    stem_bias,
    first_gain,
    first_shift,
    first_weight,
    first_bias,
    second_gain,
    second_shift,
    second_weight,
    second_bias,
    upsample_weight,
    upsample_bias,
):
    tile_count = lax.axis_size("tile")
    width = tile_count * W_DEV
    _, slot_count, row_length = owner_latent.shape
    zc, half = stem_weight.shape[1], stem_weight.shape[2]
    full = 2 * half
    out_channels = upsample_weight.shape[2]
    first_weight = first_weight.transpose(0, 2, 1)
    second_weight = second_weight.transpose(0, 2, 1)
    upsample_weight = upsample_weight.transpose(0, 2, 1)
    swap = [(0, 1), (1, 0)]
    frames = F // 2

    padded = jnp.pad(owner_latent, ((0, 0), (0, PITCH - slot_count), (0, 0)))
    small = jnp.stack(
        [
            stem_bias,
            first_gain,
            first_shift,
            second_bias,
            first_bias,
            second_gain,
            second_shift,
            jnp.zeros_like(stem_bias),
        ]
    )
    window = W_DEV + 2 * HALO
    vmem = pl.BlockSpec(memory_space=pltpu.VMEM)
    far = pl.BlockSpec(memory_space=pltpu.HBM)

    def prepare(small, small_other, stem_other, power):
        return pl.pallas_call(
            functools.partial(prepare_kernel, power),
            out_shape=(
                jax.ShapeDtypeStruct((3 * width, PITCH * tile_count), jnp.bfloat16),
                jax.ShapeDtypeStruct((3, 256, full), jnp.bfloat16),
                jax.ShapeDtypeStruct((small.shape[0], full), jnp.float32),
            ),
            in_specs=[pl.BlockSpec(memory_space=pltpu.SMEM)] + [vmem] * 4,
            out_specs=(vmem,) * 3,
            cost_estimate=pl.CostEstimate(flops=10**8, bytes_accessed=10**6, transcendentals=0),
            compiler_params=pltpu.CompilerParams(vmem_limit_bytes=8 * 1024 * 1024),
        )(tile_counts, stem_weight, stem_other, small, small_other)

    stem_other = lax.ppermute(stem_weight, "chan", swap)
    power = tile_count & (tile_count - 1) == 0 and tile_count >= 4
    if power:
        owners = exchanged(padded, 1)
        small_other = lax.ppermute(small, "chan", swap)
        owners, small_other, stem_other, second_far = lax.optimization_barrier(
            (owners, small_other, stem_other, second_weight)
        )
        second_other = lax.ppermute(second_far, "chan", swap)
        owners = exchanged(owners, 2)
        prepared = prepare(small, small_other, stem_other, power)
        owners, prepared = lax.optimization_barrier((owners, prepared))
        step = 4
        while step < tile_count:
            owners = exchanged(owners, step)
            step *= 2
    else:
        small_other = lax.ppermute(small, "chan", swap)
        second_other = lax.ppermute(second_weight, "chan", swap)
        owners = lax.all_gather(padded, "tile", axis=0, tiled=True)
        prepared = prepare(small, small_other, stem_other, power)
    selection, stem_full, vectors = prepared
    owners = owners.reshape(tile_count * PITCH, F * H * zc)
    act, hidden = pl.pallas_call(
        first_kernel,
        out_shape=(
            jax.ShapeDtypeStruct((window, F * H, half), jnp.bfloat16),
            jax.ShapeDtypeStruct((window - 2, frames * H, full), jnp.bfloat16),
        ),
        in_specs=[vmem] * 5 + [far, pl.BlockSpec(memory_space=pl.ANY)],
        out_specs=(vmem, vmem),
        scratch_shapes=[
            pltpu.VMEM((3, F, width, H_PAD * zc), jnp.float32),
            pltpu.VMEM((F, H, width, 256), jnp.bfloat16),
            pltpu.VMEM((full // 128, F * H * width, 128), jnp.float32),
            pltpu.VMEM((3, F, H + 2, width, full), jnp.bfloat16),
            pltpu.VMEM((pl.cdiv(half, 128), F * H * width, 128), jnp.float32),
            pltpu.VMEM((8, full), jnp.float32),
            pltpu.VMEM(first_weight.shape, jnp.bfloat16),
            pltpu.SemaphoreType.DMA,
        ],
        cost_estimate=pl.CostEstimate(
            flops=2 * F * H * width * 27 * full * half * 3 // 4,
            bytes_accessed=27 * full * half * 2,
            transcendentals=F * H * width * full,
        ),
        compiler_params=pltpu.CompilerParams(
            vmem_limit_bytes=min(60, 12 + 12 * width // 16) * 1024 * 1024
        ),
    )(
        owners,
        selection,
        stem_full,
        vectors,
        small,
        pltpu.with_memory_space_constraint(first_weight, pltpu.HBM),
        second_other,
    )

    act_other = lax.ppermute(act, "chan", swap)

    out = pl.pallas_call(
        functools.partial(second_kernel, tile_count),
        out_shape=jax.ShapeDtypeStruct((frames, 2 * H, 2 * W_DEV, out_channels), jnp.bfloat16),
        in_specs=[vmem] * 8,
        out_specs=vmem,
        scratch_shapes=[
            pltpu.VMEM((window, 2 * frames * 32 + 8, full), jnp.float32),
            pltpu.VMEM((9, window, frames * H, full), jnp.bfloat16),
            pltpu.VMEM((pl.cdiv(out_channels, 128), frames * 2 * H * 2 * W_DEV, 128), jnp.float32),
        ],
        cost_estimate=pl.CostEstimate(
            flops=2 * 4 * 48 * 27 * full * full,
            bytes_accessed=2 * 27 * full * half * 2,
            transcendentals=0,
        ),
        compiler_params=pltpu.CompilerParams(vmem_limit_bytes=24 * 1024 * 1024),
    )(
        act,
        act_other,
        hidden,
        second_weight,
        second_other,
        vectors,
        upsample_weight,
        upsample_bias.reshape(1, -1),
    )
    return out


def solution(mesh):
    placed = (
        P(("clip", "tile"), None, None),
        P("clip"),
        P(None, None, "chan"),
        P("chan"),
        P("chan"),
        P("chan"),
        P(None, None, "chan"),
        P("chan"),
        P("chan"),
        P("chan"),
        P(None, None, "chan"),
        P("chan"),
        P(),
        P(),
    )
    return jax.shard_map(
        on_device,
        mesh=mesh,
        in_specs=placed,
        out_specs=P(("clip", "chan"), None, "tile", None),
        check_vma=False,
    )
```

```python
import functools

import jax
import jax.numpy as jnp
from jax import lax
from jax.experimental import pallas as pl
from jax.experimental.pallas import tpu as pltpu
from jax.sharding import PartitionSpec as P

GROUPS = 32
F = 4
H = 24
W_DEV = 2
HALO = 2
PITCH = 8
H_PAD = 32
EPSILON = 1e-06


def joined(own, other, core):
    low = jnp.concatenate([own, other], axis=-1)
    high = jnp.concatenate([other, own], axis=-1)
    return jnp.where(core == 0, low, high)


def group_mean(column_sums, per_group, cells):
    channels = column_sums.shape[1]
    row = lax.broadcasted_iota(jnp.int32, (channels, channels), 0).astype(jnp.float32)
    column = lax.broadcasted_iota(jnp.int32, (channels, channels), 1).astype(jnp.float32)
    same = jnp.floor((row + 0.5) / per_group) == jnp.floor((column + 0.5) / per_group)
    total = jnp.dot(
        column_sums,
        same.astype(jnp.float32),
        precision=lax.Precision.HIGHEST,
        preferred_element_type=jnp.float32,
    )
    return total[0:1] * (1.0 / (cells * per_group))


def put(ref, place, value):
    for block in range(ref.shape[0]):
        part = value[:, block * 128 : (block + 1) * 128]
        ref[block, place, 0 : part.shape[1]] = part


def take(ref, place, channels):
    parts = []
    for block in range(ref.shape[0]):
        parts.append(ref[block, place, :][:, : channels - block * 128])
    return jnp.concatenate(parts, axis=1)


def squares(ref, mean):
    channels = mean.shape[1]
    step = 64

    def add(i, total):
        spread = take(ref, pl.ds(pl.multiple_of(i * step, step), step), channels) - mean
        return total + jnp.sum((spread * spread).reshape(step // 8, 8, channels), axis=0)

    total = lax.fori_loop(
        0, ref.shape[1] // step, add, jnp.zeros((8, channels), jnp.float32), unroll=2
    )
    return jnp.broadcast_to(jnp.sum(total, axis=0, keepdims=True), (8, channels))


def times(lhs, weight, taps):
    rhs = jnp.concatenate([weight[tap] for tap in taps], axis=1)
    return lax.dot_general(lhs, rhs, (((1,), (1,)), ((), ())), preferred_element_type=jnp.float32)


def silu(value):
    half = 0.5 * value
    return half + half * jnp.tanh(half)


def prepare_kernel(
    power, counts, stem_own, stem_other, small_own, small_other, selection, stem_full, vectors
):
    tile_count = counts.shape[0]
    width = tile_count * W_DEV
    me = lax.axis_index("tile")
    core = lax.axis_index("chan")
    zc = stem_own.shape[1]
    leftmost = me * W_DEV - HALO

    slots = PITCH * tile_count
    lane = lax.broadcasted_iota(jnp.int32, (3 * width, slots), 1)
    owner_at = lane // PITCH
    slot_at = lane - owner_at * PITCH
    held = jnp.full((3 * width, slots), -5, jnp.int32)
    start = jnp.int32(0)
    for owner in range(tile_count):
        place = jnp.int32(owner)
        if power:
            bits = tile_count.bit_length() - 1
            apart = me ^ owner
            place = sum(((apart >> bit) & 1) << (bits - 1 - bit) for bit in range(bits))
        count = counts[owner]
        held = jnp.where((owner_at == place) & (slot_at < count), start + slot_at, held)
        start = start + count
    position = lax.broadcasted_iota(jnp.int32, (3 * width, slots), 0)
    shift = (position >= width).astype(jnp.int32) + (position >= 2 * width).astype(jnp.int32)
    column = position - shift * width + leftmost
    column = jnp.where(column < 0, column + width, column)
    column = jnp.where(column >= width, column - width, column)
    selection[...] = (held == column + shift - 1).astype(jnp.bfloat16)

    stem_full[...] = jnp.zeros(stem_full.shape, jnp.bfloat16)
    for tap in range(27):
        a, b, e = tap // 9, tap // 3 % 3, tap % 3
        at = e * 4 * zc + b * zc
        stem_full[a, at : at + zc, :] = joined(stem_own[tap], stem_other[tap], core)
    vectors[...] = joined(small_own[...], small_other[...], core)


def first_kernel(
    owners,
    selection,
    stem_full,
    vectors,
    small_own,
    weight_far,
    unread,
    act_out,
    hidden_out,
    shifted,
    patches,
    hidden,
    acts,
    produced,
    sums,
    weight,
    arrival,
):
    fetch = pltpu.make_async_copy(weight_far, weight, arrival)
    fetch.start()
    tile_count = owners.shape[0] // PITCH
    width = tile_count * W_DEV
    me = lax.axis_index("tile")
    core = lax.axis_index("chan")
    full, half = vectors.shape[1], small_own.shape[1]
    frame_lanes = owners.shape[1] // F
    zc = frame_lanes // H
    pieces = max(1, width // 16)
    rows = H // pieces
    cells = F * H * width
    leftmost = me * W_DEV - HALO
    for frame in range(F):
        lanes = slice(frame * frame_lanes, (frame + 1) * frame_lanes)
        chosen = jnp.dot(selection[...], owners[:, lanes], preferred_element_type=jnp.float32)
        blank = jnp.zeros((3 * width, shifted.shape[3] - frame_lanes), jnp.float32)
        chosen = pltpu.roll(jnp.concatenate([chosen, blank], axis=1), zc, axis=1)
        shifted[:, frame] = chosen.reshape(3, width, shifted.shape[3])

    stem_bias = vectors[0:1]
    first_gain = vectors[1:2]
    first_shift = vectors[2:3]

    per_block = 128 // zc
    lane128 = lax.broadcasted_iota(jnp.int32, (F, width, 128), 2)
    for row in range(H):
        block = row // per_block * 128
        offset = row % per_block * zc
        window = shifted[:, :, :, block : block + 256]
        one = pltpu.roll(window[0], (256 - offset) % 256, axis=2)[:, :, :128]
        two = pltpu.roll(window[1], (320 - offset) % 256, axis=2)[:, :, :128]
        three = pltpu.roll(window[2], (256 - offset) % 256, axis=2)[:, :, :128]
        patches[:, row, :, 0:128] = jnp.where(lane128 < 64, one, two).astype(jnp.bfloat16)
        patches[:, row, :, 128:256] = three.astype(jnp.bfloat16)

    def over_pieces(body):
        if pieces == 1:
            body(0)
        else:
            lax.fori_loop(0, pieces, lambda i, _: (body(i * rows), 0)[1], 0)

    def span(frame, row):
        return pl.ds(pl.multiple_of((frame * H + row) * width, 16), rows * width)

    sums[...] = jnp.zeros_like(sums)
    for frame in range(F):

        def stem(row):
            total = jnp.zeros((rows * width, full), jnp.float32)
            for a in range(max(0, 2 - frame), 3):
                lhs = patches[frame + a - 2, pl.ds(row, rows)].reshape(rows * width, 256)
                total += jnp.dot(lhs, stem_full[a], preferred_element_type=jnp.float32)
            value = (total + stem_bias).astype(jnp.bfloat16).astype(jnp.float32)
            put(hidden, span(frame, row), value)
            sums[0:1, :] += jnp.sum(value, axis=0, keepdims=True)

        over_pieces(stem)

    per_group = full // GROUPS
    mean = group_mean(jnp.broadcast_to(sums[0:1, :], (8, full)), per_group, cells)
    variance = group_mean(squares(hidden, mean), per_group, cells)
    scale = lax.rsqrt(variance + EPSILON) * first_gain

    spot = lax.broadcasted_iota(jnp.int32, (1, width, full), 1) + leftmost
    spot = jnp.where(spot < 0, spot + width, spot)
    spot = jnp.where(spot >= width, spot - width, spot)
    zero_row = jnp.zeros((width, full), jnp.bfloat16)
    for e in range(3):
        for frame in range(F):
            acts[e, frame, 0] = zero_row
            acts[e, frame, H + 1] = zero_row
    for frame in range(F):

        def activate(i, _):
            row = i * 2
            place = pl.ds(pl.multiple_of((frame * H + row) * width, 16), 2 * width)
            spread = take(hidden, place, full) - mean
            value = silu(spread * scale + first_shift).reshape(2, width, full)
            left = jnp.where(spot == 0, 0.0, pltpu.roll(value, 1, axis=1))
            right = jnp.where(spot == width - 1, 0.0, pltpu.roll(value, width - 1, axis=1))
            place = pl.ds(row + 1, 2)
            acts[0, frame, place] = left.astype(jnp.bfloat16)
            acts[1, frame, place] = value.astype(jnp.bfloat16)
            acts[2, frame, place] = right.astype(jnp.bfloat16)
            return _

        lax.fori_loop(0, H // 2, activate, 0, unroll=2)

    fetch.wait()
    first_bias = small_own[4:5]
    for frame in range(F):

        def convolve(row):
            used = range(max(0, 2 - frame) * 9, 27)
            lhs = jnp.concatenate(
                [
                    acts[tap % 3, frame + tap // 9 - 2, pl.ds(row + tap // 3 % 3, rows)].reshape(
                        rows * width, full
                    )
                    for tap in used
                ],
                axis=1,
            )
            total = times(lhs, weight, used)
            value = (total + first_bias).astype(jnp.bfloat16).astype(jnp.float32)
            put(produced, span(frame, row), value)
            sums[2:3, 0:half] += jnp.sum(value, axis=0, keepdims=True)

        over_pieces(convolve)

    mean = group_mean(jnp.broadcast_to(sums[2:3, 0:half], (8, half)), per_group, cells)
    variance = group_mean(squares(produced, mean), per_group, cells)
    scale = lax.rsqrt(variance + EPSILON) * small_own[5:6]
    second_shift = small_own[6:7]
    for spot_at in range(W_DEV + 2 * HALO):
        value = take(produced, pl.ds(spot_at, F * H, stride=width), half)
        value = silu((value - mean) * scale + second_shift)
        real = (leftmost + spot_at >= 0) & (leftmost + spot_at < width)
        act_out[spot_at] = jnp.where(real, value, 0.0).astype(jnp.bfloat16)
    frames = F // 2
    for spot_at in range(1, W_DEV + 3):
        begin = core * (frames * H * width) + spot_at
        value = take(hidden, pl.ds(begin, frames * H, stride=width), full)
        hidden_out[spot_at - 1] = value.astype(jnp.bfloat16)


def second_kernel(
    tile_count,
    act_own,
    act_other,
    hidden_in,
    weight_own,
    weight_other,
    vectors,
    up_weight,
    up_bias,
    out,
    slots,
    taps,
    flat,
):
    width = tile_count * W_DEV
    me = lax.axis_index("tile")
    core = lax.axis_index("chan")
    columns, cells, half = act_own.shape
    full = 2 * half
    frames = F // 2
    rows = frames * H
    inner = columns - 2
    slots[...] = jnp.zeros_like(slots)
    for column in range(columns):
        value = joined(
            act_own[column].astype(jnp.float32), act_other[column].astype(jnp.float32), core
        )
        before = jnp.where(core == 0, 0.0, value[0:rows])
        now = jnp.where(core == 0, value[0:rows], value[rows:])
        for slot in range(frames):
            at = slot * 32 + 8
            slots[column, at : at + H, :] = before[slot * H : (slot + 1) * H]
            at = (slot + frames) * 32 + 8
            slots[column, at : at + H, :] = now[slot * H : (slot + 1) * H]
    for a in range(3):
        for b in range(3):
            parts = []
            for frame in range(frames):
                at = (frame + a) * 32 + 7 + b
                parts.append(slots[:, at : at + H, :])
            taps[3 * a + b] = jnp.concatenate(parts, axis=1).astype(jnp.bfloat16)


    def convolve(weight):
        lhs = jnp.concatenate(
            [
                taps[tap // 3, tap % 3 : tap % 3 + inner].reshape(inner * rows, full)
                for tap in range(27)
            ],
            axis=1,
        )
        return times(lhs, weight, range(27))

    mine = convolve(weight_own)
    theirs = convolve(weight_other)
    second_out = joined(mine, theirs, core) + vectors[3:4]
    hidden = hidden_in[...].astype(jnp.float32) + second_out.reshape(inner, rows, full)
    spot = lax.broadcasted_iota(jnp.int32, (inner, rows, full), 0) + me * W_DEV - 1
    hidden = jnp.where((spot >= 0) & (spot < width), hidden, 0.0).astype(jnp.bfloat16)
    hidden = hidden.reshape(inner * rows, full)

    line = lax.broadcasted_iota(jnp.int32, (inner * frames, H, half), 1)
    upper, lower = [], []
    pad = jnp.zeros((256 - half % 256, full), jnp.bfloat16)
    rhs = jnp.concatenate(
        [part for tap in range(9) for part in (up_weight[tap], pad)], axis=0
    )
    spread = rhs.shape[0] // 9
    every = lax.dot_general(
        hidden, rhs, (((1,), (1,)), ((), ())), preferred_element_type=jnp.float32
    )
    for e in range(3):
        made = []
        for b in range(3):
            at = (3 * b + e) * spread
            made.append(every[:, at : at + half].reshape(inner * frames, H, half))
        above = jnp.where(line == 0, 0.0, pltpu.roll(made[0], 1, axis=1))
        below = jnp.where(line == H - 1, 0.0, pltpu.roll(made[2], H - 1, axis=1))
        upper.append((above + made[1] + made[2]).reshape(inner, frames, H, half))
        lower.append((made[0] + made[1] + below).reshape(inner, frames, H, half))
    bias = up_bias[...]
    span = 2 * W_DEV
    for parity, sums in ((0, upper), (1, lower)):
        for x in range(W_DEV):
            at = x + 1
            for side in range(2):
                if side == 0:
                    value = sums[0][at - 1] + sums[1][at] + sums[2][at]
                else:
                    value = sums[0][at] + sums[1][at] + sums[2][at + 1]
                for frame in range(frames):
                    begin = frame * 2 * H * span + parity * span + 2 * x + side
                    put(flat, pl.ds(begin, H, stride=2 * span), value[frame] + bias)
    out[...] = take(flat, slice(None), out.shape[-1]).astype(jnp.bfloat16).reshape(out.shape)


def exchanged(block, step):
    count = lax.axis_size("tile")
    moved = lax.ppermute(block, "tile", [(i, i ^ step) for i in range(count)])
    return jnp.concatenate([block, moved], axis=0)


def on_device(
    owner_latent,
    tile_counts,
    stem_weight,
    stem_bias,
    first_gain,
    first_shift,
    first_weight,
    first_bias,
    second_gain,
    second_shift,
    second_weight,
    second_bias,
    upsample_weight,
    upsample_bias,
):
    tile_count = lax.axis_size("tile")
    width = tile_count * W_DEV
    _, slot_count, row_length = owner_latent.shape
    zc, half = stem_weight.shape[1], stem_weight.shape[2]
    full = 2 * half
    out_channels = upsample_weight.shape[2]
    first_weight = first_weight.transpose(0, 2, 1)
    second_weight = second_weight.transpose(0, 2, 1)
    upsample_weight = upsample_weight.transpose(0, 2, 1)
    swap = [(0, 1), (1, 0)]
    frames = F // 2

    padded = jnp.pad(owner_latent, ((0, 0), (0, PITCH - slot_count), (0, 0)))
    small = jnp.stack(
        [
            stem_bias,
            first_gain,
            first_shift,
            second_bias,
            first_bias,
            second_gain,
            second_shift,
            jnp.zeros_like(stem_bias),
        ]
    )
    window = W_DEV + 2 * HALO
    vmem = pl.BlockSpec(memory_space=pltpu.VMEM)
    far = pl.BlockSpec(memory_space=pltpu.HBM)

    def prepare(small, small_other, stem_other, power):
        return pl.pallas_call(
            functools.partial(prepare_kernel, power),
            out_shape=(
                jax.ShapeDtypeStruct((3 * width, PITCH * tile_count), jnp.bfloat16),
                jax.ShapeDtypeStruct((3, 256, full), jnp.bfloat16),
                jax.ShapeDtypeStruct((small.shape[0], full), jnp.float32),
            ),
            in_specs=[pl.BlockSpec(memory_space=pltpu.SMEM)] + [vmem] * 4,
            out_specs=(vmem,) * 3,
            cost_estimate=pl.CostEstimate(flops=10**8, bytes_accessed=10**6, transcendentals=0),
            compiler_params=pltpu.CompilerParams(vmem_limit_bytes=8 * 1024 * 1024),
        )(tile_counts, stem_weight, stem_other, small, small_other)

    stem_other = lax.ppermute(stem_weight, "chan", swap)
    power = tile_count & (tile_count - 1) == 0 and tile_count >= 4
    if power:
        step = tile_count // 2
        owners = exchanged(padded, step)
        small_other = lax.ppermute(small, "chan", swap)
        owners, small_other, stem_other, second_far = lax.optimization_barrier(
            (owners, small_other, stem_other, second_weight)
        )
        second_other = lax.ppermute(second_far, "chan", swap)
        step //= 2
        owners = exchanged(owners, step)
        prepared = prepare(small, small_other, stem_other, power)
        owners, prepared = lax.optimization_barrier((owners, prepared))
        while step > 1:
            step //= 2
            owners = exchanged(owners, step)
    else:
        small_other = lax.ppermute(small, "chan", swap)
        second_other = lax.ppermute(second_weight, "chan", swap)
        owners = lax.all_gather(padded, "tile", axis=0, tiled=True)
        prepared = prepare(small, small_other, stem_other, power)
    selection, stem_full, vectors = prepared
    owners = owners.reshape(tile_count * PITCH, F * H * zc)
    act, hidden = pl.pallas_call(
        first_kernel,
        out_shape=(
            jax.ShapeDtypeStruct((window, F * H, half), jnp.bfloat16),
            jax.ShapeDtypeStruct((window - 2, frames * H, full), jnp.bfloat16),
        ),
        in_specs=[vmem] * 5 + [far, pl.BlockSpec(memory_space=pl.ANY)],
        out_specs=(vmem, vmem),
        scratch_shapes=[
            pltpu.VMEM((3, F, width, H_PAD * zc), jnp.float32),
            pltpu.VMEM((F, H, width, 256), jnp.bfloat16),
            pltpu.VMEM((full // 128, F * H * width, 128), jnp.float32),
            pltpu.VMEM((3, F, H + 2, width, full), jnp.bfloat16),
            pltpu.VMEM((pl.cdiv(half, 128), F * H * width, 128), jnp.float32),
            pltpu.VMEM((8, full), jnp.float32),
            pltpu.VMEM(first_weight.shape, jnp.bfloat16),
            pltpu.SemaphoreType.DMA,
        ],
        cost_estimate=pl.CostEstimate(
            flops=2 * F * H * width * 27 * full * half * 3 // 4,
            bytes_accessed=27 * full * half * 2,
            transcendentals=F * H * width * full,
        ),
        compiler_params=pltpu.CompilerParams(
            vmem_limit_bytes=min(60, 12 + 12 * width // 16) * 1024 * 1024
        ),
    )(
        owners,
        selection,
        stem_full,
        vectors,
        small,
        pltpu.with_memory_space_constraint(first_weight, pltpu.HBM),
        second_other,
    )

    act_other = lax.ppermute(act, "chan", swap)

    out = pl.pallas_call(
        functools.partial(second_kernel, tile_count),
        out_shape=jax.ShapeDtypeStruct((frames, 2 * H, 2 * W_DEV, out_channels), jnp.bfloat16),
        in_specs=[vmem] * 8,
        out_specs=vmem,
        scratch_shapes=[
            pltpu.VMEM((window, 2 * frames * 32 + 8, full), jnp.float32),
            pltpu.VMEM((9, window, frames * H, full), jnp.bfloat16),
            pltpu.VMEM((pl.cdiv(out_channels, 128), frames * 2 * H * 2 * W_DEV, 128), jnp.float32),
        ],
        cost_estimate=pl.CostEstimate(
            flops=2 * 4 * 48 * 27 * full * full,
            bytes_accessed=2 * 27 * full * half * 2,
            transcendentals=0,
        ),
        compiler_params=pltpu.CompilerParams(vmem_limit_bytes=24 * 1024 * 1024),
    )(
        act,
        act_other,
        hidden,
        second_weight,
        second_other,
        vectors,
        upsample_weight,
        upsample_bias.reshape(1, -1),
    )
    return out


def solution(mesh):
    placed = (
        P(("clip", "tile"), None, None),
        P("clip"),
        P(None, None, "chan"),
        P("chan"),
        P("chan"),
        P("chan"),
        P(None, None, "chan"),
        P("chan"),
        P("chan"),
        P("chan"),
        P(None, None, "chan"),
        P("chan"),
        P(),
        P(),
    )
    return jax.shard_map(
        on_device,
        mesh=mesh,
        in_specs=placed,
        out_specs=P(("clip", "chan"), None, "tile", None),
        check_vma=False,
    )
```

```python
import functools

import jax
import jax.numpy as jnp
from jax import lax
from jax.experimental import pallas as pl
from jax.experimental.pallas import tpu as pltpu
from jax.sharding import PartitionSpec as P

GROUPS = 32
F = 4
H = 24
W_DEV = 2
HALO = 2
PACKED = 64
H_PAD = 32
EPSILON = 1e-06


def joined(own, other, core):
    low = jnp.concatenate([own, other], axis=-1)
    high = jnp.concatenate([other, own], axis=-1)
    return jnp.where(core == 0, low, high)


def group_mean(column_sums, per_group, cells):
    channels = column_sums.shape[1]
    row = lax.broadcasted_iota(jnp.int32, (channels, channels), 0).astype(jnp.float32)
    column = lax.broadcasted_iota(jnp.int32, (channels, channels), 1).astype(jnp.float32)
    same = jnp.floor((row + 0.5) / per_group) == jnp.floor((column + 0.5) / per_group)
    total = jnp.dot(
        column_sums,
        same.astype(jnp.float32),
        precision=lax.Precision.HIGHEST,
        preferred_element_type=jnp.float32,
    )
    return total[0:1] * (1.0 / (cells * per_group))


def put(ref, place, value):
    for block in range(ref.shape[0]):
        part = value[:, block * 128 : (block + 1) * 128]
        ref[block, place, 0 : part.shape[1]] = part


def take(ref, place, channels):
    parts = []
    for block in range(ref.shape[0]):
        parts.append(ref[block, place, :][:, : channels - block * 128])
    return jnp.concatenate(parts, axis=1)


def squares(ref, mean):
    channels = mean.shape[1]
    step = 64

    def add(i, total):
        spread = take(ref, pl.ds(pl.multiple_of(i * step, step), step), channels) - mean
        return total + jnp.sum((spread * spread).reshape(step // 8, 8, channels), axis=0)

    total = lax.fori_loop(
        0, ref.shape[1] // step, add, jnp.zeros((8, channels), jnp.float32), unroll=2
    )
    return jnp.broadcast_to(jnp.sum(total, axis=0, keepdims=True), (8, channels))


def times(lhs, weight, taps):
    rhs = jnp.concatenate([weight[tap] for tap in taps], axis=1)
    return lax.dot_general(lhs, rhs, (((1,), (1,)), ((), ())), preferred_element_type=jnp.float32)


def silu(value):
    half = 0.5 * value
    return half + half * jnp.tanh(half)


def prepare_kernel(
    power, counts, stem_own, stem_other, small_own, small_other, selection, stem_full, vectors
):
    tile_count = counts.shape[0]
    width = tile_count * W_DEV
    me = lax.axis_index("tile")
    core = lax.axis_index("chan")
    zc = stem_own.shape[1]
    leftmost = me * W_DEV - HALO

    blocks = selection.shape[0] // (3 * width)
    packed_rows = tile_count * PACKED
    lane = lax.broadcasted_iota(jnp.int32, (8, packed_rows), 1)
    place_at = lane // PACKED
    row_at = lane - place_at * PACKED
    slot_at = jnp.floor((row_at.astype(jnp.float32) + 0.5) * (1.0 / blocks)).astype(jnp.int32)
    held = jnp.full((8, packed_rows), -5, jnp.int32)
    start = jnp.int32(0)
    bits = tile_count.bit_length() - 1
    for owner in range(tile_count):
        place = jnp.int32(owner)
        if power:
            apart = me ^ owner
            far = apart >> (bits - 2)
            place = jnp.where(far == 2, 1 + 2 * core, jnp.where(far == 1, 3 - 2 * core, far))
            place = jnp.where(far == 3, 2, place)
            for bit in range(bits - 2):
                place += ((apart >> bit) & 1) << (bits - 1 - bit)
        count = counts[owner]
        held = jnp.where((place_at == place) & (slot_at < count), start + slot_at, held)
        start = start + count
    code = (held * 16 + row_at - slot_at * blocks)[0:1]
    position = lax.broadcasted_iota(jnp.int32, (3 * width, packed_rows), 0)
    shift = (position >= width).astype(jnp.int32) + (position >= 2 * width).astype(jnp.int32)
    column = position - shift * width + leftmost
    column = jnp.where(column < 0, column + width, column)
    column = jnp.where(column >= width, column - width, column)
    wanted = (column + shift - 1) * 16
    for block in range(blocks):
        rows = slice(block * 3 * width, (block + 1) * 3 * width)
        selection[rows, :] = (wanted + block == code).astype(jnp.bfloat16)

    stem_full[...] = jnp.zeros(stem_full.shape, jnp.bfloat16)
    for tap in range(27):
        a, b, e = tap // 9, tap // 3 % 3, tap % 3
        at = e * 4 * zc + b * zc
        stem_full[a, at : at + zc, :] = joined(stem_own[tap], stem_other[tap], core)
    vectors[...] = joined(small_own[...], small_other[...], core)


def first_kernel(
    owners,
    selection,
    stem_full,
    vectors,
    small_own,
    weight_far,
    unread,
    act_out,
    hidden_out,
    packed,
    shifted,
    patches,
    hidden,
    acts,
    produced,
    sums,
    weight,
    arrival,
):
    fetch = pltpu.make_async_copy(weight_far, weight, arrival)
    fetch.start()
    tile_count = owners.shape[0]
    width = tile_count * W_DEV
    me = lax.axis_index("tile")
    core = lax.axis_index("chan")
    full, half = vectors.shape[1], small_own.shape[1]
    blocks = selection.shape[0] // (3 * width)
    frame_blocks = blocks // F
    frame_lanes = frame_blocks * 128
    zc = frame_lanes // H
    pieces = max(1, width // 16)
    rows = H // pieces
    cells = F * H * width
    leftmost = me * W_DEV - HALO
    packed[...] = jnp.zeros(packed.shape, jnp.bfloat16)
    packed[:, 0 : owners.shape[1], :] = owners[...]
    every = jnp.dot(
        selection[...],
        packed[...].reshape(tile_count * PACKED, 128),
        preferred_element_type=jnp.float32,
    )
    blank = jnp.zeros((3 * width, shifted.shape[3] - frame_lanes), jnp.float32)
    for frame in range(F):
        parts = []
        for block in range(frame * frame_blocks, (frame + 1) * frame_blocks):
            parts.append(every[block * 3 * width : (block + 1) * 3 * width])
        chosen = pltpu.roll(jnp.concatenate(parts + [blank], axis=1), zc, axis=1)
        shifted[:, frame] = chosen.reshape(3, width, shifted.shape[3])

    stem_bias = vectors[0:1]
    first_gain = vectors[1:2]
    first_shift = vectors[2:3]

    per_block = 128 // zc
    lane128 = lax.broadcasted_iota(jnp.int32, (F, width, 128), 2)
    for row in range(H):
        block = row // per_block * 128
        offset = row % per_block * zc
        window = shifted[:, :, :, block : block + 256]
        one = pltpu.roll(window[0], (256 - offset) % 256, axis=2)[:, :, :128]
        two = pltpu.roll(window[1], (320 - offset) % 256, axis=2)[:, :, :128]
        three = pltpu.roll(window[2], (256 - offset) % 256, axis=2)[:, :, :128]
        patches[:, row, :, 0:128] = jnp.where(lane128 < 64, one, two).astype(jnp.bfloat16)
        patches[:, row, :, 128:256] = three.astype(jnp.bfloat16)

    def over_pieces(body):
        if pieces == 1:
            body(0)
        else:
            lax.fori_loop(0, pieces, lambda i, _: (body(i * rows), 0)[1], 0)

    def span(frame, row):
        return pl.ds(pl.multiple_of((frame * H + row) * width, 16), rows * width)

    sums[...] = jnp.zeros_like(sums)
    for frame in range(F):

        def stem(row):
            total = jnp.zeros((rows * width, full), jnp.float32)
            for a in range(max(0, 2 - frame), 3):
                lhs = patches[frame + a - 2, pl.ds(row, rows)].reshape(rows * width, 256)
                total += jnp.dot(lhs, stem_full[a], preferred_element_type=jnp.float32)
            value = (total + stem_bias).astype(jnp.bfloat16).astype(jnp.float32)
            put(hidden, span(frame, row), value)
            sums[0:1, :] += jnp.sum(value, axis=0, keepdims=True)

        over_pieces(stem)

    per_group = full // GROUPS
    mean = group_mean(jnp.broadcast_to(sums[0:1, :], (8, full)), per_group, cells)
    variance = group_mean(squares(hidden, mean), per_group, cells)
    scale = lax.rsqrt(variance + EPSILON) * first_gain

    spot = lax.broadcasted_iota(jnp.int32, (1, width, full), 1) + leftmost
    spot = jnp.where(spot < 0, spot + width, spot)
    spot = jnp.where(spot >= width, spot - width, spot)
    zero_row = jnp.zeros((width, full), jnp.bfloat16)
    for e in range(3):
        for frame in range(F):
            acts[e, frame, 0] = zero_row
            acts[e, frame, H + 1] = zero_row
    for frame in range(F):

        def activate(i, _):
            row = i * 2
            place = pl.ds(pl.multiple_of((frame * H + row) * width, 16), 2 * width)
            spread = take(hidden, place, full) - mean
            value = silu(spread * scale + first_shift).reshape(2, width, full)
            left = jnp.where(spot == 0, 0.0, pltpu.roll(value, 1, axis=1))
            right = jnp.where(spot == width - 1, 0.0, pltpu.roll(value, width - 1, axis=1))
            place = pl.ds(row + 1, 2)
            acts[0, frame, place] = left.astype(jnp.bfloat16)
            acts[1, frame, place] = value.astype(jnp.bfloat16)
            acts[2, frame, place] = right.astype(jnp.bfloat16)
            return _

        lax.fori_loop(0, H // 2, activate, 0, unroll=2)

    fetch.wait()
    first_bias = small_own[4:5]
    for frame in range(F):

        def convolve(row):
            used = range(max(0, 2 - frame) * 9, 27)
            lhs = jnp.concatenate(
                [
                    acts[tap % 3, frame + tap // 9 - 2, pl.ds(row + tap // 3 % 3, rows)].reshape(
                        rows * width, full
                    )
                    for tap in used
                ],
                axis=1,
            )
            total = times(lhs, weight, used)
            value = (total + first_bias).astype(jnp.bfloat16).astype(jnp.float32)
            put(produced, span(frame, row), value)
            sums[2:3, 0:half] += jnp.sum(value, axis=0, keepdims=True)

        over_pieces(convolve)

    mean = group_mean(jnp.broadcast_to(sums[2:3, 0:half], (8, half)), per_group, cells)
    variance = group_mean(squares(produced, mean), per_group, cells)
    scale = lax.rsqrt(variance + EPSILON) * small_own[5:6]
    second_shift = small_own[6:7]
    for spot_at in range(W_DEV + 2 * HALO):
        value = take(produced, pl.ds(spot_at, F * H, stride=width), half)
        value = silu((value - mean) * scale + second_shift)
        real = (leftmost + spot_at >= 0) & (leftmost + spot_at < width)
        act_out[spot_at] = jnp.where(real, value, 0.0).astype(jnp.bfloat16)
    frames = F // 2
    for spot_at in range(1, W_DEV + 3):
        begin = core * (frames * H * width) + spot_at
        value = take(hidden, pl.ds(begin, frames * H, stride=width), full)
        hidden_out[spot_at - 1] = value.astype(jnp.bfloat16)


def second_kernel(
    tile_count,
    act_own,
    act_other,
    hidden_in,
    weight_own,
    weight_other,
    vectors,
    up_weight,
    up_bias,
    out,
    slots,
    taps,
    flat,
):
    width = tile_count * W_DEV
    me = lax.axis_index("tile")
    core = lax.axis_index("chan")
    columns, cells, half = act_own.shape
    full = 2 * half
    frames = F // 2
    rows = frames * H
    inner = columns - 2
    slots[...] = jnp.zeros_like(slots)
    for column in range(columns):
        value = joined(
            act_own[column].astype(jnp.float32), act_other[column].astype(jnp.float32), core
        )
        before = jnp.where(core == 0, 0.0, value[0:rows])
        now = jnp.where(core == 0, value[0:rows], value[rows:])
        for slot in range(frames):
            at = slot * 32 + 8
            slots[column, at : at + H, :] = before[slot * H : (slot + 1) * H]
            at = (slot + frames) * 32 + 8
            slots[column, at : at + H, :] = now[slot * H : (slot + 1) * H]
    for a in range(3):
        for b in range(3):
            parts = []
            for frame in range(frames):
                at = (frame + a) * 32 + 7 + b
                parts.append(slots[:, at : at + H, :])
            taps[3 * a + b] = jnp.concatenate(parts, axis=1).astype(jnp.bfloat16)


    def convolve(weight):
        lhs = jnp.concatenate(
            [
                taps[tap // 3, tap % 3 : tap % 3 + inner].reshape(inner * rows, full)
                for tap in range(27)
            ],
            axis=1,
        )
        return times(lhs, weight, range(27))

    mine = convolve(weight_own)
    theirs = convolve(weight_other)
    second_out = joined(mine, theirs, core) + vectors[3:4]
    hidden = hidden_in[...].astype(jnp.float32) + second_out.reshape(inner, rows, full)
    spot = lax.broadcasted_iota(jnp.int32, (inner, rows, full), 0) + me * W_DEV - 1
    hidden = jnp.where((spot >= 0) & (spot < width), hidden, 0.0).astype(jnp.bfloat16)
    hidden = hidden.reshape(inner * rows, full)

    line = lax.broadcasted_iota(jnp.int32, (inner * frames, H, half), 1)
    upper, lower = [], []
    pad = jnp.zeros((256 - half % 256, full), jnp.bfloat16)
    rhs = jnp.concatenate(
        [part for tap in range(9) for part in (up_weight[tap], pad)], axis=0
    )
    spread = rhs.shape[0] // 9
    every = lax.dot_general(
        hidden, rhs, (((1,), (1,)), ((), ())), preferred_element_type=jnp.float32
    )
    for e in range(3):
        made = []
        for b in range(3):
            at = (3 * b + e) * spread
            made.append(every[:, at : at + half].reshape(inner * frames, H, half))
        above = jnp.where(line == 0, 0.0, pltpu.roll(made[0], 1, axis=1))
        below = jnp.where(line == H - 1, 0.0, pltpu.roll(made[2], H - 1, axis=1))
        upper.append((above + made[1] + made[2]).reshape(inner, frames, H, half))
        lower.append((made[0] + made[1] + below).reshape(inner, frames, H, half))
    bias = up_bias[...]
    span = 2 * W_DEV
    for parity, sums in ((0, upper), (1, lower)):
        for x in range(W_DEV):
            at = x + 1
            for side in range(2):
                if side == 0:
                    value = sums[0][at - 1] + sums[1][at] + sums[2][at]
                else:
                    value = sums[0][at] + sums[1][at] + sums[2][at + 1]
                for frame in range(frames):
                    begin = frame * 2 * H * span + parity * span + 2 * x + side
                    put(flat, pl.ds(begin, H, stride=2 * span), value[frame] + bias)
    out[...] = take(flat, slice(None), out.shape[-1]).astype(jnp.bfloat16).reshape(out.shape)


def exchanged(block, step):
    count = lax.axis_size("tile")
    moved = lax.ppermute(block, "tile", [(i, i ^ step) for i in range(count)])
    return jnp.concatenate([block, moved], axis=0)


def on_device(
    owner_latent,
    tile_counts,
    stem_weight,
    stem_bias,
    first_gain,
    first_shift,
    first_weight,
    first_bias,
    second_gain,
    second_shift,
    second_weight,
    second_bias,
    upsample_weight,
    upsample_bias,
):
    tile_count = lax.axis_size("tile")
    width = tile_count * W_DEV
    _, slot_count, row_length = owner_latent.shape
    zc, half = stem_weight.shape[1], stem_weight.shape[2]
    full = 2 * half
    out_channels = upsample_weight.shape[2]
    first_weight = first_weight.transpose(0, 2, 1)
    second_weight = second_weight.transpose(0, 2, 1)
    upsample_weight = upsample_weight.transpose(0, 2, 1)
    swap = [(0, 1), (1, 0)]
    frames = F // 2

    block_rows = slot_count * row_length // 128
    latents = owner_latent.reshape(1, block_rows, 128)
    small = jnp.stack(
        [
            stem_bias,
            first_gain,
            first_shift,
            second_bias,
            first_bias,
            second_gain,
            second_shift,
            jnp.zeros_like(stem_bias),
        ]
    )
    window = W_DEV + 2 * HALO
    vmem = pl.BlockSpec(memory_space=pltpu.VMEM)
    far = pl.BlockSpec(memory_space=pltpu.HBM)

    def prepare(small, small_other, stem_other, power):
        return pl.pallas_call(
            functools.partial(prepare_kernel, power),
            out_shape=(
                jax.ShapeDtypeStruct((row_length // 128 * 3 * width, PACKED * tile_count), jnp.bfloat16),
                jax.ShapeDtypeStruct((3, 256, full), jnp.bfloat16),
                jax.ShapeDtypeStruct((small.shape[0], full), jnp.float32),
            ),
            in_specs=[pl.BlockSpec(memory_space=pltpu.SMEM)] + [vmem] * 4,
            out_specs=(vmem,) * 3,
            cost_estimate=pl.CostEstimate(flops=10**8, bytes_accessed=10**6, transcendentals=0),
            compiler_params=pltpu.CompilerParams(
                vmem_limit_bytes=(6 + 2 * width // 16) * 1024 * 1024
            ),
        )(tile_counts, stem_weight, stem_other, small, small_other)

    stem_other = lax.ppermute(stem_weight, "chan", swap)
    power = tile_count & (tile_count - 1) == 0 and tile_count >= 4
    if power:
        away, near = tile_count // 2, tile_count // 4
        pairs = [
            (2 * i + c, 2 * (i ^ (near if c else away)) + c)
            for i in range(tile_count)
            for c in range(2)
        ]
        one = lax.ppermute(latents, ("tile", "chan"), pairs)
        both = [(i, i ^ away ^ near) for i in range(tile_count)]
        two = lax.ppermute(latents, "tile", both)
        small_other = lax.ppermute(small, "chan", swap)
        three = lax.ppermute(one, "chan", swap)
        owners = jnp.concatenate([latents, one, two, three], axis=0)
        owners, small_other, stem_other, second_far = lax.optimization_barrier(
            (owners, small_other, stem_other, second_weight)
        )
        second_other = lax.ppermute(second_far, "chan", swap)
        step = near
        while step > 1:
            step //= 2
            owners = exchanged(owners, step)
        prepared = prepare(small, small_other, stem_other, power)
    else:
        small_other = lax.ppermute(small, "chan", swap)
        second_other = lax.ppermute(second_weight, "chan", swap)
        owners = lax.all_gather(latents, "tile", axis=0, tiled=True)
        prepared = prepare(small, small_other, stem_other, power)
    selection, stem_full, vectors = prepared
    act, hidden = pl.pallas_call(
        first_kernel,
        out_shape=(
            jax.ShapeDtypeStruct((window, F * H, half), jnp.bfloat16),
            jax.ShapeDtypeStruct((window - 2, frames * H, full), jnp.bfloat16),
        ),
        in_specs=[vmem] * 5 + [far, pl.BlockSpec(memory_space=pl.ANY)],
        out_specs=(vmem, vmem),
        scratch_shapes=[
            pltpu.VMEM((tile_count, PACKED, 128), jnp.bfloat16),
            pltpu.VMEM((3, F, width, H_PAD * zc), jnp.float32),
            pltpu.VMEM((F, H, width, 256), jnp.bfloat16),
            pltpu.VMEM((full // 128, F * H * width, 128), jnp.float32),
            pltpu.VMEM((3, F, H + 2, width, full), jnp.bfloat16),
            pltpu.VMEM((pl.cdiv(half, 128), F * H * width, 128), jnp.float32),
            pltpu.VMEM((8, full), jnp.float32),
            pltpu.VMEM(first_weight.shape, jnp.bfloat16),
            pltpu.SemaphoreType.DMA,
        ],
        cost_estimate=pl.CostEstimate(
            flops=2 * F * H * width * 27 * full * half * 3 // 4,
            bytes_accessed=27 * full * half * 2,
            transcendentals=F * H * width * full,
        ),
        compiler_params=pltpu.CompilerParams(
            vmem_limit_bytes=min(60, 12 + 12 * width // 16) * 1024 * 1024
        ),
    )(
        owners,
        selection,
        stem_full,
        vectors,
        small,
        pltpu.with_memory_space_constraint(first_weight, pltpu.HBM),
        second_other,
    )

    act_other = lax.ppermute(act, "chan", swap)

    out = pl.pallas_call(
        functools.partial(second_kernel, tile_count),
        out_shape=jax.ShapeDtypeStruct((frames, 2 * H, 2 * W_DEV, out_channels), jnp.bfloat16),
        in_specs=[vmem] * 8,
        out_specs=vmem,
        scratch_shapes=[
            pltpu.VMEM((window, 2 * frames * 32 + 8, full), jnp.float32),
            pltpu.VMEM((9, window, frames * H, full), jnp.bfloat16),
            pltpu.VMEM((pl.cdiv(out_channels, 128), frames * 2 * H * 2 * W_DEV, 128), jnp.float32),
        ],
        cost_estimate=pl.CostEstimate(
            flops=2 * 4 * 48 * 27 * full * full,
            bytes_accessed=2 * 27 * full * half * 2,
            transcendentals=0,
        ),
        compiler_params=pltpu.CompilerParams(vmem_limit_bytes=24 * 1024 * 1024),
    )(
        act,
        act_other,
        hidden,
        second_weight,
        second_other,
        vectors,
        upsample_weight,
        upsample_bias.reshape(1, -1),
    )
    return out


def solution(mesh):
    placed = (
        P(("clip", "tile"), None, None),
        P("clip"),
        P(None, None, "chan"),
        P("chan"),
        P("chan"),
        P("chan"),
        P(None, None, "chan"),
        P("chan"),
        P("chan"),
        P("chan"),
        P(None, None, "chan"),
        P("chan"),
        P(),
        P(),
    )
    return jax.shard_map(
        on_device,
        mesh=mesh,
        in_specs=placed,
        out_specs=P(("clip", "chan"), None, "tile", None),
        check_vma=False,
    )
```

```python
import functools

import jax
import jax.numpy as jnp
from jax import lax
from jax.experimental import pallas as pl
from jax.experimental.pallas import tpu as pltpu
from jax.sharding import PartitionSpec as P


GROUPS = 32
F = 4
H = 24
W_DEV = 2
HALO = 2
PACKED = 64
H_PAD = 32
EPSILON = 1e-06


def joined(own, other, core):
    low = jnp.concatenate([own, other], axis=-1)
    high = jnp.concatenate([other, own], axis=-1)
    return jnp.where(core == 0, low, high)


def group_mean(column_sums, per_group, cells):
    channels = column_sums.shape[1]
    row = lax.broadcasted_iota(jnp.int32, (channels, channels), 0).astype(jnp.float32)
    column = lax.broadcasted_iota(jnp.int32, (channels, channels), 1).astype(jnp.float32)
    same = jnp.floor((row + 0.5) / per_group) == jnp.floor((column + 0.5) / per_group)
    total = jnp.dot(
        column_sums,
        same.astype(jnp.float32),
        precision=lax.Precision.HIGHEST,
        preferred_element_type=jnp.float32,
    )
    return total[0:1] * (1.0 / (cells * per_group))


def put(ref, place, value):
    for block in range(ref.shape[0]):
        part = value[:, block * 128 : (block + 1) * 128]
        ref[block, place, 0 : part.shape[1]] = part


def take(ref, place, channels):
    parts = []
    for block in range(ref.shape[0]):
        parts.append(ref[block, place, :][:, : channels - block * 128])
    return jnp.concatenate(parts, axis=1)


def squares(ref, mean):
    channels = mean.shape[1]
    step = 64

    def add(i, total):
        spread = take(ref, pl.ds(pl.multiple_of(i * step, step), step), channels) - mean
        return total + jnp.sum((spread * spread).reshape(step // 8, 8, channels), axis=0)

    total = lax.fori_loop(
        0, ref.shape[1] // step, add, jnp.zeros((8, channels), jnp.float32), unroll=2
    )
    return jnp.broadcast_to(jnp.sum(total, axis=0, keepdims=True), (8, channels))


def times(lhs, weight, taps):
    rhs = jnp.concatenate([weight[tap] for tap in taps], axis=1)
    return lax.dot_general(lhs, rhs, (((1,), (1,)), ((), ())), preferred_element_type=jnp.float32)


def silu(value):
    half = 0.5 * value
    return half + half * jnp.tanh(half)


def prepare_kernel(
    power, counts, stem_own, stem_other, small_own, small_other, selection, stem_full, vectors
):
    tile_count = counts.shape[0]
    width = tile_count * W_DEV
    me = lax.axis_index("tile")
    core = lax.axis_index("chan")
    zc = stem_own.shape[1]
    leftmost = me * W_DEV - HALO

    blocks = selection.shape[0] // (3 * width)
    packed_rows = tile_count * PACKED
    lane = lax.broadcasted_iota(jnp.int32, (8, packed_rows), 1)
    place_at = lane // PACKED
    row_at = lane - place_at * PACKED
    slot_at = jnp.floor((row_at.astype(jnp.float32) + 0.5) * (1.0 / blocks)).astype(jnp.int32)
    held = jnp.full((8, packed_rows), -5, jnp.int32)
    start = jnp.int32(0)
    bits = tile_count.bit_length() - 1
    for owner in range(tile_count):
        place = jnp.int32(owner)
        if power:
            apart = me ^ owner
            far = apart >> (bits - 2)
            place = jnp.where(far == 2, 1 + 2 * core, jnp.where(far == 1, 3 - 2 * core, far))
            place = jnp.where(far == 3, 2, place)
            for bit in range(bits - 2):
                place += ((apart >> bit) & 1) << (bits - 1 - bit)
        count = counts[owner]
        held = jnp.where((place_at == place) & (slot_at < count), start + slot_at, held)
        start = start + count
    code = (held * 16 + row_at - slot_at * blocks)[0:1]
    position = lax.broadcasted_iota(jnp.int32, (3 * width, packed_rows), 0)
    shift = (position >= width).astype(jnp.int32) + (position >= 2 * width).astype(jnp.int32)
    column = position - shift * width + leftmost
    column = jnp.where(column < 0, column + width, column)
    column = jnp.where(column >= width, column - width, column)
    wanted = (column + shift - 1) * 16
    for block in range(blocks):
        rows = slice(block * 3 * width, (block + 1) * 3 * width)
        selection[rows, :] = (wanted + block == code).astype(jnp.bfloat16)

    stem_full[...] = jnp.zeros(stem_full.shape, jnp.bfloat16)
    for tap in range(27):
        a, b, e = tap // 9, tap // 3 % 3, tap % 3
        at = e * 4 * zc + b * zc
        stem_full[a, at : at + zc, :] = joined(stem_own[tap], stem_other[tap], core)
    vectors[...] = joined(small_own[...], small_other[...], core)


def first_kernel(
    owners,
    selection,
    stem_full,
    vectors,
    small_own,
    weight_far,
    unread,
    act_out,
    hidden_out,
    packed,
    shifted,
    patches,
    hidden,
    acts,
    produced,
    sums,
    weight,
    arrival,
):
    fetch = pltpu.make_async_copy(weight_far, weight, arrival)
    fetch.start()
    tile_count = owners.shape[0]
    width = tile_count * W_DEV
    me = lax.axis_index("tile")
    core = lax.axis_index("chan")
    full, half = vectors.shape[1], small_own.shape[1]
    blocks = selection.shape[0] // (3 * width)
    frame_blocks = blocks // F
    frame_lanes = frame_blocks * 128
    zc = frame_lanes // H
    pieces = max(1, width // 16)
    rows = H // pieces
    cells = F * H * width
    leftmost = me * W_DEV - HALO
    packed[...] = jnp.zeros(packed.shape, jnp.bfloat16)
    packed[:, 0 : owners.shape[1], :] = owners[...]
    every = jnp.dot(
        selection[...],
        packed[...].reshape(tile_count * PACKED, 128),
        preferred_element_type=jnp.float32,
    )
    blank = jnp.zeros((3 * width, shifted.shape[3] - frame_lanes), jnp.float32)
    for frame in range(F):
        parts = []
        for block in range(frame * frame_blocks, (frame + 1) * frame_blocks):
            parts.append(every[block * 3 * width : (block + 1) * 3 * width])
        chosen = pltpu.roll(jnp.concatenate(parts + [blank], axis=1), zc, axis=1)
        shifted[:, frame] = chosen.reshape(3, width, shifted.shape[3])

    stem_bias = vectors[0:1]
    first_gain = vectors[1:2]
    first_shift = vectors[2:3]

    per_block = 128 // zc
    lane128 = lax.broadcasted_iota(jnp.int32, (F, width, 128), 2)
    for row in range(H):
        block = row // per_block * 128
        offset = row % per_block * zc
        window = shifted[:, :, :, block : block + 256]
        one = pltpu.roll(window[0], (256 - offset) % 256, axis=2)[:, :, :128]
        two = pltpu.roll(window[1], (320 - offset) % 256, axis=2)[:, :, :128]
        three = pltpu.roll(window[2], (256 - offset) % 256, axis=2)[:, :, :128]
        patches[:, row, :, 0:128] = jnp.where(lane128 < 64, one, two).astype(jnp.bfloat16)
        patches[:, row, :, 128:256] = three.astype(jnp.bfloat16)

    def over_pieces(body):
        if pieces == 1:
            body(0)
        else:
            lax.fori_loop(0, pieces, lambda i, _: (body(i * rows), 0)[1], 0)

    def span(frame, row):
        return pl.ds(pl.multiple_of((frame * H + row) * width, 16), rows * width)

    sums[...] = jnp.zeros_like(sums)
    for frame in range(F):

        def stem(row):
            total = jnp.zeros((rows * width, full), jnp.float32)
            for a in range(max(0, 2 - frame), 3):
                lhs = patches[frame + a - 2, pl.ds(row, rows)].reshape(rows * width, 256)
                total += jnp.dot(lhs, stem_full[a], preferred_element_type=jnp.float32)
            value = (total + stem_bias).astype(jnp.bfloat16).astype(jnp.float32)
            put(hidden, span(frame, row), value)
            sums[0:1, :] += jnp.sum(value, axis=0, keepdims=True)

        over_pieces(stem)

    per_group = full // GROUPS
    mean = group_mean(jnp.broadcast_to(sums[0:1, :], (8, full)), per_group, cells)
    variance = group_mean(squares(hidden, mean), per_group, cells)
    scale = lax.rsqrt(variance + EPSILON) * first_gain

    spot = lax.broadcasted_iota(jnp.int32, (1, width, full), 1) + leftmost
    spot = jnp.where(spot < 0, spot + width, spot)
    spot = jnp.where(spot >= width, spot - width, spot)
    zero_row = jnp.zeros((width, full), jnp.bfloat16)
    for e in range(3):
        for frame in range(F):
            acts[e, frame, 0] = zero_row
            acts[e, frame, H + 1] = zero_row
    for frame in range(F):

        def activate(i, _):
            row = i * 2
            place = pl.ds(pl.multiple_of((frame * H + row) * width, 16), 2 * width)
            spread = take(hidden, place, full) - mean
            value = silu(spread * scale + first_shift).reshape(2, width, full)
            left = jnp.where(spot == 0, 0.0, pltpu.roll(value, 1, axis=1))
            right = jnp.where(spot == width - 1, 0.0, pltpu.roll(value, width - 1, axis=1))
            place = pl.ds(row + 1, 2)
            acts[0, frame, place] = left.astype(jnp.bfloat16)
            acts[1, frame, place] = value.astype(jnp.bfloat16)
            acts[2, frame, place] = right.astype(jnp.bfloat16)
            return _

        lax.fori_loop(0, H // 2, activate, 0, unroll=2)

    fetch.wait()
    first_bias = small_own[4:5]
    for frame in range(F):

        def convolve(row):
            used = range(max(0, 2 - frame) * 9, 27)
            lhs = jnp.concatenate(
                [
                    acts[tap % 3, frame + tap // 9 - 2, pl.ds(row + tap // 3 % 3, rows)].reshape(
                        rows * width, full
                    )
                    for tap in used
                ],
                axis=1,
            )
            total = times(lhs, weight, used)
            value = (total + first_bias).astype(jnp.bfloat16).astype(jnp.float32)
            put(produced, span(frame, row), value)
            sums[2:3, 0:half] += jnp.sum(value, axis=0, keepdims=True)

        over_pieces(convolve)

    mean = group_mean(jnp.broadcast_to(sums[2:3, 0:half], (8, half)), per_group, cells)
    variance = group_mean(squares(produced, mean), per_group, cells)
    scale = lax.rsqrt(variance + EPSILON) * small_own[5:6]
    second_shift = small_own[6:7]
    for spot_at in range(W_DEV + 2 * HALO):
        value = take(produced, pl.ds(spot_at, F * H, stride=width), half)
        value = silu((value - mean) * scale + second_shift)
        real = (leftmost + spot_at >= 0) & (leftmost + spot_at < width)
        act_out[spot_at] = jnp.where(real, value, 0.0).astype(jnp.bfloat16)
    frames = F // 2
    for spot_at in range(1, W_DEV + 3):
        begin = core * (frames * H * width) + spot_at
        value = take(hidden, pl.ds(begin, frames * H, stride=width), full)
        hidden_out[spot_at - 1] = value.astype(jnp.bfloat16)


def second_kernel(
    tile_count,
    act_own,
    act_other,
    hidden_in,
    weight_own,
    weight_other,
    vectors,
    up_weight,
    up_bias,
    out,
    slots,
    taps,
    flat,
):
    width = tile_count * W_DEV
    me = lax.axis_index("tile")
    core = lax.axis_index("chan")
    columns, cells, half = act_own.shape
    full = 2 * half
    frames = F // 2
    rows = frames * H
    inner = columns - 2
    slots[...] = jnp.zeros_like(slots)
    for column in range(columns):
        value = joined(
            act_own[column].astype(jnp.float32), act_other[column].astype(jnp.float32), core
        )
        before = jnp.where(core == 0, 0.0, value[0:rows])
        now = jnp.where(core == 0, value[0:rows], value[rows:])
        for slot in range(frames):
            at = slot * 32 + 8
            slots[column, at : at + H, :] = before[slot * H : (slot + 1) * H]
            at = (slot + frames) * 32 + 8
            slots[column, at : at + H, :] = now[slot * H : (slot + 1) * H]
    for a in range(3):
        for b in range(3):
            parts = []
            for frame in range(frames):
                at = (frame + a) * 32 + 7 + b
                parts.append(slots[:, at : at + H, :])
            taps[3 * a + b] = jnp.concatenate(parts, axis=1).astype(jnp.bfloat16)


    def convolve(weight):
        lhs = jnp.concatenate(
            [
                taps[tap // 3, tap % 3 : tap % 3 + inner].reshape(inner * rows, full)
                for tap in range(27)
            ],
            axis=1,
        )
        return times(lhs, weight, range(27))

    mine = convolve(weight_own)
    theirs = convolve(weight_other)
    second_out = joined(mine, theirs, core) + vectors[3:4]
    hidden = hidden_in[...].astype(jnp.float32) + second_out.reshape(inner, rows, full)
    spot = lax.broadcasted_iota(jnp.int32, (inner, rows, full), 0) + me * W_DEV - 1
    hidden = jnp.where((spot >= 0) & (spot < width), hidden, 0.0).astype(jnp.bfloat16)
    hidden = hidden.reshape(inner * rows, full)

    line = lax.broadcasted_iota(jnp.int32, (inner * frames, H, half), 1)
    upper, lower = [], []
    pad = jnp.zeros((256 - half % 256, full), jnp.bfloat16)
    rhs = jnp.concatenate(
        [part for tap in range(9) for part in (up_weight[tap], pad)], axis=0
    )
    spread = rhs.shape[0] // 9
    every = lax.dot_general(
        hidden, rhs, (((1,), (1,)), ((), ())), preferred_element_type=jnp.float32
    )
    for e in range(3):
        made = []
        for b in range(3):
            at = (3 * b + e) * spread
            made.append(every[:, at : at + half].reshape(inner * frames, H, half))
        above = jnp.where(line == 0, 0.0, pltpu.roll(made[0], 1, axis=1))
        below = jnp.where(line == H - 1, 0.0, pltpu.roll(made[2], H - 1, axis=1))
        upper.append((above + made[1] + made[2]).reshape(inner, frames, H, half))
        lower.append((made[0] + made[1] + below).reshape(inner, frames, H, half))
    bias = up_bias[...]
    span = 2 * W_DEV
    for parity, sums in ((0, upper), (1, lower)):
        for x in range(W_DEV):
            at = x + 1
            for side in range(2):
                if side == 0:
                    value = sums[0][at - 1] + sums[1][at] + sums[2][at]
                else:
                    value = sums[0][at] + sums[1][at] + sums[2][at + 1]
                for frame in range(frames):
                    begin = frame * 2 * H * span + parity * span + 2 * x + side
                    put(flat, pl.ds(begin, H, stride=2 * span), value[frame] + bias)
    out[...] = take(flat, slice(None), out.shape[-1]).astype(jnp.bfloat16).reshape(out.shape)


def exchanged(block, step):
    count = lax.axis_size("tile")
    moved = lax.ppermute(block, "tile", [(i, i ^ step) for i in range(count)])
    return jnp.concatenate([block, moved], axis=0)


def on_device(
    owner_latent,
    tile_counts,
    stem_weight,
    stem_bias,
    first_gain,
    first_shift,
    first_weight,
    first_bias,
    second_gain,
    second_shift,
    second_weight,
    second_bias,
    upsample_weight,
    upsample_bias,
):
    tile_count = lax.axis_size("tile")
    width = tile_count * W_DEV
    _, slot_count, row_length = owner_latent.shape
    zc, half = stem_weight.shape[1], stem_weight.shape[2]
    full = 2 * half
    out_channels = upsample_weight.shape[2]
    first_weight = first_weight.transpose(0, 2, 1)
    second_weight = second_weight.transpose(0, 2, 1)
    upsample_weight = upsample_weight.transpose(0, 2, 1)
    swap = [(0, 1), (1, 0)]
    frames = F // 2

    block_rows = slot_count * row_length // 128
    latents = owner_latent.reshape(1, block_rows, 128)
    small = jnp.stack(
        [
            stem_bias,
            first_gain,
            first_shift,
            second_bias,
            first_bias,
            second_gain,
            second_shift,
            jnp.zeros_like(stem_bias),
        ]
    )
    window = W_DEV + 2 * HALO
    vmem = pl.BlockSpec(memory_space=pltpu.VMEM)
    far = pl.BlockSpec(memory_space=pltpu.HBM)

    def prepare(small, small_other, stem_other, power):
        return pl.pallas_call(
            functools.partial(prepare_kernel, power),
            out_shape=(
                jax.ShapeDtypeStruct((row_length // 128 * 3 * width, PACKED * tile_count), jnp.bfloat16),
                jax.ShapeDtypeStruct((3, 256, full), jnp.bfloat16),
                jax.ShapeDtypeStruct((small.shape[0], full), jnp.float32),
            ),
            in_specs=[pl.BlockSpec(memory_space=pltpu.SMEM)] + [vmem] * 4,
            out_specs=(vmem,) * 3,
            cost_estimate=pl.CostEstimate(flops=10**8, bytes_accessed=10**6, transcendentals=0),
            compiler_params=pltpu.CompilerParams(
                vmem_limit_bytes=(6 + 2 * width // 16) * 1024 * 1024
            ),
        )(tile_counts, stem_weight, stem_other, small, small_other)

    stem_other = lax.ppermute(stem_weight, "chan", swap)
    second_other = lax.ppermute(second_weight, "chan", swap)
    power = tile_count & (tile_count - 1) == 0 and tile_count >= 4
    if power:
        away, near = tile_count // 2, tile_count // 4
        pairs = [
            (2 * i + c, 2 * (i ^ (near if c else away)) + c)
            for i in range(tile_count)
            for c in range(2)
        ]
        one = lax.ppermute(latents, ("tile", "chan"), pairs)
        both = [(i, i ^ away ^ near) for i in range(tile_count)]
        two = lax.ppermute(latents, "tile", both)
        small_other = lax.ppermute(small, "chan", swap)
        three = lax.ppermute(one, "chan", swap)
        owners = jnp.concatenate([latents, one, two, three], axis=0)
        owners, small_other, stem_other = lax.optimization_barrier(
            (owners, small_other, stem_other)
        )
        step = near
        while step > 1:
            step //= 2
            owners = exchanged(owners, step)
        prepared = prepare(small, small_other, stem_other, power)
    else:
        small_other = lax.ppermute(small, "chan", swap)
        owners = lax.all_gather(latents, "tile", axis=0, tiled=True)
        prepared = prepare(small, small_other, stem_other, power)
    selection, stem_full, vectors = prepared
    act, hidden = pl.pallas_call(
        first_kernel,
        out_shape=(
            jax.ShapeDtypeStruct((window, F * H, half), jnp.bfloat16),
            jax.ShapeDtypeStruct((window - 2, frames * H, full), jnp.bfloat16),
        ),
        in_specs=[vmem] * 5 + [far, pl.BlockSpec(memory_space=pl.ANY)],
        out_specs=(vmem, vmem),
        scratch_shapes=[
            pltpu.VMEM((tile_count, PACKED, 128), jnp.bfloat16),
            pltpu.VMEM((3, F, width, H_PAD * zc), jnp.float32),
            pltpu.VMEM((F, H, width, 256), jnp.bfloat16),
            pltpu.VMEM((full // 128, F * H * width, 128), jnp.float32),
            pltpu.VMEM((3, F, H + 2, width, full), jnp.bfloat16),
            pltpu.VMEM((pl.cdiv(half, 128), F * H * width, 128), jnp.float32),
            pltpu.VMEM((8, full), jnp.float32),
            pltpu.VMEM(first_weight.shape, jnp.bfloat16),
            pltpu.SemaphoreType.DMA,
        ],
        cost_estimate=pl.CostEstimate(
            flops=2 * F * H * width * 27 * full * half * 3 // 4,
            bytes_accessed=27 * full * half * 2,
            transcendentals=F * H * width * full,
        ),
        compiler_params=pltpu.CompilerParams(
            vmem_limit_bytes=min(60, 12 + 12 * width // 16) * 1024 * 1024
        ),
    )(
        owners,
        selection,
        stem_full,
        vectors,
        small,
        pltpu.with_memory_space_constraint(first_weight, pltpu.HBM),
        second_other,
    )

    act_other = lax.ppermute(act, "chan", swap)

    out = pl.pallas_call(
        functools.partial(second_kernel, tile_count),
        out_shape=jax.ShapeDtypeStruct((frames, 2 * H, 2 * W_DEV, out_channels), jnp.bfloat16),
        in_specs=[vmem] * 8,
        out_specs=vmem,
        scratch_shapes=[
            pltpu.VMEM((window, 2 * frames * 32 + 8, full), jnp.float32),
            pltpu.VMEM((9, window, frames * H, full), jnp.bfloat16),
            pltpu.VMEM((pl.cdiv(out_channels, 128), frames * 2 * H * 2 * W_DEV, 128), jnp.float32),
        ],
        cost_estimate=pl.CostEstimate(
            flops=2 * 4 * 48 * 27 * full * full,
            bytes_accessed=2 * 27 * full * half * 2,
            transcendentals=0,
        ),
        compiler_params=pltpu.CompilerParams(vmem_limit_bytes=24 * 1024 * 1024),
    )(
        act,
        act_other,
        hidden,
        second_weight,
        second_other,
        vectors,
        upsample_weight,
        upsample_bias.reshape(1, -1),
    )
    return out


def solution(mesh):
    placed = (
        P(("clip", "tile"), None, None),
        P("clip"),
        P(None, None, "chan"),
        P("chan"),
        P("chan"),
        P("chan"),
        P(None, None, "chan"),
        P("chan"),
        P("chan"),
        P("chan"),
        P(None, None, "chan"),
        P("chan"),
        P(),
        P(),
    )

    return jax.shard_map(
        on_device,
        mesh=mesh,
        in_specs=placed,
        out_specs=P(("clip", "chan"), None, "tile", None),
        check_vma=False,
    )
```

```python
import functools

import jax
import jax.numpy as jnp
from jax import lax
from jax.experimental import pallas as pl
from jax.experimental.pallas import tpu as pltpu
from jax.sharding import PartitionSpec as P


GROUPS = 32
F = 4
H = 24
W_DEV = 2
HALO = 2
PACKED = 64
H_PAD = 32
EPSILON = 1e-06


def joined(own, other, core):
    low = jnp.concatenate([own, other], axis=-1)
    high = jnp.concatenate([other, own], axis=-1)
    return jnp.where(core == 0, low, high)


def group_mean(column_sums, per_group, cells):
    channels = column_sums.shape[1]
    row = lax.broadcasted_iota(jnp.int32, (channels, channels), 0).astype(jnp.float32)
    column = lax.broadcasted_iota(jnp.int32, (channels, channels), 1).astype(jnp.float32)
    same = jnp.floor((row + 0.5) / per_group) == jnp.floor((column + 0.5) / per_group)
    total = jnp.dot(
        column_sums,
        same.astype(jnp.float32),
        precision=lax.Precision.HIGHEST,
        preferred_element_type=jnp.float32,
    )
    return total[0:1] * (1.0 / (cells * per_group))


def put(ref, place, value):
    for block in range(ref.shape[0]):
        part = value[:, block * 128 : (block + 1) * 128]
        ref[block, place, 0 : part.shape[1]] = part


def take(ref, place, channels):
    parts = []
    for block in range(ref.shape[0]):
        parts.append(ref[block, place, :][:, : channels - block * 128])
    return jnp.concatenate(parts, axis=1)


def squares(ref, mean):
    channels = mean.shape[1]
    step = 64

    def add(i, total):
        spread = take(ref, pl.ds(pl.multiple_of(i * step, step), step), channels) - mean
        return total + jnp.sum((spread * spread).reshape(step // 8, 8, channels), axis=0)

    total = lax.fori_loop(
        0, ref.shape[1] // step, add, jnp.zeros((8, channels), jnp.float32), unroll=2
    )
    return jnp.broadcast_to(jnp.sum(total, axis=0, keepdims=True), (8, channels))


def times(lhs, weight, taps):
    rhs = jnp.concatenate([weight[tap] for tap in taps], axis=1)
    return lax.dot_general(lhs, rhs, (((1,), (1,)), ((), ())), preferred_element_type=jnp.float32)


def silu(value):
    half = 0.5 * value
    return half + half * jnp.tanh(half)


def prepare_kernel(
    power, counts, stem_own, stem_other, small_own, small_other, selection, stem_full, vectors
):
    tile_count = counts.shape[0]
    width = tile_count * W_DEV
    me = lax.axis_index("tile")
    core = lax.axis_index("chan")
    zc = stem_own.shape[1]
    leftmost = me * W_DEV - HALO

    blocks = selection.shape[0] // (3 * width)
    packed_rows = tile_count * PACKED
    lane = lax.broadcasted_iota(jnp.int32, (8, packed_rows), 1)
    place_at = lane // PACKED
    row_at = lane - place_at * PACKED
    slot_at = jnp.floor((row_at.astype(jnp.float32) + 0.5) * (1.0 / blocks)).astype(jnp.int32)
    held = jnp.full((8, packed_rows), -5, jnp.int32)
    start = jnp.int32(0)
    bits = tile_count.bit_length() - 1
    for owner in range(tile_count):
        place = jnp.int32(owner)
        if power:
            apart = me ^ owner
            far = apart >> (bits - 2)
            place = jnp.where(far == 2, 1 + 2 * core, jnp.where(far == 1, 3 - 2 * core, far))
            place = jnp.where(far == 3, 2, place)
            for bit in range(bits - 2):
                place += ((apart >> bit) & 1) << (bits - 1 - bit)
        count = counts[owner]
        held = jnp.where((place_at == place) & (slot_at < count), start + slot_at, held)
        start = start + count
    code = (held * 16 + row_at - slot_at * blocks)[0:1]
    position = lax.broadcasted_iota(jnp.int32, (3 * width, packed_rows), 0)
    shift = (position >= width).astype(jnp.int32) + (position >= 2 * width).astype(jnp.int32)
    column = position - shift * width + leftmost
    column = jnp.where(column < 0, column + width, column)
    column = jnp.where(column >= width, column - width, column)
    wanted = (column + shift - 1) * 16
    for block in range(blocks):
        rows = slice(block * 3 * width, (block + 1) * 3 * width)
        selection[rows, :] = (wanted + block == code).astype(jnp.bfloat16)

    stem_full[...] = jnp.zeros(stem_full.shape, jnp.bfloat16)
    for tap in range(27):
        a, b, e = tap // 9, tap // 3 % 3, tap % 3
        at = e * 4 * zc + b * zc
        stem_full[a, at : at + zc, :] = joined(stem_own[tap], stem_other[tap], core)
    vectors[...] = joined(small_own[...], small_other[...], core)


def first_kernel(
    owners,
    selection,
    stem_full,
    vectors,
    small_own,
    weight_far,
    next_far,
    act_out,
    hidden_out,
    next_near,
    packed,
    shifted,
    patches,
    hidden,
    acts,
    produced,
    sums,
    weight,
    arrival,
    next_arrival,
):
    fetch = pltpu.make_async_copy(weight_far, weight, arrival)
    fetch.start()
    tile_count = owners.shape[0]
    width = tile_count * W_DEV
    me = lax.axis_index("tile")
    core = lax.axis_index("chan")
    full, half = vectors.shape[1], small_own.shape[1]
    blocks = selection.shape[0] // (3 * width)
    frame_blocks = blocks // F
    frame_lanes = frame_blocks * 128
    zc = frame_lanes // H
    pieces = max(1, width // 16)
    rows = H // pieces
    cells = F * H * width
    leftmost = me * W_DEV - HALO
    packed[...] = jnp.zeros(packed.shape, jnp.bfloat16)
    packed[:, 0 : owners.shape[1], :] = owners[...]
    every = jnp.dot(
        selection[...],
        packed[...].reshape(tile_count * PACKED, 128),
        preferred_element_type=jnp.float32,
    )
    blank = jnp.zeros((3 * width, shifted.shape[3] - frame_lanes), jnp.float32)
    for frame in range(F):
        parts = []
        for block in range(frame * frame_blocks, (frame + 1) * frame_blocks):
            parts.append(every[block * 3 * width : (block + 1) * 3 * width])
        chosen = pltpu.roll(jnp.concatenate(parts + [blank], axis=1), zc, axis=1)
        shifted[:, frame] = chosen.reshape(3, width, shifted.shape[3])

    stem_bias = vectors[0:1]
    first_gain = vectors[1:2]
    first_shift = vectors[2:3]

    per_block = 128 // zc
    lane128 = lax.broadcasted_iota(jnp.int32, (F, width, 128), 2)
    for row in range(H):
        block = row // per_block * 128
        offset = row % per_block * zc
        window = shifted[:, :, :, block : block + 256]
        one = pltpu.roll(window[0], (256 - offset) % 256, axis=2)[:, :, :128]
        two = pltpu.roll(window[1], (320 - offset) % 256, axis=2)[:, :, :128]
        three = pltpu.roll(window[2], (256 - offset) % 256, axis=2)[:, :, :128]
        patches[:, row, :, 0:128] = jnp.where(lane128 < 64, one, two).astype(jnp.bfloat16)
        patches[:, row, :, 128:256] = three.astype(jnp.bfloat16)

    def over_pieces(body):
        if pieces == 1:
            body(0)
        else:
            lax.fori_loop(0, pieces, lambda i, _: (body(i * rows), 0)[1], 0)

    def span(frame, row):
        return pl.ds(pl.multiple_of((frame * H + row) * width, 16), rows * width)

    sums[...] = jnp.zeros_like(sums)
    for frame in range(F):

        def stem(row):
            total = jnp.zeros((rows * width, full), jnp.float32)
            for a in range(max(0, 2 - frame), 3):
                lhs = patches[frame + a - 2, pl.ds(row, rows)].reshape(rows * width, 256)
                total += jnp.dot(lhs, stem_full[a], preferred_element_type=jnp.float32)
            value = (total + stem_bias).astype(jnp.bfloat16).astype(jnp.float32)
            put(hidden, span(frame, row), value)
            sums[0:1, :] += jnp.sum(value, axis=0, keepdims=True)

        over_pieces(stem)

    per_group = full // GROUPS
    mean = group_mean(jnp.broadcast_to(sums[0:1, :], (8, full)), per_group, cells)
    variance = group_mean(squares(hidden, mean), per_group, cells)
    scale = lax.rsqrt(variance + EPSILON) * first_gain

    spot = lax.broadcasted_iota(jnp.int32, (1, width, full), 1) + leftmost
    spot = jnp.where(spot < 0, spot + width, spot)
    spot = jnp.where(spot >= width, spot - width, spot)
    zero_row = jnp.zeros((width, full), jnp.bfloat16)
    for e in range(3):
        for frame in range(F):
            acts[e, frame, 0] = zero_row
            acts[e, frame, H + 1] = zero_row
    for frame in range(F):

        def activate(i, _):
            row = i * 2
            place = pl.ds(pl.multiple_of((frame * H + row) * width, 16), 2 * width)
            spread = take(hidden, place, full) - mean
            value = silu(spread * scale + first_shift).reshape(2, width, full)
            left = jnp.where(spot == 0, 0.0, pltpu.roll(value, 1, axis=1))
            right = jnp.where(spot == width - 1, 0.0, pltpu.roll(value, width - 1, axis=1))
            place = pl.ds(row + 1, 2)
            acts[0, frame, place] = left.astype(jnp.bfloat16)
            acts[1, frame, place] = value.astype(jnp.bfloat16)
            acts[2, frame, place] = right.astype(jnp.bfloat16)
            return _

        lax.fori_loop(0, H // 2, activate, 0, unroll=2)

    fetch.wait()
    carry = pltpu.make_async_copy(next_far, next_near, next_arrival)
    carry.start()
    first_bias = small_own[4:5]
    for frame in range(F):

        def convolve(row):
            used = range(max(0, 2 - frame) * 9, 27)
            lhs = jnp.concatenate(
                [
                    acts[tap % 3, frame + tap // 9 - 2, pl.ds(row + tap // 3 % 3, rows)].reshape(
                        rows * width, full
                    )
                    for tap in used
                ],
                axis=1,
            )
            total = times(lhs, weight, used)
            value = (total + first_bias).astype(jnp.bfloat16).astype(jnp.float32)
            put(produced, span(frame, row), value)
            sums[2:3, 0:half] += jnp.sum(value, axis=0, keepdims=True)

        over_pieces(convolve)

    mean = group_mean(jnp.broadcast_to(sums[2:3, 0:half], (8, half)), per_group, cells)
    variance = group_mean(squares(produced, mean), per_group, cells)
    scale = lax.rsqrt(variance + EPSILON) * small_own[5:6]
    second_shift = small_own[6:7]
    for spot_at in range(W_DEV + 2 * HALO):
        value = take(produced, pl.ds(spot_at, F * H, stride=width), half)
        value = silu((value - mean) * scale + second_shift)
        real = (leftmost + spot_at >= 0) & (leftmost + spot_at < width)
        act_out[spot_at] = jnp.where(real, value, 0.0).astype(jnp.bfloat16)
    frames = F // 2
    for spot_at in range(1, W_DEV + 3):
        begin = core * (frames * H * width) + spot_at
        value = take(hidden, pl.ds(begin, frames * H, stride=width), full)
        hidden_out[spot_at - 1] = value.astype(jnp.bfloat16)
    carry.wait()


def second_kernel(
    tile_count,
    act_own,
    act_other,
    hidden_in,
    weight_own,
    weight_other,
    vectors,
    up_weight,
    up_bias,
    out,
    slots,
    taps,
    flat,
):
    width = tile_count * W_DEV
    me = lax.axis_index("tile")
    core = lax.axis_index("chan")
    columns, cells, half = act_own.shape
    full = 2 * half
    frames = F // 2
    rows = frames * H
    inner = columns - 2
    slots[...] = jnp.zeros_like(slots)
    for column in range(columns):
        value = joined(
            act_own[column].astype(jnp.float32), act_other[column].astype(jnp.float32), core
        )
        before = jnp.where(core == 0, 0.0, value[0:rows])
        now = jnp.where(core == 0, value[0:rows], value[rows:])
        for slot in range(frames):
            at = slot * 32 + 8
            slots[column, at : at + H, :] = before[slot * H : (slot + 1) * H]
            at = (slot + frames) * 32 + 8
            slots[column, at : at + H, :] = now[slot * H : (slot + 1) * H]
    for a in range(3):
        for b in range(3):
            parts = []
            for frame in range(frames):
                at = (frame + a) * 32 + 7 + b
                parts.append(slots[:, at : at + H, :])
            taps[3 * a + b] = jnp.concatenate(parts, axis=1).astype(jnp.bfloat16)


    def convolve(weight):
        lhs = jnp.concatenate(
            [
                taps[tap // 3, tap % 3 : tap % 3 + inner].reshape(inner * rows, full)
                for tap in range(27)
            ],
            axis=1,
        )
        return times(lhs, weight, range(27))

    mine = convolve(weight_own)
    theirs = convolve(weight_other)
    second_out = joined(mine, theirs, core) + vectors[3:4]
    hidden = hidden_in[...].astype(jnp.float32) + second_out.reshape(inner, rows, full)
    spot = lax.broadcasted_iota(jnp.int32, (inner, rows, full), 0) + me * W_DEV - 1
    hidden = jnp.where((spot >= 0) & (spot < width), hidden, 0.0).astype(jnp.bfloat16)
    hidden = hidden.reshape(inner * rows, full)

    line = lax.broadcasted_iota(jnp.int32, (inner * frames, H, half), 1)
    upper, lower = [], []
    pad = jnp.zeros((256 - half % 256, full), jnp.bfloat16)
    rhs = jnp.concatenate(
        [part for tap in range(9) for part in (up_weight[tap], pad)], axis=0
    )
    spread = rhs.shape[0] // 9
    every = lax.dot_general(
        hidden, rhs, (((1,), (1,)), ((), ())), preferred_element_type=jnp.float32
    )
    for e in range(3):
        made = []
        for b in range(3):
            at = (3 * b + e) * spread
            made.append(every[:, at : at + half].reshape(inner * frames, H, half))
        above = jnp.where(line == 0, 0.0, pltpu.roll(made[0], 1, axis=1))
        below = jnp.where(line == H - 1, 0.0, pltpu.roll(made[2], H - 1, axis=1))
        upper.append((above + made[1] + made[2]).reshape(inner, frames, H, half))
        lower.append((made[0] + made[1] + below).reshape(inner, frames, H, half))
    bias = up_bias[...]
    span = 2 * W_DEV
    for parity, sums in ((0, upper), (1, lower)):
        for x in range(W_DEV):
            at = x + 1
            for side in range(2):
                if side == 0:
                    value = sums[0][at - 1] + sums[1][at] + sums[2][at]
                else:
                    value = sums[0][at] + sums[1][at] + sums[2][at + 1]
                for frame in range(frames):
                    begin = frame * 2 * H * span + parity * span + 2 * x + side
                    put(flat, pl.ds(begin, H, stride=2 * span), value[frame] + bias)
    out[...] = take(flat, slice(None), out.shape[-1]).astype(jnp.bfloat16).reshape(out.shape)


def exchanged(block, step):
    count = lax.axis_size("tile")
    moved = lax.ppermute(block, "tile", [(i, i ^ step) for i in range(count)])
    return jnp.concatenate([block, moved], axis=0)


def on_device(
    owner_latent,
    tile_counts,
    stem_weight,
    stem_bias,
    first_gain,
    first_shift,
    first_weight,
    first_bias,
    second_gain,
    second_shift,
    second_weight,
    second_bias,
    upsample_weight,
    upsample_bias,
):
    tile_count = lax.axis_size("tile")
    width = tile_count * W_DEV
    _, slot_count, row_length = owner_latent.shape
    zc, half = stem_weight.shape[1], stem_weight.shape[2]
    full = 2 * half
    out_channels = upsample_weight.shape[2]
    first_weight = first_weight.transpose(0, 2, 1)
    second_weight = second_weight.transpose(0, 2, 1)
    upsample_weight = upsample_weight.transpose(0, 2, 1)
    swap = [(0, 1), (1, 0)]
    frames = F // 2

    block_rows = slot_count * row_length // 128
    latents = owner_latent.reshape(1, block_rows, 128)
    small = jnp.stack(
        [
            stem_bias,
            first_gain,
            first_shift,
            second_bias,
            first_bias,
            second_gain,
            second_shift,
            jnp.zeros_like(stem_bias),
        ]
    )
    window = W_DEV + 2 * HALO
    vmem = pl.BlockSpec(memory_space=pltpu.VMEM)
    far = pl.BlockSpec(memory_space=pltpu.HBM)

    def prepare(small, small_other, stem_other, power):
        return pl.pallas_call(
            functools.partial(prepare_kernel, power),
            out_shape=(
                jax.ShapeDtypeStruct((row_length // 128 * 3 * width, PACKED * tile_count), jnp.bfloat16),
                jax.ShapeDtypeStruct((3, 256, full), jnp.bfloat16),
                jax.ShapeDtypeStruct((small.shape[0], full), jnp.float32),
            ),
            in_specs=[pl.BlockSpec(memory_space=pltpu.SMEM)] + [vmem] * 4,
            out_specs=(vmem,) * 3,
            cost_estimate=pl.CostEstimate(flops=10**8, bytes_accessed=10**6, transcendentals=0),
            compiler_params=pltpu.CompilerParams(
                vmem_limit_bytes=(6 + 2 * width // 16) * 1024 * 1024
            ),
        )(tile_counts, stem_weight, stem_other, small, small_other)

    stem_other = lax.ppermute(stem_weight, "chan", swap)
    second_other = lax.ppermute(second_weight, "chan", swap)
    power = tile_count & (tile_count - 1) == 0 and tile_count >= 4
    if power:
        away, near = tile_count // 2, tile_count // 4
        pairs = [
            (2 * i + c, 2 * (i ^ (near if c else away)) + c)
            for i in range(tile_count)
            for c in range(2)
        ]
        one = lax.ppermute(latents, ("tile", "chan"), pairs)
        both = [(i, i ^ away ^ near) for i in range(tile_count)]
        two = lax.ppermute(latents, "tile", both)
        small_other = lax.ppermute(small, "chan", swap)
        three = lax.ppermute(one, "chan", swap)
        owners = jnp.concatenate([latents, one, two, three], axis=0)
        owners, small_other, stem_other = lax.optimization_barrier(
            (owners, small_other, stem_other)
        )
        step = near
        while step > 1:
            step //= 2
            owners = exchanged(owners, step)
        prepared = prepare(small, small_other, stem_other, power)
    else:
        small_other = lax.ppermute(small, "chan", swap)
        owners = lax.all_gather(latents, "tile", axis=0, tiled=True)
        prepared = prepare(small, small_other, stem_other, power)
    selection, stem_full, vectors = prepared
    act, hidden, second_near = pl.pallas_call(
        first_kernel,
        out_shape=(
            jax.ShapeDtypeStruct((window, F * H, half), jnp.bfloat16),
            jax.ShapeDtypeStruct((window - 2, frames * H, full), jnp.bfloat16),
            jax.ShapeDtypeStruct(second_weight.shape, jnp.bfloat16),
        ),
        in_specs=[vmem] * 5 + [far, far],
        out_specs=(vmem, vmem, vmem),
        scratch_shapes=[
            pltpu.VMEM((tile_count, PACKED, 128), jnp.bfloat16),
            pltpu.VMEM((3, F, width, H_PAD * zc), jnp.float32),
            pltpu.VMEM((F, H, width, 256), jnp.bfloat16),
            pltpu.VMEM((full // 128, F * H * width, 128), jnp.float32),
            pltpu.VMEM((3, F, H + 2, width, full), jnp.bfloat16),
            pltpu.VMEM((pl.cdiv(half, 128), F * H * width, 128), jnp.float32),
            pltpu.VMEM((8, full), jnp.float32),
            pltpu.VMEM(first_weight.shape, jnp.bfloat16),
            pltpu.SemaphoreType.DMA,
            pltpu.SemaphoreType.DMA,
        ],
        cost_estimate=pl.CostEstimate(
            flops=2 * F * H * width * 27 * full * half * 3 // 4,
            bytes_accessed=27 * full * half * 2,
            transcendentals=F * H * width * full,
        ),
        compiler_params=pltpu.CompilerParams(
            vmem_limit_bytes=min(60, 12 + 12 * width // 16) * 1024 * 1024
        ),
    )(
        owners,
        selection,
        stem_full,
        vectors,
        small,
        pltpu.with_memory_space_constraint(first_weight, pltpu.HBM),
        pltpu.with_memory_space_constraint(second_other, pltpu.HBM),
    )

    act_other = lax.ppermute(act, "chan", swap)

    out = pl.pallas_call(
        functools.partial(second_kernel, tile_count),
        out_shape=jax.ShapeDtypeStruct((frames, 2 * H, 2 * W_DEV, out_channels), jnp.bfloat16),
        in_specs=[vmem] * 8,
        out_specs=vmem,
        scratch_shapes=[
            pltpu.VMEM((window, 2 * frames * 32 + 8, full), jnp.float32),
            pltpu.VMEM((9, window, frames * H, full), jnp.bfloat16),
            pltpu.VMEM((pl.cdiv(out_channels, 128), frames * 2 * H * 2 * W_DEV, 128), jnp.float32),
        ],
        cost_estimate=pl.CostEstimate(
            flops=2 * 4 * 48 * 27 * full * full,
            bytes_accessed=2 * 27 * full * half * 2,
            transcendentals=0,
        ),
        compiler_params=pltpu.CompilerParams(vmem_limit_bytes=24 * 1024 * 1024),
    )(
        act,
        act_other,
        hidden,
        second_weight,
        second_near,
        vectors,
        upsample_weight,
        upsample_bias.reshape(1, -1),
    )
    return out


def solution(mesh):
    placed = (
        P(("clip", "tile"), None, None),
        P("clip"),
        P(None, None, "chan"),
        P("chan"),
        P("chan"),
        P("chan"),
        P(None, None, "chan"),
        P("chan"),
        P("chan"),
        P("chan"),
        P(None, None, "chan"),
        P("chan"),
        P(),
        P(),
    )

    return jax.shard_map(
        on_device,
        mesh=mesh,
        in_specs=placed,
        out_specs=P(("clip", "chan"), None, "tile", None),
        check_vma=False,
    )
```

```python
import functools

import jax
import jax.numpy as jnp
from jax import lax
from jax.experimental import pallas as pl
from jax.experimental.pallas import tpu as pltpu
from jax.sharding import PartitionSpec as P


GROUPS = 32
F = 4
H = 24
W_DEV = 2
HALO = 2
PACKED = 64
H_PAD = 32
EPSILON = 1e-06


def joined(own, other, core):
    low = jnp.concatenate([own, other], axis=-1)
    high = jnp.concatenate([other, own], axis=-1)
    return jnp.where(core == 0, low, high)


def group_mean(column_sums, per_group, cells):
    channels = column_sums.shape[1]
    row = lax.broadcasted_iota(jnp.int32, (channels, channels), 0).astype(jnp.float32)
    column = lax.broadcasted_iota(jnp.int32, (channels, channels), 1).astype(jnp.float32)
    same = jnp.floor((row + 0.5) / per_group) == jnp.floor((column + 0.5) / per_group)
    total = jnp.dot(
        column_sums,
        same.astype(jnp.float32),
        precision=lax.Precision.HIGHEST,
        preferred_element_type=jnp.float32,
    )
    return total[0:1] * (1.0 / (cells * per_group))


def put(ref, place, value):
    for block in range(ref.shape[0]):
        part = value[:, block * 128 : (block + 1) * 128]
        ref[block, place, 0 : part.shape[1]] = part


def take(ref, place, channels):
    parts = []
    for block in range(ref.shape[0]):
        parts.append(ref[block, place, :][:, : channels - block * 128])
    return jnp.concatenate(parts, axis=1)


def squares(ref, mean):
    channels = mean.shape[1]
    step = 64

    def add(i, total):
        spread = take(ref, pl.ds(pl.multiple_of(i * step, step), step), channels) - mean
        return total + jnp.sum((spread * spread).reshape(step // 8, 8, channels), axis=0)

    total = lax.fori_loop(
        0, ref.shape[1] // step, add, jnp.zeros((8, channels), jnp.float32), unroll=2
    )
    return jnp.broadcast_to(jnp.sum(total, axis=0, keepdims=True), (8, channels))


def times(lhs, weight, taps):
    rhs = jnp.concatenate([weight[tap] for tap in taps], axis=1)
    return lax.dot_general(lhs, rhs, (((1,), (1,)), ((), ())), preferred_element_type=jnp.float32)


def silu(value):
    half = 0.5 * value
    return half + half * jnp.tanh(half)


def prepare_kernel(
    power,
    counts_far,
    stem_far,
    stem_other,
    small_own,
    small_other,
    selection,
    stem_full,
    vectors,
    counts,
    stem_own,
    counts_arrival,
    stem_arrival,
):
    counts_fetch = pltpu.make_async_copy(counts_far, counts, counts_arrival)
    counts_fetch.start()
    stem_fetch = pltpu.make_async_copy(stem_far, stem_own, stem_arrival)
    stem_fetch.start()
    tile_count = counts.shape[0]
    width = tile_count * W_DEV
    me = lax.axis_index("tile")
    core = lax.axis_index("chan")
    zc = stem_own.shape[1]
    leftmost = me * W_DEV - HALO

    blocks = selection.shape[0] // (3 * width)
    packed_rows = tile_count * PACKED
    lane = lax.broadcasted_iota(jnp.int32, (8, packed_rows), 1)
    place_at = lane // PACKED
    row_at = lane - place_at * PACKED
    slot_at = jnp.floor((row_at.astype(jnp.float32) + 0.5) * (1.0 / blocks)).astype(jnp.int32)
    held = jnp.full((8, packed_rows), -5, jnp.int32)
    counts_fetch.wait()
    start = jnp.int32(0)
    bits = tile_count.bit_length() - 1
    for owner in range(tile_count):
        place = jnp.int32(owner)
        if power:
            apart = me ^ owner
            far = apart >> (bits - 2)
            place = jnp.where(far == 2, 1 + 2 * core, jnp.where(far == 1, 3 - 2 * core, far))
            place = jnp.where(far == 3, 2, place)
            for bit in range(bits - 2):
                place += ((apart >> bit) & 1) << (bits - 1 - bit)
        count = counts[owner]
        held = jnp.where((place_at == place) & (slot_at < count), start + slot_at, held)
        start = start + count
    code = (held * 16 + row_at - slot_at * blocks)[0:1]
    position = lax.broadcasted_iota(jnp.int32, (3 * width, packed_rows), 0)
    shift = (position >= width).astype(jnp.int32) + (position >= 2 * width).astype(jnp.int32)
    column = position - shift * width + leftmost
    column = jnp.where(column < 0, column + width, column)
    column = jnp.where(column >= width, column - width, column)
    wanted = (column + shift - 1) * 16
    for block in range(blocks):
        rows = slice(block * 3 * width, (block + 1) * 3 * width)
        selection[rows, :] = (wanted + block == code).astype(jnp.bfloat16)

    stem_full[...] = jnp.zeros(stem_full.shape, jnp.bfloat16)
    stem_fetch.wait()
    for tap in range(27):
        a, b, e = tap // 9, tap // 3 % 3, tap % 3
        at = e * 4 * zc + b * zc
        stem_full[a, at : at + zc, :] = joined(stem_own[tap], stem_other[tap], core)
    vectors[...] = joined(small_own[...], small_other[...], core)


def first_kernel(
    owners,
    selection,
    stem_full,
    vectors,
    small_own,
    weight_far,
    others_far,
    own_far,
    up_far,
    act_out,
    hidden_out,
    others_near,
    own_near,
    up_near,
    packed,
    shifted,
    patches,
    hidden,
    acts,
    produced,
    sums,
    weight,
    arrival,
    next_arrivals,
):
    fetch = pltpu.make_async_copy(weight_far, weight, arrival)
    fetch.start()
    tile_count = owners.shape[0]
    width = tile_count * W_DEV
    me = lax.axis_index("tile")
    core = lax.axis_index("chan")
    full, half = vectors.shape[1], small_own.shape[1]
    blocks = selection.shape[0] // (3 * width)
    frame_blocks = blocks // F
    frame_lanes = frame_blocks * 128
    zc = frame_lanes // H
    pieces = max(1, width // 16)
    rows = H // pieces
    cells = F * H * width
    leftmost = me * W_DEV - HALO
    packed[...] = jnp.zeros(packed.shape, jnp.bfloat16)
    packed[:, 0 : owners.shape[1], :] = owners[...]
    every = jnp.dot(
        selection[...],
        packed[...].reshape(tile_count * PACKED, 128),
        preferred_element_type=jnp.float32,
    )
    blank = jnp.zeros((3 * width, shifted.shape[3] - frame_lanes), jnp.float32)
    for frame in range(F):
        parts = []
        for block in range(frame * frame_blocks, (frame + 1) * frame_blocks):
            parts.append(every[block * 3 * width : (block + 1) * 3 * width])
        chosen = pltpu.roll(jnp.concatenate(parts + [blank], axis=1), zc, axis=1)
        shifted[:, frame] = chosen.reshape(3, width, shifted.shape[3])

    stem_bias = vectors[0:1]
    first_gain = vectors[1:2]
    first_shift = vectors[2:3]

    per_block = 128 // zc
    lane128 = lax.broadcasted_iota(jnp.int32, (F, width, 128), 2)
    for row in range(H):
        block = row // per_block * 128
        offset = row % per_block * zc
        window = shifted[:, :, :, block : block + 256]
        one = pltpu.roll(window[0], (256 - offset) % 256, axis=2)[:, :, :128]
        two = pltpu.roll(window[1], (320 - offset) % 256, axis=2)[:, :, :128]
        three = pltpu.roll(window[2], (256 - offset) % 256, axis=2)[:, :, :128]
        patches[:, row, :, 0:128] = jnp.where(lane128 < 64, one, two).astype(jnp.bfloat16)
        patches[:, row, :, 128:256] = three.astype(jnp.bfloat16)

    def over_pieces(body):
        if pieces == 1:
            body(0)
        else:
            lax.fori_loop(0, pieces, lambda i, _: (body(i * rows), 0)[1], 0)

    def span(frame, row):
        return pl.ds(pl.multiple_of((frame * H + row) * width, 16), rows * width)

    sums[...] = jnp.zeros_like(sums)
    for frame in range(F):

        def stem(row):
            total = jnp.zeros((rows * width, full), jnp.float32)
            for a in range(max(0, 2 - frame), 3):
                lhs = patches[frame + a - 2, pl.ds(row, rows)].reshape(rows * width, 256)
                total += jnp.dot(lhs, stem_full[a], preferred_element_type=jnp.float32)
            value = (total + stem_bias).astype(jnp.bfloat16).astype(jnp.float32)
            put(hidden, span(frame, row), value)
            sums[0:1, :] += jnp.sum(value, axis=0, keepdims=True)

        over_pieces(stem)

    per_group = full // GROUPS
    mean = group_mean(jnp.broadcast_to(sums[0:1, :], (8, full)), per_group, cells)
    variance = group_mean(squares(hidden, mean), per_group, cells)
    scale = lax.rsqrt(variance + EPSILON) * first_gain

    spot = lax.broadcasted_iota(jnp.int32, (1, width, full), 1) + leftmost
    spot = jnp.where(spot < 0, spot + width, spot)
    spot = jnp.where(spot >= width, spot - width, spot)
    zero_row = jnp.zeros((width, full), jnp.bfloat16)
    for e in range(3):
        for frame in range(F):
            acts[e, frame, 0] = zero_row
            acts[e, frame, H + 1] = zero_row
    for frame in range(F):

        def activate(i, _):
            row = i * 2
            place = pl.ds(pl.multiple_of((frame * H + row) * width, 16), 2 * width)
            spread = take(hidden, place, full) - mean
            value = silu(spread * scale + first_shift).reshape(2, width, full)
            left = jnp.where(spot == 0, 0.0, pltpu.roll(value, 1, axis=1))
            right = jnp.where(spot == width - 1, 0.0, pltpu.roll(value, width - 1, axis=1))
            place = pl.ds(row + 1, 2)
            acts[0, frame, place] = left.astype(jnp.bfloat16)
            acts[1, frame, place] = value.astype(jnp.bfloat16)
            acts[2, frame, place] = right.astype(jnp.bfloat16)
            return _

        lax.fori_loop(0, H // 2, activate, 0, unroll=2)

    fetch.wait()
    carries = [
        pltpu.make_async_copy(source, target, next_arrivals.at[at])
        for at, (source, target) in enumerate(
            ((own_far, own_near), (others_far, others_near), (up_far, up_near))
        )
    ]
    for carry in carries:
        carry.start()
    first_bias = small_own[4:5]
    for frame in range(F):

        def convolve(row):
            used = range(max(0, 2 - frame) * 9, 27)
            lhs = jnp.concatenate(
                [
                    acts[tap % 3, frame + tap // 9 - 2, pl.ds(row + tap // 3 % 3, rows)].reshape(
                        rows * width, full
                    )
                    for tap in used
                ],
                axis=1,
            )
            total = times(lhs, weight, used)
            value = (total + first_bias).astype(jnp.bfloat16).astype(jnp.float32)
            put(produced, span(frame, row), value)
            sums[2:3, 0:half] += jnp.sum(value, axis=0, keepdims=True)

        over_pieces(convolve)

    mean = group_mean(jnp.broadcast_to(sums[2:3, 0:half], (8, half)), per_group, cells)
    variance = group_mean(squares(produced, mean), per_group, cells)
    scale = lax.rsqrt(variance + EPSILON) * small_own[5:6]
    second_shift = small_own[6:7]
    for spot_at in range(W_DEV + 2 * HALO):
        value = take(produced, pl.ds(spot_at, F * H, stride=width), half)
        value = silu((value - mean) * scale + second_shift)
        real = (leftmost + spot_at >= 0) & (leftmost + spot_at < width)
        act_out[spot_at] = jnp.where(real, value, 0.0).astype(jnp.bfloat16)
    frames = F // 2
    for spot_at in range(1, W_DEV + 3):
        begin = core * (frames * H * width) + spot_at
        value = take(hidden, pl.ds(begin, frames * H, stride=width), full)
        hidden_out[spot_at - 1] = value.astype(jnp.bfloat16)
    for carry in carries:
        carry.wait()


def second_kernel(
    tile_count,
    act_own,
    act_other,
    hidden_in,
    weight_own,
    weight_other,
    vectors,
    up_weight,
    up_bias,
    out,
    slots,
    taps,
    flat,
):
    width = tile_count * W_DEV
    me = lax.axis_index("tile")
    core = lax.axis_index("chan")
    columns, cells, half = act_own.shape
    full = 2 * half
    frames = F // 2
    rows = frames * H
    inner = columns - 2
    slots[...] = jnp.zeros_like(slots)
    for column in range(columns):
        value = joined(
            act_own[column].astype(jnp.float32), act_other[column].astype(jnp.float32), core
        )
        before = jnp.where(core == 0, 0.0, value[0:rows])
        now = jnp.where(core == 0, value[0:rows], value[rows:])
        for slot in range(frames):
            at = slot * 32 + 8
            slots[column, at : at + H, :] = before[slot * H : (slot + 1) * H]
            at = (slot + frames) * 32 + 8
            slots[column, at : at + H, :] = now[slot * H : (slot + 1) * H]
    for a in range(3):
        for b in range(3):
            parts = []
            for frame in range(frames):
                at = (frame + a) * 32 + 7 + b
                parts.append(slots[:, at : at + H, :])
            taps[3 * a + b] = jnp.concatenate(parts, axis=1).astype(jnp.bfloat16)


    def convolve(weight):
        lhs = jnp.concatenate(
            [
                taps[tap // 3, tap % 3 : tap % 3 + inner].reshape(inner * rows, full)
                for tap in range(27)
            ],
            axis=1,
        )
        return times(lhs, weight, range(27))

    mine = convolve(weight_own)
    theirs = convolve(weight_other)
    second_out = joined(mine, theirs, core) + vectors[3:4]
    hidden = hidden_in[...].astype(jnp.float32) + second_out.reshape(inner, rows, full)
    spot = lax.broadcasted_iota(jnp.int32, (inner, rows, full), 0) + me * W_DEV - 1
    hidden = jnp.where((spot >= 0) & (spot < width), hidden, 0.0).astype(jnp.bfloat16)
    hidden = hidden.reshape(inner * rows, full)

    line = lax.broadcasted_iota(jnp.int32, (inner * frames, H, half), 1)
    upper, lower = [], []
    pad = jnp.zeros((256 - half % 256, full), jnp.bfloat16)
    rhs = jnp.concatenate(
        [part for tap in range(9) for part in (up_weight[tap], pad)], axis=0
    )
    spread = rhs.shape[0] // 9
    every = lax.dot_general(
        hidden, rhs, (((1,), (1,)), ((), ())), preferred_element_type=jnp.float32
    )
    for e in range(3):
        made = []
        for b in range(3):
            at = (3 * b + e) * spread
            made.append(every[:, at : at + half].reshape(inner * frames, H, half))
        above = jnp.where(line == 0, 0.0, pltpu.roll(made[0], 1, axis=1))
        below = jnp.where(line == H - 1, 0.0, pltpu.roll(made[2], H - 1, axis=1))
        upper.append((above + made[1] + made[2]).reshape(inner, frames, H, half))
        lower.append((made[0] + made[1] + below).reshape(inner, frames, H, half))
    bias = up_bias[...]
    span = 2 * W_DEV
    for parity, sums in ((0, upper), (1, lower)):
        for x in range(W_DEV):
            at = x + 1
            for side in range(2):
                if side == 0:
                    value = sums[0][at - 1] + sums[1][at] + sums[2][at]
                else:
                    value = sums[0][at] + sums[1][at] + sums[2][at + 1]
                for frame in range(frames):
                    begin = frame * 2 * H * span + parity * span + 2 * x + side
                    put(flat, pl.ds(begin, H, stride=2 * span), value[frame] + bias)
    out[...] = take(flat, slice(None), out.shape[-1]).astype(jnp.bfloat16).reshape(out.shape)


def exchanged(block, step):
    count = lax.axis_size("tile")
    moved = lax.ppermute(block, "tile", [(i, i ^ step) for i in range(count)])
    return jnp.concatenate([block, moved], axis=0)


def on_device(
    owner_latent,
    tile_counts,
    stem_weight,
    stem_bias,
    first_gain,
    first_shift,
    first_weight,
    first_bias,
    second_gain,
    second_shift,
    second_weight,
    second_bias,
    upsample_weight,
    upsample_bias,
):
    tile_count = lax.axis_size("tile")
    width = tile_count * W_DEV
    _, slot_count, row_length = owner_latent.shape
    zc, half = stem_weight.shape[1], stem_weight.shape[2]
    full = 2 * half
    out_channels = upsample_weight.shape[2]
    first_weight = first_weight.transpose(0, 2, 1)
    second_weight = second_weight.transpose(0, 2, 1)
    upsample_weight = upsample_weight.transpose(0, 2, 1)
    swap = [(0, 1), (1, 0)]
    frames = F // 2

    block_rows = slot_count * row_length // 128
    latents = owner_latent.reshape(1, block_rows, 128)
    small = jnp.stack(
        [
            stem_bias,
            first_gain,
            first_shift,
            second_bias,
            first_bias,
            second_gain,
            second_shift,
            jnp.zeros_like(stem_bias),
        ]
    )
    window = W_DEV + 2 * HALO
    vmem = pl.BlockSpec(memory_space=pltpu.VMEM)
    far = pl.BlockSpec(memory_space=pltpu.HBM)

    def prepare(small, small_other, stem_other, power):
        return pl.pallas_call(
            functools.partial(prepare_kernel, power),
            out_shape=(
                jax.ShapeDtypeStruct((row_length // 128 * 3 * width, PACKED * tile_count), jnp.bfloat16),
                jax.ShapeDtypeStruct((3, 256, full), jnp.bfloat16),
                jax.ShapeDtypeStruct((small.shape[0], full), jnp.float32),
            ),
            in_specs=[far] * 2 + [vmem] * 3,
            out_specs=(vmem,) * 3,
            scratch_shapes=[
                pltpu.SMEM(tile_counts.shape, jnp.int32),
                pltpu.VMEM(stem_weight.shape, jnp.bfloat16),
                pltpu.SemaphoreType.DMA,
                pltpu.SemaphoreType.DMA,
            ],
            cost_estimate=pl.CostEstimate(flops=10**8, bytes_accessed=10**6, transcendentals=0),
            compiler_params=pltpu.CompilerParams(
                vmem_limit_bytes=(6 + 2 * width // 16) * 1024 * 1024
            ),
        )(
            pltpu.with_memory_space_constraint(tile_counts, pltpu.HBM),
            pltpu.with_memory_space_constraint(stem_weight, pltpu.HBM),
            stem_other,
            small,
            small_other,
        )

    stem_other = lax.ppermute(stem_weight, "chan", swap)
    second_other = lax.ppermute(second_weight, "chan", swap)
    power = tile_count & (tile_count - 1) == 0 and tile_count >= 4
    if power:
        away, near = tile_count // 2, tile_count // 4
        pairs = [
            (2 * i + c, 2 * (i ^ (near if c else away)) + c)
            for i in range(tile_count)
            for c in range(2)
        ]
        one = lax.ppermute(latents, ("tile", "chan"), pairs)
        both = [(i, i ^ away ^ near) for i in range(tile_count)]
        two = lax.ppermute(latents, "tile", both)
        small_other = lax.ppermute(small, "chan", swap)
        three = lax.ppermute(one, "chan", swap)
        owners = jnp.concatenate([latents, one, two, three], axis=0)
        owners, small_other, stem_other = lax.optimization_barrier(
            (owners, small_other, stem_other)
        )
        step = near
        while step > 1:
            step //= 2
            owners = exchanged(owners, step)
        prepared = prepare(small, small_other, stem_other, power)
    else:
        small_other = lax.ppermute(small, "chan", swap)
        owners = lax.all_gather(latents, "tile", axis=0, tiled=True)
        prepared = prepare(small, small_other, stem_other, power)
    selection, stem_full, vectors = prepared
    act, hidden, other_near, own_near, up_near = pl.pallas_call(
        first_kernel,
        out_shape=(
            jax.ShapeDtypeStruct((window, F * H, half), jnp.bfloat16),
            jax.ShapeDtypeStruct((window - 2, frames * H, full), jnp.bfloat16),
            jax.ShapeDtypeStruct(second_weight.shape, jnp.bfloat16),
            jax.ShapeDtypeStruct(second_weight.shape, jnp.bfloat16),
            jax.ShapeDtypeStruct(upsample_weight.shape, jnp.bfloat16),
        ),
        in_specs=[vmem] * 5 + [far] * 4,
        out_specs=(vmem,) * 5,
        scratch_shapes=[
            pltpu.VMEM((tile_count, PACKED, 128), jnp.bfloat16),
            pltpu.VMEM((3, F, width, H_PAD * zc), jnp.float32),
            pltpu.VMEM((F, H, width, 256), jnp.bfloat16),
            pltpu.VMEM((full // 128, F * H * width, 128), jnp.float32),
            pltpu.VMEM((3, F, H + 2, width, full), jnp.bfloat16),
            pltpu.VMEM((pl.cdiv(half, 128), F * H * width, 128), jnp.float32),
            pltpu.VMEM((8, full), jnp.float32),
            pltpu.VMEM(first_weight.shape, jnp.bfloat16),
            pltpu.SemaphoreType.DMA,
            pltpu.SemaphoreType.DMA((3,)),
        ],
        cost_estimate=pl.CostEstimate(
            flops=2 * F * H * width * 27 * full * half * 3 // 4,
            bytes_accessed=27 * full * half * 2,
            transcendentals=F * H * width * full,
        ),
        compiler_params=pltpu.CompilerParams(
            vmem_limit_bytes=min(60, 12 + 12 * width // 16) * 1024 * 1024
        ),
    )(
        owners,
        selection,
        stem_full,
        vectors,
        small,
        pltpu.with_memory_space_constraint(first_weight, pltpu.HBM),
        pltpu.with_memory_space_constraint(second_other, pltpu.HBM),
        pltpu.with_memory_space_constraint(second_weight, pltpu.HBM),
        pltpu.with_memory_space_constraint(upsample_weight, pltpu.HBM),
    )

    act_other = lax.ppermute(act, "chan", swap)

    out = pl.pallas_call(
        functools.partial(second_kernel, tile_count),
        out_shape=jax.ShapeDtypeStruct((frames, 2 * H, 2 * W_DEV, out_channels), jnp.bfloat16),
        in_specs=[vmem] * 8,
        out_specs=vmem,
        scratch_shapes=[
            pltpu.VMEM((window, 2 * frames * 32 + 8, full), jnp.float32),
            pltpu.VMEM((9, window, frames * H, full), jnp.bfloat16),
            pltpu.VMEM((pl.cdiv(out_channels, 128), frames * 2 * H * 2 * W_DEV, 128), jnp.float32),
        ],
        cost_estimate=pl.CostEstimate(
            flops=2 * 4 * 48 * 27 * full * full,
            bytes_accessed=2 * 27 * full * half * 2,
            transcendentals=0,
        ),
        compiler_params=pltpu.CompilerParams(vmem_limit_bytes=24 * 1024 * 1024),
    )(
        act,
        act_other,
        hidden,
        own_near,
        other_near,
        vectors,
        up_near,
        upsample_bias.reshape(1, -1),
    )
    return out


def solution(mesh):
    placed = (
        P(("clip", "tile"), None, None),
        P("clip"),
        P(None, None, "chan"),
        P("chan"),
        P("chan"),
        P("chan"),
        P(None, None, "chan"),
        P("chan"),
        P("chan"),
        P("chan"),
        P(None, None, "chan"),
        P("chan"),
        P(),
        P(),
    )

    return jax.shard_map(
        on_device,
        mesh=mesh,
        in_specs=placed,
        out_specs=P(("clip", "chan"), None, "tile", None),
        check_vma=False,
    )
```

```python
import functools

import jax
import jax.numpy as jnp
from jax import lax
from jax.experimental import pallas as pl
from jax.experimental.pallas import tpu as pltpu
from jax.sharding import PartitionSpec as P


GROUPS = 32
F = 4
H = 24
W_DEV = 2
HALO = 2
PACKED = 64
H_PAD = 32
EPSILON = 1e-06


def joined(own, other, core):
    low = jnp.concatenate([own, other], axis=-1)
    high = jnp.concatenate([other, own], axis=-1)
    return jnp.where(core == 0, low, high)


def same_group(channels, per_group):
    row = lax.broadcasted_iota(jnp.int32, (channels, channels), 0).astype(jnp.float32)
    column = lax.broadcasted_iota(jnp.int32, (channels, channels), 1).astype(jnp.float32)
    same = jnp.floor((row + 0.5) / per_group) == jnp.floor((column + 0.5) / per_group)
    return same.astype(jnp.bfloat16)


def group_mean(column_sums, same, per_group, cells):
    channels = column_sums.shape[1]
    high = column_sums.astype(jnp.bfloat16).astype(jnp.float32)
    rest = column_sums - high
    middle = rest.astype(jnp.bfloat16).astype(jnp.float32)
    terms = jnp.concatenate([high, middle, rest - middle], axis=0).astype(jnp.bfloat16)
    totals = jnp.dot(
        terms, same[0:channels, 0:channels], preferred_element_type=jnp.float32
    )
    return (totals[0:1] + totals[8:9] + totals[16:17]) * (1.0 / (cells * per_group))


def put(ref, place, value):
    for block in range(ref.shape[0]):
        part = value[:, block * 128 : (block + 1) * 128]
        ref[block, place, 0 : part.shape[1]] = part


def take(ref, place, channels):
    parts = []
    for block in range(ref.shape[0]):
        parts.append(ref[block, place, :][:, : channels - block * 128])
    return jnp.concatenate(parts, axis=1)


def squares(ref, mean):
    channels = mean.shape[1]
    step = 64

    def add(i, total):
        spread = take(ref, pl.ds(pl.multiple_of(i * step, step), step), channels) - mean
        return total + jnp.sum((spread * spread).reshape(step // 8, 8, channels), axis=0)

    total = lax.fori_loop(
        0, ref.shape[1] // step, add, jnp.zeros((8, channels), jnp.float32), unroll=2
    )
    return jnp.broadcast_to(jnp.sum(total, axis=0, keepdims=True), (8, channels))


def times(lhs, weight, taps):
    rhs = jnp.concatenate([weight[tap] for tap in taps], axis=1)
    return lax.dot_general(lhs, rhs, (((1,), (1,)), ((), ())), preferred_element_type=jnp.float32)


def silu(value):
    half = 0.5 * value
    return half + half * jnp.tanh(half)


def prepare_kernel(
    power,
    counts_far,
    stem_far,
    stem_other,
    small_own,
    small_other,
    selection,
    stem_full,
    vectors,
    same,
    counts,
    stem_own,
    counts_arrival,
    stem_arrival,
):
    counts_fetch = pltpu.make_async_copy(counts_far, counts, counts_arrival)
    counts_fetch.start()
    stem_fetch = pltpu.make_async_copy(stem_far, stem_own, stem_arrival)
    stem_fetch.start()
    tile_count = counts.shape[0]
    width = tile_count * W_DEV
    me = lax.axis_index("tile")
    core = lax.axis_index("chan")
    zc = stem_own.shape[1]
    leftmost = me * W_DEV - HALO

    blocks = selection.shape[0] // (3 * width)
    packed_rows = tile_count * PACKED
    lane = lax.broadcasted_iota(jnp.int32, (8, packed_rows), 1)
    place_at = lane // PACKED
    row_at = lane - place_at * PACKED
    slot_at = jnp.floor((row_at.astype(jnp.float32) + 0.5) * (1.0 / blocks)).astype(jnp.int32)
    held = jnp.full((8, packed_rows), -5, jnp.int32)
    counts_fetch.wait()
    start = jnp.int32(0)
    bits = tile_count.bit_length() - 1
    for owner in range(tile_count):
        place = jnp.int32(owner)
        if power:
            apart = me ^ owner
            far = apart >> (bits - 2)
            place = jnp.where(far == 2, 1 + 2 * core, jnp.where(far == 1, 3 - 2 * core, far))
            place = jnp.where(far == 3, 2, place)
            for bit in range(bits - 2):
                place += ((apart >> bit) & 1) << (bits - 1 - bit)
        count = counts[owner]
        held = jnp.where((place_at == place) & (slot_at < count), start + slot_at, held)
        start = start + count
    code = (held * 16 + row_at - slot_at * blocks)[0:1]
    position = lax.broadcasted_iota(jnp.int32, (3 * width, packed_rows), 0)
    shift = (position >= width).astype(jnp.int32) + (position >= 2 * width).astype(jnp.int32)
    column = position - shift * width + leftmost
    column = jnp.where(column < 0, column + width, column)
    column = jnp.where(column >= width, column - width, column)
    wanted = (column + shift - 1) * 16
    for block in range(blocks):
        rows = slice(block * 3 * width, (block + 1) * 3 * width)
        selection[rows, :] = (wanted + block == code).astype(jnp.bfloat16)

    stem_full[...] = jnp.zeros(stem_full.shape, jnp.bfloat16)
    stem_fetch.wait()
    for tap in range(27):
        a, b, e = tap // 9, tap // 3 % 3, tap % 3
        at = e * 4 * zc + b * zc
        stem_full[a, at : at + zc, :] = joined(stem_own[tap], stem_other[tap], core)
    vectors[...] = joined(small_own[...], small_other[...], core)
    same[...] = same_group(same.shape[0], same.shape[0] // GROUPS)


def first_kernel(
    owners,
    selection,
    stem_full,
    vectors,
    same,
    small_own,
    weight_far,
    others_far,
    own_far,
    up_far,
    act_out,
    hidden_out,
    others_near,
    own_near,
    up_near,
    packed,
    shifted,
    patches,
    hidden,
    acts,
    produced,
    sums,
    weight,
    arrival,
    next_arrivals,
):
    fetch = pltpu.make_async_copy(weight_far, weight, arrival)
    fetch.start()
    tile_count = owners.shape[0]
    width = tile_count * W_DEV
    me = lax.axis_index("tile")
    core = lax.axis_index("chan")
    full, half = vectors.shape[1], small_own.shape[1]
    blocks = selection.shape[0] // (3 * width)
    frame_blocks = blocks // F
    frame_lanes = frame_blocks * 128
    zc = frame_lanes // H
    pieces = max(1, width // 16)
    rows = H // pieces
    cells = F * H * width
    leftmost = me * W_DEV - HALO
    packed[...] = jnp.zeros(packed.shape, jnp.bfloat16)
    packed[:, 0 : owners.shape[1], :] = owners[...]
    every = jnp.dot(
        selection[...],
        packed[...].reshape(tile_count * PACKED, 128),
        preferred_element_type=jnp.float32,
    )
    blank = jnp.zeros((3 * width, shifted.shape[3] - frame_lanes), jnp.float32)
    for frame in range(F):
        parts = []
        for block in range(frame * frame_blocks, (frame + 1) * frame_blocks):
            parts.append(every[block * 3 * width : (block + 1) * 3 * width])
        chosen = pltpu.roll(jnp.concatenate(parts + [blank], axis=1), zc, axis=1)
        shifted[:, frame] = chosen.reshape(3, width, shifted.shape[3])

    stem_bias = vectors[0:1]
    first_gain = vectors[1:2]
    first_shift = vectors[2:3]

    per_block = 128 // zc
    lane128 = lax.broadcasted_iota(jnp.int32, (F, width, 128), 2)
    for row in range(H):
        block = row // per_block * 128
        offset = row % per_block * zc
        window = shifted[:, :, :, block : block + 256]
        one = pltpu.roll(window[0], (256 - offset) % 256, axis=2)[:, :, :128]
        two = pltpu.roll(window[1], (320 - offset) % 256, axis=2)[:, :, :128]
        three = pltpu.roll(window[2], (256 - offset) % 256, axis=2)[:, :, :128]
        patches[:, row, :, 0:128] = jnp.where(lane128 < 64, one, two).astype(jnp.bfloat16)
        patches[:, row, :, 128:256] = three.astype(jnp.bfloat16)

    def over_pieces(body):
        if pieces == 1:
            body(0)
        else:
            lax.fori_loop(0, pieces, lambda i, _: (body(i * rows), 0)[1], 0)

    def span(frame, row):
        return pl.ds(pl.multiple_of((frame * H + row) * width, 16), rows * width)

    sums[...] = jnp.zeros_like(sums)
    for frame in range(F):

        def stem(row):
            total = jnp.zeros((rows * width, full), jnp.float32)
            for a in range(max(0, 2 - frame), 3):
                lhs = patches[frame + a - 2, pl.ds(row, rows)].reshape(rows * width, 256)
                total += jnp.dot(lhs, stem_full[a], preferred_element_type=jnp.float32)
            value = (total + stem_bias).astype(jnp.bfloat16).astype(jnp.float32)
            put(hidden, span(frame, row), value)
            sums[0:1, :] += jnp.sum(value, axis=0, keepdims=True)

        over_pieces(stem)

    per_group = full // GROUPS
    mean = group_mean(jnp.broadcast_to(sums[0:1, :], (8, full)), same, per_group, cells)
    variance = group_mean(squares(hidden, mean), same, per_group, cells)
    scale = lax.rsqrt(variance + EPSILON) * first_gain

    spot = lax.broadcasted_iota(jnp.int32, (1, width, full), 1) + leftmost
    spot = jnp.where(spot < 0, spot + width, spot)
    spot = jnp.where(spot >= width, spot - width, spot)
    zero_row = jnp.zeros((width, full), jnp.bfloat16)
    for e in range(3):
        for frame in range(F):
            acts[e, frame, 0] = zero_row
            acts[e, frame, H + 1] = zero_row
    for frame in range(F):

        def activate(i, _):
            row = i * 2
            place = pl.ds(pl.multiple_of((frame * H + row) * width, 16), 2 * width)
            spread = take(hidden, place, full) - mean
            value = silu(spread * scale + first_shift).reshape(2, width, full)
            left = jnp.where(spot == 0, 0.0, pltpu.roll(value, 1, axis=1))
            right = jnp.where(spot == width - 1, 0.0, pltpu.roll(value, width - 1, axis=1))
            place = pl.ds(row + 1, 2)
            acts[0, frame, place] = left.astype(jnp.bfloat16)
            acts[1, frame, place] = value.astype(jnp.bfloat16)
            acts[2, frame, place] = right.astype(jnp.bfloat16)
            return _

        lax.fori_loop(0, H // 2, activate, 0, unroll=2)

    fetch.wait()
    carries = [
        pltpu.make_async_copy(source, target, next_arrivals.at[at])
        for at, (source, target) in enumerate(
            ((own_far, own_near), (others_far, others_near), (up_far, up_near))
        )
    ]
    for carry in carries:
        carry.start()
    first_bias = small_own[4:5]
    for frame in range(F):

        def convolve(row):
            used = range(max(0, 2 - frame) * 9, 27)
            lhs = jnp.concatenate(
                [
                    acts[tap % 3, frame + tap // 9 - 2, pl.ds(row + tap // 3 % 3, rows)].reshape(
                        rows * width, full
                    )
                    for tap in used
                ],
                axis=1,
            )
            total = times(lhs, weight, used)
            value = (total + first_bias).astype(jnp.bfloat16).astype(jnp.float32)
            put(produced, span(frame, row), value)
            sums[2:3, 0:half] += jnp.sum(value, axis=0, keepdims=True)

        over_pieces(convolve)

    mean = group_mean(
        jnp.broadcast_to(sums[2:3, 0:half], (8, half)), same, per_group, cells
    )
    variance = group_mean(squares(produced, mean), same, per_group, cells)
    scale = lax.rsqrt(variance + EPSILON) * small_own[5:6]
    second_shift = small_own[6:7]
    for spot_at in range(W_DEV + 2 * HALO):
        value = take(produced, pl.ds(spot_at, F * H, stride=width), half)
        value = silu((value - mean) * scale + second_shift)
        real = (leftmost + spot_at >= 0) & (leftmost + spot_at < width)
        act_out[spot_at] = jnp.where(real, value, 0.0).astype(jnp.bfloat16)
    frames = F // 2
    for spot_at in range(1, W_DEV + 3):
        begin = core * (frames * H * width) + spot_at
        value = take(hidden, pl.ds(begin, frames * H, stride=width), full)
        hidden_out[spot_at - 1] = value.astype(jnp.bfloat16)
    for carry in carries:
        carry.wait()


def second_kernel(
    tile_count,
    act_own,
    act_other,
    hidden_in,
    weight_own,
    weight_other,
    vectors,
    up_weight,
    up_bias,
    out,
    slots,
    taps,
    flat,
):
    width = tile_count * W_DEV
    me = lax.axis_index("tile")
    core = lax.axis_index("chan")
    columns, cells, half = act_own.shape
    full = 2 * half
    frames = F // 2
    rows = frames * H
    inner = columns - 2
    slots[...] = jnp.zeros_like(slots)
    for column in range(columns):
        value = joined(
            act_own[column].astype(jnp.float32), act_other[column].astype(jnp.float32), core
        )
        before = jnp.where(core == 0, 0.0, value[0:rows])
        now = jnp.where(core == 0, value[0:rows], value[rows:])
        for slot in range(frames):
            at = slot * 32 + 8
            slots[column, at : at + H, :] = before[slot * H : (slot + 1) * H]
            at = (slot + frames) * 32 + 8
            slots[column, at : at + H, :] = now[slot * H : (slot + 1) * H]
    for a in range(3):
        for b in range(3):
            parts = []
            for frame in range(frames):
                at = (frame + a) * 32 + 7 + b
                parts.append(slots[:, at : at + H, :])
            taps[3 * a + b] = jnp.concatenate(parts, axis=1).astype(jnp.bfloat16)


    def convolve(weight):
        lhs = jnp.concatenate(
            [
                taps[tap // 3, tap % 3 : tap % 3 + inner].reshape(inner * rows, full)
                for tap in range(27)
            ],
            axis=1,
        )
        return times(lhs, weight, range(27))

    mine = convolve(weight_own)
    theirs = convolve(weight_other)
    second_out = joined(mine, theirs, core) + vectors[3:4]
    hidden = hidden_in[...].astype(jnp.float32) + second_out.reshape(inner, rows, full)
    spot = lax.broadcasted_iota(jnp.int32, (inner, rows, full), 0) + me * W_DEV - 1
    hidden = jnp.where((spot >= 0) & (spot < width), hidden, 0.0).astype(jnp.bfloat16)
    hidden = hidden.reshape(inner * rows, full)

    line = lax.broadcasted_iota(jnp.int32, (inner * frames, H, half), 1)
    upper, lower = [], []
    pad = jnp.zeros((256 - half % 256, full), jnp.bfloat16)
    rhs = jnp.concatenate(
        [part for tap in range(9) for part in (up_weight[tap], pad)], axis=0
    )
    spread = rhs.shape[0] // 9
    every = lax.dot_general(
        hidden, rhs, (((1,), (1,)), ((), ())), preferred_element_type=jnp.float32
    )
    for e in range(3):
        made = []
        for b in range(3):
            at = (3 * b + e) * spread
            made.append(every[:, at : at + half].reshape(inner * frames, H, half))
        above = jnp.where(line == 0, 0.0, pltpu.roll(made[0], 1, axis=1))
        below = jnp.where(line == H - 1, 0.0, pltpu.roll(made[2], H - 1, axis=1))
        upper.append((above + made[1] + made[2]).reshape(inner, frames, H, half))
        lower.append((made[0] + made[1] + below).reshape(inner, frames, H, half))
    bias = up_bias[...]
    span = 2 * W_DEV
    for parity, sums in ((0, upper), (1, lower)):
        for x in range(W_DEV):
            at = x + 1
            for side in range(2):
                if side == 0:
                    value = sums[0][at - 1] + sums[1][at] + sums[2][at]
                else:
                    value = sums[0][at] + sums[1][at] + sums[2][at + 1]
                for frame in range(frames):
                    begin = frame * 2 * H * span + parity * span + 2 * x + side
                    put(flat, pl.ds(begin, H, stride=2 * span), value[frame] + bias)
    out[...] = take(flat, slice(None), out.shape[-1]).astype(jnp.bfloat16).reshape(out.shape)


def exchanged(block, step):
    count = lax.axis_size("tile")
    moved = lax.ppermute(block, "tile", [(i, i ^ step) for i in range(count)])
    return jnp.concatenate([block, moved], axis=0)


def on_device(
    owner_latent,
    tile_counts,
    stem_weight,
    stem_bias,
    first_gain,
    first_shift,
    first_weight,
    first_bias,
    second_gain,
    second_shift,
    second_weight,
    second_bias,
    upsample_weight,
    upsample_bias,
):
    tile_count = lax.axis_size("tile")
    width = tile_count * W_DEV
    _, slot_count, row_length = owner_latent.shape
    zc, half = stem_weight.shape[1], stem_weight.shape[2]
    full = 2 * half
    out_channels = upsample_weight.shape[2]
    first_weight = first_weight.transpose(0, 2, 1)
    second_weight = second_weight.transpose(0, 2, 1)
    upsample_weight = upsample_weight.transpose(0, 2, 1)
    swap = [(0, 1), (1, 0)]
    frames = F // 2

    block_rows = slot_count * row_length // 128
    latents = owner_latent.reshape(1, block_rows, 128)
    small = jnp.stack(
        [
            stem_bias,
            first_gain,
            first_shift,
            second_bias,
            first_bias,
            second_gain,
            second_shift,
            jnp.zeros_like(stem_bias),
        ]
    )
    window = W_DEV + 2 * HALO
    vmem = pl.BlockSpec(memory_space=pltpu.VMEM)
    far = pl.BlockSpec(memory_space=pltpu.HBM)

    def prepare(small, small_other, stem_other, power):
        return pl.pallas_call(
            functools.partial(prepare_kernel, power),
            out_shape=(
                jax.ShapeDtypeStruct((row_length // 128 * 3 * width, PACKED * tile_count), jnp.bfloat16),
                jax.ShapeDtypeStruct((3, 256, full), jnp.bfloat16),
                jax.ShapeDtypeStruct((small.shape[0], full), jnp.float32),
                jax.ShapeDtypeStruct((full, full), jnp.bfloat16),
            ),
            in_specs=[far] * 2 + [vmem] * 3,
            out_specs=(vmem,) * 4,
            scratch_shapes=[
                pltpu.SMEM(tile_counts.shape, jnp.int32),
                pltpu.VMEM(stem_weight.shape, jnp.bfloat16),
                pltpu.SemaphoreType.DMA,
                pltpu.SemaphoreType.DMA,
            ],
            cost_estimate=pl.CostEstimate(flops=10**8, bytes_accessed=10**6, transcendentals=0),
            compiler_params=pltpu.CompilerParams(
                vmem_limit_bytes=(6 + 2 * width // 16) * 1024 * 1024
            ),
        )(
            pltpu.with_memory_space_constraint(tile_counts, pltpu.HBM),
            pltpu.with_memory_space_constraint(stem_weight, pltpu.HBM),
            stem_other,
            small,
            small_other,
        )

    stem_other = lax.ppermute(stem_weight, "chan", swap)
    second_other = lax.ppermute(second_weight, "chan", swap)
    power = tile_count & (tile_count - 1) == 0 and tile_count >= 4
    if power:
        away, near = tile_count // 2, tile_count // 4
        pairs = [
            (2 * i + c, 2 * (i ^ (near if c else away)) + c)
            for i in range(tile_count)
            for c in range(2)
        ]
        one = lax.ppermute(latents, ("tile", "chan"), pairs)
        both = [(i, i ^ away ^ near) for i in range(tile_count)]
        two = lax.ppermute(latents, "tile", both)
        small_other = lax.ppermute(small, "chan", swap)
        three = lax.ppermute(one, "chan", swap)
        owners = jnp.concatenate([latents, one, two, three], axis=0)
        owners, small_other, stem_other = lax.optimization_barrier(
            (owners, small_other, stem_other)
        )
        step = near
        while step > 1:
            step //= 2
            owners = exchanged(owners, step)
        prepared = prepare(small, small_other, stem_other, power)
    else:
        small_other = lax.ppermute(small, "chan", swap)
        owners = lax.all_gather(latents, "tile", axis=0, tiled=True)
        prepared = prepare(small, small_other, stem_other, power)
    selection, stem_full, vectors, same = prepared
    act, hidden, other_near, own_near, up_near = pl.pallas_call(
        first_kernel,
        out_shape=(
            jax.ShapeDtypeStruct((window, F * H, half), jnp.bfloat16),
            jax.ShapeDtypeStruct((window - 2, frames * H, full), jnp.bfloat16),
            jax.ShapeDtypeStruct(second_weight.shape, jnp.bfloat16),
            jax.ShapeDtypeStruct(second_weight.shape, jnp.bfloat16),
            jax.ShapeDtypeStruct(upsample_weight.shape, jnp.bfloat16),
        ),
        in_specs=[vmem] * 6 + [far] * 4,
        out_specs=(vmem,) * 5,
        scratch_shapes=[
            pltpu.VMEM((tile_count, PACKED, 128), jnp.bfloat16),
            pltpu.VMEM((3, F, width, H_PAD * zc), jnp.float32),
            pltpu.VMEM((F, H, width, 256), jnp.bfloat16),
            pltpu.VMEM((full // 128, F * H * width, 128), jnp.float32),
            pltpu.VMEM((3, F, H + 2, width, full), jnp.bfloat16),
            pltpu.VMEM((pl.cdiv(half, 128), F * H * width, 128), jnp.float32),
            pltpu.VMEM((8, full), jnp.float32),
            pltpu.VMEM(first_weight.shape, jnp.bfloat16),
            pltpu.SemaphoreType.DMA,
            pltpu.SemaphoreType.DMA((3,)),
        ],
        cost_estimate=pl.CostEstimate(
            flops=2 * F * H * width * 27 * full * half * 3 // 4,
            bytes_accessed=27 * full * half * 2,
            transcendentals=F * H * width * full,
        ),
        compiler_params=pltpu.CompilerParams(
            vmem_limit_bytes=min(60, 12 + 12 * width // 16) * 1024 * 1024
        ),
    )(
        owners,
        selection,
        stem_full,
        vectors,
        same,
        small,
        pltpu.with_memory_space_constraint(first_weight, pltpu.HBM),
        pltpu.with_memory_space_constraint(second_other, pltpu.HBM),
        pltpu.with_memory_space_constraint(second_weight, pltpu.HBM),
        pltpu.with_memory_space_constraint(upsample_weight, pltpu.HBM),
    )

    act_other = lax.ppermute(act, "chan", swap)

    out = pl.pallas_call(
        functools.partial(second_kernel, tile_count),
        out_shape=jax.ShapeDtypeStruct((frames, 2 * H, 2 * W_DEV, out_channels), jnp.bfloat16),
        in_specs=[vmem] * 8,
        out_specs=vmem,
        scratch_shapes=[
            pltpu.VMEM((window, 2 * frames * 32 + 8, full), jnp.float32),
            pltpu.VMEM((9, window, frames * H, full), jnp.bfloat16),
            pltpu.VMEM((pl.cdiv(out_channels, 128), frames * 2 * H * 2 * W_DEV, 128), jnp.float32),
        ],
        cost_estimate=pl.CostEstimate(
            flops=2 * 4 * 48 * 27 * full * full,
            bytes_accessed=2 * 27 * full * half * 2,
            transcendentals=0,
        ),
        compiler_params=pltpu.CompilerParams(vmem_limit_bytes=24 * 1024 * 1024),
    )(
        act,
        act_other,
        hidden,
        own_near,
        other_near,
        vectors,
        up_near,
        upsample_bias.reshape(1, -1),
    )
    return out


def solution(mesh):
    placed = (
        P(("clip", "tile"), None, None),
        P("clip"),
        P(None, None, "chan"),
        P("chan"),
        P("chan"),
        P("chan"),
        P(None, None, "chan"),
        P("chan"),
        P("chan"),
        P("chan"),
        P(None, None, "chan"),
        P("chan"),
        P(),
        P(),
    )

    return jax.shard_map(
        on_device,
        mesh=mesh,
        in_specs=placed,
        out_specs=P(("clip", "chan"), None, "tile", None),
        check_vma=False,
    )
```

```python
import functools

import jax
import jax.numpy as jnp
from jax import lax
from jax.experimental import pallas as pl
from jax.experimental.pallas import tpu as pltpu
from jax.sharding import PartitionSpec as P


GROUPS = 32
F = 4
H = 24
W_DEV = 2
HALO = 2
PACKED = 64
H_PAD = 32
EPSILON = 1e-06


def joined(own, other, core):
    low = jnp.concatenate([own, other], axis=-1)
    high = jnp.concatenate([other, own], axis=-1)
    return jnp.where(core == 0, low, high)


def same_group(channels, per_group):
    row = lax.broadcasted_iota(jnp.int32, (channels, channels), 0).astype(jnp.float32)
    column = lax.broadcasted_iota(jnp.int32, (channels, channels), 1).astype(jnp.float32)
    same = jnp.floor((row + 0.5) / per_group) == jnp.floor((column + 0.5) / per_group)
    return same.astype(jnp.bfloat16)


def group_mean(column_sums, same, per_group, cells):
    channels = column_sums.shape[1]
    high = column_sums.astype(jnp.bfloat16).astype(jnp.float32)
    rest = column_sums - high
    middle = rest.astype(jnp.bfloat16).astype(jnp.float32)
    terms = jnp.concatenate([high, middle, rest - middle], axis=0).astype(jnp.bfloat16)
    totals = jnp.dot(
        terms, same[0:channels, 0:channels], preferred_element_type=jnp.float32
    )
    return (totals[0:1] + totals[8:9] + totals[16:17]) * (1.0 / (cells * per_group))


def put(ref, place, value):
    for block in range(ref.shape[0]):
        part = value[:, block * 128 : (block + 1) * 128]
        ref[block, place, 0 : part.shape[1]] = part


def take(ref, place, channels):
    parts = []
    for block in range(ref.shape[0]):
        parts.append(ref[block, place, :][:, : channels - block * 128])
    return jnp.concatenate(parts, axis=1)


def squares(ref, mean):
    channels = mean.shape[1]
    step = 64

    def add(i, total):
        spread = take(ref, pl.ds(pl.multiple_of(i * step, step), step), channels) - mean
        return total + jnp.sum((spread * spread).reshape(step // 8, 8, channels), axis=0)

    total = lax.fori_loop(
        0, ref.shape[1] // step, add, jnp.zeros((8, channels), jnp.float32), unroll=8
    )
    return jnp.broadcast_to(jnp.sum(total, axis=0, keepdims=True), (8, channels))


def times(lhs, weight, taps):
    rhs = jnp.concatenate([weight[tap] for tap in taps], axis=1)
    return lax.dot_general(lhs, rhs, (((1,), (1,)), ((), ())), preferred_element_type=jnp.float32)


def silu(value):
    half = 0.5 * value
    return half + half * jnp.tanh(half)


def prepare_kernel(
    power,
    counts_far,
    stem_far,
    stem_other,
    small_own,
    small_other,
    selection,
    stem_full,
    vectors,
    same,
    counts,
    stem_own,
    counts_arrival,
    stem_arrival,
):
    counts_fetch = pltpu.make_async_copy(counts_far, counts, counts_arrival)
    counts_fetch.start()
    stem_fetch = pltpu.make_async_copy(stem_far, stem_own, stem_arrival)
    stem_fetch.start()
    tile_count = counts.shape[0]
    width = tile_count * W_DEV
    me = lax.axis_index("tile")
    core = lax.axis_index("chan")
    zc = stem_own.shape[1]
    leftmost = me * W_DEV - HALO

    blocks = selection.shape[0] // (3 * width)
    packed_rows = tile_count * PACKED
    lane = lax.broadcasted_iota(jnp.int32, (8, packed_rows), 1)
    place_at = lane // PACKED
    row_at = lane - place_at * PACKED
    slot_at = jnp.floor((row_at.astype(jnp.float32) + 0.5) * (1.0 / blocks)).astype(jnp.int32)
    held = jnp.full((8, packed_rows), -5, jnp.int32)
    counts_fetch.wait()
    start = jnp.int32(0)
    bits = tile_count.bit_length() - 1
    for owner in range(tile_count):
        place = jnp.int32(owner)
        if power:
            apart = me ^ owner
            far = apart >> (bits - 2)
            place = jnp.where(far == 2, 1 + 2 * core, jnp.where(far == 1, 3 - 2 * core, far))
            place = jnp.where(far == 3, 2, place)
            for bit in range(bits - 2):
                place += ((apart >> bit) & 1) << (bits - 1 - bit)
        count = counts[owner]
        held = jnp.where((place_at == place) & (slot_at < count), start + slot_at, held)
        start = start + count
    code = (held * 16 + row_at - slot_at * blocks)[0:1]
    position = lax.broadcasted_iota(jnp.int32, (3 * width, packed_rows), 0)
    shift = (position >= width).astype(jnp.int32) + (position >= 2 * width).astype(jnp.int32)
    column = position - shift * width + leftmost
    column = jnp.where(column < 0, column + width, column)
    column = jnp.where(column >= width, column - width, column)
    wanted = (column + shift - 1) * 16
    for block in range(blocks):
        rows = slice(block * 3 * width, (block + 1) * 3 * width)
        selection[rows, :] = (wanted + block == code).astype(jnp.bfloat16)

    stem_full[...] = jnp.zeros(stem_full.shape, jnp.bfloat16)
    stem_fetch.wait()
    for tap in range(27):
        a, b, e = tap // 9, tap // 3 % 3, tap % 3
        at = e * 4 * zc + b * zc
        stem_full[a, at : at + zc, :] = joined(stem_own[tap], stem_other[tap], core)
    vectors[...] = joined(small_own[...], small_other[...], core)
    same[...] = same_group(same.shape[0], same.shape[0] // GROUPS)


def first_kernel(
    owners,
    selection,
    stem_full,
    vectors,
    same,
    small_own,
    weight_far,
    others_far,
    own_far,
    up_far,
    act_out,
    hidden_out,
    others_near,
    own_near,
    up_near,
    packed,
    shifted,
    patches,
    hidden,
    acts,
    produced,
    sums,
    weight,
    arrival,
    next_arrivals,
):
    fetch = pltpu.make_async_copy(weight_far, weight, arrival)
    fetch.start()
    tile_count = owners.shape[0]
    width = tile_count * W_DEV
    me = lax.axis_index("tile")
    core = lax.axis_index("chan")
    full, half = vectors.shape[1], small_own.shape[1]
    blocks = selection.shape[0] // (3 * width)
    frame_blocks = blocks // F
    frame_lanes = frame_blocks * 128
    zc = frame_lanes // H
    pieces = max(1, width // 16)
    rows = H // pieces
    cells = F * H * width
    leftmost = me * W_DEV - HALO
    packed[...] = jnp.zeros(packed.shape, jnp.bfloat16)
    packed[:, 0 : owners.shape[1], :] = owners[...]
    every = jnp.dot(
        selection[...],
        packed[...].reshape(tile_count * PACKED, 128),
        preferred_element_type=jnp.float32,
    )
    blank = jnp.zeros((3 * width, shifted.shape[3] - frame_lanes), jnp.float32)
    for frame in range(F):
        parts = []
        for block in range(frame * frame_blocks, (frame + 1) * frame_blocks):
            parts.append(every[block * 3 * width : (block + 1) * 3 * width])
        chosen = pltpu.roll(jnp.concatenate(parts + [blank], axis=1), zc, axis=1)
        shifted[:, frame] = chosen.reshape(3, width, shifted.shape[3])

    stem_bias = vectors[0:1]
    first_gain = vectors[1:2]
    first_shift = vectors[2:3]

    per_block = 128 // zc
    lane128 = lax.broadcasted_iota(jnp.int32, (F, width, 128), 2)
    for row in range(H):
        block = row // per_block * 128
        offset = row % per_block * zc
        window = shifted[:, :, :, block : block + 256]
        one = pltpu.roll(window[0], (256 - offset) % 256, axis=2)[:, :, :128]
        two = pltpu.roll(window[1], (320 - offset) % 256, axis=2)[:, :, :128]
        three = pltpu.roll(window[2], (256 - offset) % 256, axis=2)[:, :, :128]
        patches[:, row, :, 0:128] = jnp.where(lane128 < 64, one, two).astype(jnp.bfloat16)
        patches[:, row, :, 128:256] = three.astype(jnp.bfloat16)

    def over_pieces(body):
        if pieces == 1:
            body(0)
        else:
            lax.fori_loop(0, pieces, lambda i, _: (body(i * rows), 0)[1], 0)

    def span(frame, row):
        return pl.ds(pl.multiple_of((frame * H + row) * width, 16), rows * width)

    sums[...] = jnp.zeros_like(sums)
    for frame in range(F):

        def stem(row):
            total = jnp.zeros((rows * width, full), jnp.float32)
            for a in range(max(0, 2 - frame), 3):
                lhs = patches[frame + a - 2, pl.ds(row, rows)].reshape(rows * width, 256)
                total += jnp.dot(lhs, stem_full[a], preferred_element_type=jnp.float32)
            value = (total + stem_bias).astype(jnp.bfloat16).astype(jnp.float32)
            put(hidden, span(frame, row), value)
            sums[0:1, :] += jnp.sum(value, axis=0, keepdims=True)

        over_pieces(stem)

    per_group = full // GROUPS
    mean = group_mean(jnp.broadcast_to(sums[0:1, :], (8, full)), same, per_group, cells)
    variance = group_mean(squares(hidden, mean), same, per_group, cells)
    scale = lax.rsqrt(variance + EPSILON) * first_gain

    spot = lax.broadcasted_iota(jnp.int32, (1, width, full), 1) + leftmost
    spot = jnp.where(spot < 0, spot + width, spot)
    spot = jnp.where(spot >= width, spot - width, spot)
    zero_row = jnp.zeros((width, full), jnp.bfloat16)
    for e in range(3):
        for frame in range(F):
            acts[e, frame, 0] = zero_row
            acts[e, frame, H + 1] = zero_row
    for frame in range(F):

        def activate(i, _):
            row = i * 2
            place = pl.ds(pl.multiple_of((frame * H + row) * width, 16), 2 * width)
            spread = take(hidden, place, full) - mean
            value = silu(spread * scale + first_shift).reshape(2, width, full)
            left = jnp.where(spot == 0, 0.0, pltpu.roll(value, 1, axis=1))
            right = jnp.where(spot == width - 1, 0.0, pltpu.roll(value, width - 1, axis=1))
            place = pl.ds(row + 1, 2)
            acts[0, frame, place] = left.astype(jnp.bfloat16)
            acts[1, frame, place] = value.astype(jnp.bfloat16)
            acts[2, frame, place] = right.astype(jnp.bfloat16)
            return _

        lax.fori_loop(0, H // 2, activate, 0, unroll=3)

    fetch.wait()
    carries = [
        pltpu.make_async_copy(source, target, next_arrivals.at[at])
        for at, (source, target) in enumerate(
            ((own_far, own_near), (others_far, others_near), (up_far, up_near))
        )
    ]
    for carry in carries:
        carry.start()
    first_bias = small_own[4:5]
    together = (tuple(range(2, F)), (1,), (0,))
    for group in together if pieces == 1 else [(frame,) for frame in range(F)]:

        def convolve(row):
            used = range(max(0, 2 - group[0]) * 9, 27)
            lhs = jnp.concatenate(
                [
                    jnp.concatenate(
                        [
                            acts[
                                tap % 3, frame + tap // 9 - 2, pl.ds(row + tap // 3 % 3, rows)
                            ].reshape(rows * width, full)
                            for frame in group
                        ],
                        axis=0,
                    )
                    for tap in used
                ],
                axis=1,
            )
            total = times(lhs, weight, used)
            value = (total + first_bias).astype(jnp.bfloat16).astype(jnp.float32)
            for at, frame in enumerate(group):
                part = value[at * rows * width : (at + 1) * rows * width]
                put(produced, span(frame, row), part)
            sums[2:3, 0:half] += jnp.sum(value, axis=0, keepdims=True)

        over_pieces(convolve)

    mean = group_mean(
        jnp.broadcast_to(sums[2:3, 0:half], (8, half)), same, per_group, cells
    )
    variance = group_mean(squares(produced, mean), same, per_group, cells)
    scale = lax.rsqrt(variance + EPSILON) * small_own[5:6]
    second_shift = small_own[6:7]
    for spot_at in range(W_DEV + 2 * HALO):
        value = take(produced, pl.ds(spot_at, F * H, stride=width), half)
        value = silu((value - mean) * scale + second_shift)
        real = (leftmost + spot_at >= 0) & (leftmost + spot_at < width)
        act_out[spot_at] = jnp.where(real, value, 0.0).astype(jnp.bfloat16)
    frames = F // 2
    for spot_at in range(1, W_DEV + 3):
        begin = core * (frames * H * width) + spot_at
        value = take(hidden, pl.ds(begin, frames * H, stride=width), full)
        hidden_out[spot_at - 1] = value.astype(jnp.bfloat16)
    for carry in carries:
        carry.wait()


def second_kernel(
    tile_count,
    act_own,
    act_other,
    hidden_in,
    weight_own,
    weight_other,
    vectors,
    up_weight,
    up_bias,
    out,
    slots,
    taps,
    flat,
):
    width = tile_count * W_DEV
    me = lax.axis_index("tile")
    core = lax.axis_index("chan")
    columns, cells, half = act_own.shape
    full = 2 * half
    frames = F // 2
    rows = frames * H
    inner = columns - 2
    slots[...] = jnp.zeros_like(slots)
    for column in range(columns):
        value = joined(
            act_own[column].astype(jnp.float32), act_other[column].astype(jnp.float32), core
        )
        before = jnp.where(core == 0, 0.0, value[0:rows])
        now = jnp.where(core == 0, value[0:rows], value[rows:])
        for slot in range(frames):
            at = slot * 32 + 8
            slots[column, at : at + H, :] = before[slot * H : (slot + 1) * H]
            at = (slot + frames) * 32 + 8
            slots[column, at : at + H, :] = now[slot * H : (slot + 1) * H]
    for a in range(3):
        for b in range(3):
            parts = []
            for frame in range(frames):
                at = (frame + a) * 32 + 7 + b
                parts.append(slots[:, at : at + H, :])
            taps[3 * a + b] = jnp.concatenate(parts, axis=1).astype(jnp.bfloat16)


    def convolve(weight):
        lhs = jnp.concatenate(
            [
                taps[tap // 3, tap % 3 : tap % 3 + inner].reshape(inner * rows, full)
                for tap in range(27)
            ],
            axis=1,
        )
        return times(lhs, weight, range(27))

    mine = convolve(weight_own)
    theirs = convolve(weight_other)
    second_out = joined(mine, theirs, core) + vectors[3:4]
    hidden = hidden_in[...].astype(jnp.float32) + second_out.reshape(inner, rows, full)
    spot = lax.broadcasted_iota(jnp.int32, (inner, rows, full), 0) + me * W_DEV - 1
    hidden = jnp.where((spot >= 0) & (spot < width), hidden, 0.0).astype(jnp.bfloat16)
    hidden = hidden.reshape(inner * rows, full)

    line = lax.broadcasted_iota(jnp.int32, (inner * frames, H, half), 1)
    upper, lower = [], []
    pad = jnp.zeros((256 - half % 256, full), jnp.bfloat16)
    rhs = jnp.concatenate(
        [part for tap in range(9) for part in (up_weight[tap], pad)], axis=0
    )
    spread = rhs.shape[0] // 9
    every = lax.dot_general(
        hidden, rhs, (((1,), (1,)), ((), ())), preferred_element_type=jnp.float32
    )
    for e in range(3):
        made = []
        for b in range(3):
            at = (3 * b + e) * spread
            made.append(every[:, at : at + half].reshape(inner * frames, H, half))
        above = jnp.where(line == 0, 0.0, pltpu.roll(made[0], 1, axis=1))
        below = jnp.where(line == H - 1, 0.0, pltpu.roll(made[2], H - 1, axis=1))
        upper.append((above + made[1] + made[2]).reshape(inner, frames, H, half))
        lower.append((made[0] + made[1] + below).reshape(inner, frames, H, half))
    bias = up_bias[...]
    span = 2 * W_DEV
    for parity, sums in ((0, upper), (1, lower)):
        for x in range(W_DEV):
            at = x + 1
            for side in range(2):
                if side == 0:
                    value = sums[0][at - 1] + sums[1][at] + sums[2][at]
                else:
                    value = sums[0][at] + sums[1][at] + sums[2][at + 1]
                for frame in range(frames):
                    begin = frame * 2 * H * span + parity * span + 2 * x + side
                    put(flat, pl.ds(begin, H, stride=2 * span), value[frame] + bias)
    out[...] = take(flat, slice(None), out.shape[-1]).astype(jnp.bfloat16).reshape(out.shape)


def exchanged(block, step):
    count = lax.axis_size("tile")
    moved = lax.ppermute(block, "tile", [(i, i ^ step) for i in range(count)])
    return jnp.concatenate([block, moved], axis=0)


def on_device(
    owner_latent,
    tile_counts,
    stem_weight,
    stem_bias,
    first_gain,
    first_shift,
    first_weight,
    first_bias,
    second_gain,
    second_shift,
    second_weight,
    second_bias,
    upsample_weight,
    upsample_bias,
):
    tile_count = lax.axis_size("tile")
    width = tile_count * W_DEV
    _, slot_count, row_length = owner_latent.shape
    zc, half = stem_weight.shape[1], stem_weight.shape[2]
    full = 2 * half
    out_channels = upsample_weight.shape[2]
    first_weight = first_weight.transpose(0, 2, 1)
    second_weight = second_weight.transpose(0, 2, 1)
    upsample_weight = upsample_weight.transpose(0, 2, 1)
    swap = [(0, 1), (1, 0)]
    frames = F // 2

    block_rows = slot_count * row_length // 128
    latents = owner_latent.reshape(1, block_rows, 128)
    small = jnp.stack(
        [
            stem_bias,
            first_gain,
            first_shift,
            second_bias,
            first_bias,
            second_gain,
            second_shift,
            jnp.zeros_like(stem_bias),
        ]
    )
    window = W_DEV + 2 * HALO
    vmem = pl.BlockSpec(memory_space=pltpu.VMEM)
    far = pl.BlockSpec(memory_space=pltpu.HBM)

    def prepare(small, small_other, stem_other, power):
        return pl.pallas_call(
            functools.partial(prepare_kernel, power),
            out_shape=(
                jax.ShapeDtypeStruct((row_length // 128 * 3 * width, PACKED * tile_count), jnp.bfloat16),
                jax.ShapeDtypeStruct((3, 256, full), jnp.bfloat16),
                jax.ShapeDtypeStruct((small.shape[0], full), jnp.float32),
                jax.ShapeDtypeStruct((full, full), jnp.bfloat16),
            ),
            in_specs=[far] * 2 + [vmem] * 3,
            out_specs=(vmem,) * 4,
            scratch_shapes=[
                pltpu.SMEM(tile_counts.shape, jnp.int32),
                pltpu.VMEM(stem_weight.shape, jnp.bfloat16),
                pltpu.SemaphoreType.DMA,
                pltpu.SemaphoreType.DMA,
            ],
            cost_estimate=pl.CostEstimate(flops=10**8, bytes_accessed=10**6, transcendentals=0),
            compiler_params=pltpu.CompilerParams(
                vmem_limit_bytes=(6 + 2 * width // 16) * 1024 * 1024
            ),
        )(
            pltpu.with_memory_space_constraint(tile_counts, pltpu.HBM),
            pltpu.with_memory_space_constraint(stem_weight, pltpu.HBM),
            stem_other,
            small,
            small_other,
        )

    stem_other = lax.ppermute(stem_weight, "chan", swap)
    second_other = lax.ppermute(second_weight, "chan", swap)
    power = tile_count & (tile_count - 1) == 0 and tile_count >= 4
    if power:
        away, near = tile_count // 2, tile_count // 4
        pairs = [
            (2 * i + c, 2 * (i ^ (near if c else away)) + c)
            for i in range(tile_count)
            for c in range(2)
        ]
        one = lax.ppermute(latents, ("tile", "chan"), pairs)
        both = [(i, i ^ away ^ near) for i in range(tile_count)]
        two = lax.ppermute(latents, "tile", both)
        small_other = lax.ppermute(small, "chan", swap)
        three = lax.ppermute(one, "chan", swap)
        owners = jnp.concatenate([latents, one, two, three], axis=0)
        owners, small_other, stem_other = lax.optimization_barrier(
            (owners, small_other, stem_other)
        )
        step = near
        while step > 1:
            step //= 2
            owners = exchanged(owners, step)
        prepared = prepare(small, small_other, stem_other, power)
    else:
        small_other = lax.ppermute(small, "chan", swap)
        owners = lax.all_gather(latents, "tile", axis=0, tiled=True)
        prepared = prepare(small, small_other, stem_other, power)
    selection, stem_full, vectors, same = prepared
    act, hidden, other_near, own_near, up_near = pl.pallas_call(
        first_kernel,
        out_shape=(
            jax.ShapeDtypeStruct((window, F * H, half), jnp.bfloat16),
            jax.ShapeDtypeStruct((window - 2, frames * H, full), jnp.bfloat16),
            jax.ShapeDtypeStruct(second_weight.shape, jnp.bfloat16),
            jax.ShapeDtypeStruct(second_weight.shape, jnp.bfloat16),
            jax.ShapeDtypeStruct(upsample_weight.shape, jnp.bfloat16),
        ),
        in_specs=[vmem] * 6 + [far] * 4,
        out_specs=(vmem,) * 5,
        scratch_shapes=[
            pltpu.VMEM((tile_count, PACKED, 128), jnp.bfloat16),
            pltpu.VMEM((3, F, width, H_PAD * zc), jnp.float32),
            pltpu.VMEM((F, H, width, 256), jnp.bfloat16),
            pltpu.VMEM((full // 128, F * H * width, 128), jnp.float32),
            pltpu.VMEM((3, F, H + 2, width, full), jnp.bfloat16),
            pltpu.VMEM((pl.cdiv(half, 128), F * H * width, 128), jnp.float32),
            pltpu.VMEM((8, full), jnp.float32),
            pltpu.VMEM(first_weight.shape, jnp.bfloat16),
            pltpu.SemaphoreType.DMA,
            pltpu.SemaphoreType.DMA((3,)),
        ],
        cost_estimate=pl.CostEstimate(
            flops=2 * F * H * width * 27 * full * half * 3 // 4,
            bytes_accessed=27 * full * half * 2,
            transcendentals=F * H * width * full,
        ),
        compiler_params=pltpu.CompilerParams(
            vmem_limit_bytes=min(60, 12 + 12 * width // 16) * 1024 * 1024
        ),
    )(
        owners,
        selection,
        stem_full,
        vectors,
        same,
        small,
        pltpu.with_memory_space_constraint(first_weight, pltpu.HBM),
        pltpu.with_memory_space_constraint(second_other, pltpu.HBM),
        pltpu.with_memory_space_constraint(second_weight, pltpu.HBM),
        pltpu.with_memory_space_constraint(upsample_weight, pltpu.HBM),
    )

    act_other = lax.ppermute(act, "chan", swap)

    out = pl.pallas_call(
        functools.partial(second_kernel, tile_count),
        out_shape=jax.ShapeDtypeStruct((frames, 2 * H, 2 * W_DEV, out_channels), jnp.bfloat16),
        in_specs=[vmem] * 8,
        out_specs=vmem,
        scratch_shapes=[
            pltpu.VMEM((window, 2 * frames * 32 + 8, full), jnp.float32),
            pltpu.VMEM((9, window, frames * H, full), jnp.bfloat16),
            pltpu.VMEM((pl.cdiv(out_channels, 128), frames * 2 * H * 2 * W_DEV, 128), jnp.float32),
        ],
        cost_estimate=pl.CostEstimate(
            flops=2 * 4 * 48 * 27 * full * full,
            bytes_accessed=2 * 27 * full * half * 2,
            transcendentals=0,
        ),
        compiler_params=pltpu.CompilerParams(vmem_limit_bytes=24 * 1024 * 1024),
    )(
        act,
        act_other,
        hidden,
        own_near,
        other_near,
        vectors,
        up_near,
        upsample_bias.reshape(1, -1),
    )
    return out


def solution(mesh):
    placed = (
        P(("clip", "tile"), None, None),
        P("clip"),
        P(None, None, "chan"),
        P("chan"),
        P("chan"),
        P("chan"),
        P(None, None, "chan"),
        P("chan"),
        P("chan"),
        P("chan"),
        P(None, None, "chan"),
        P("chan"),
        P(),
        P(),
    )

    return jax.shard_map(
        on_device,
        mesh=mesh,
        in_specs=placed,
        out_specs=P(("clip", "chan"), None, "tile", None),
        check_vma=False,
    )
```
